512 devices in a mesh: ctx: 64 (over z, x, y_lo), tp: 8 (over y_hi, core).
Axes of the slice: x: 4, y: 8 (y_hi: 4, y_lo: 2; y = y_hi * 2 + y_lo), z: 8, core: 2. Of those that a mesh axis runs over, the one named last changes fastest.
Arguments:
- tokens: bfloat16 [8192, 4096], P('ctx'), may hold values from -6 to 6
- new_token_states: bfloat16 [4, 4096], replicated, may hold values from -6.0625 to 6.0625
- w_query: bfloat16 [4096, 2048], P('ctx', 'tp'), may hold values from -0.12162204 to 0.12162204
- key_matrix: bfloat16 [4096, 1024], P('ctx', 'tp'), may hold values from -0.12162204 to 0.12162204
- value_matrix: bfloat16 [4096, 1024], P('ctx', 'tp'), may hold values from -0.09375 to 0.09375
- w_out: bfloat16 [2048, 4096], P('tp', 'ctx'), may hold values from -0.125 to 0.125
- lengths: int32 [4], replicated, may hold values from 1 to 4096, 8192 in all
- block_map: int32 [128], replicated, may hold values from 0 to 127, each once
Outputs:
- prefill_out: bfloat16 [8192, 4096], P('ctx', 'tp')
- decode_out: bfloat16 [4, 4096], P(None, 'tp')
The draws below stay inside these ranges and needn't reach their ends.
Inputs may be any that keep to these rules, and one draw needn't show every extreme that they name: The lengths sum to 8192, and some request has exactly 4096 tokens. `block_map`: each of the 128 initial blocks is held exactly once.
All inputs are finite; a program needn't handle non-finite values.
Results may differ from the reference program's by a relative error of at most 0.015.
Values may be sent and summed in bfloat16 or wider, within the bound.
A program may use at most 64 MiB of HBM per device.

```python
import math
import jax
import jax.numpy as jnp
import numpy as np
from jax import lax

MODEL_WIDTH = 4096
QUERY_HEAD_COUNT = 16
KEY_VALUE_HEADS = 8
HEAD_SIZE = 128
REQUEST_COUNT = 4
BLOCK = 64
PROMPT_TOKENS = 8192
NBLOCKS = 128
LONGEST_PROMPT = 4096


def draw_w_query(key, part):
    random_jitter = jax.random.truncated_normal(jax.random.fold_in(key, 101), -6.0, 6.0, (MODEL_WIDTH, QUERY_HEAD_COUNT * HEAD_SIZE), jnp.float32)
    random_jitter = random_jitter * MODEL_WIDTH ** (-0.5)
    return random_jitter.astype(jnp.bfloat16)


def draw_key_matrix(key, part):
    random_jitter = jax.random.truncated_normal(jax.random.fold_in(key, 202), -6.0, 6.0, (MODEL_WIDTH, KEY_VALUE_HEADS * HEAD_SIZE), jnp.float32)
    random_jitter = random_jitter * MODEL_WIDTH ** (-0.5)
    return random_jitter.astype(jnp.bfloat16)


def draw_new_token_states(key, part):
    values = jax.random.truncated_normal(jax.random.fold_in(key, 303), -6.0, 6.0, (REQUEST_COUNT, MODEL_WIDTH), jnp.float32)
    return values.astype(jnp.bfloat16)


def block_levels(key, dims, pieces, low, high):
    gain, own = 1.0, jax.random.fold_in(key, 6)
    for position, blocks in pieces:
        steps = jnp.exp(jax.random.uniform(jax.random.fold_in(own, position), (blocks,), jnp.float32, low / len(pieces), high / len(pieces)))
        gain = gain * jnp.repeat(steps, dims[position] // blocks).reshape([-1 if axis == position else 1 for axis in range(len(dims))])
    return gain


def length_profile(amount, total, reach, skew):
    weights = [(1 << 20) // math.isqrt(grade ** skew) + 1 for grade in range(2, amount + 1)]
    surplus, counts = total - reach - (amount - 1), [1] * (amount - 1)
    while surplus > 0:
        free = [i for i in range(amount - 1) if counts[i] < reach]
        mass, budget = sum([weights[i] for i in free]), surplus
        for i in free:
            addition = min(reach - counts[i], max(1, budget * weights[i] // mass), surplus)
            counts[i] = counts[i] + addition
            surplus = surplus - addition
    return np.array([reach] + counts)


def ragged_sizes(key, count, total, reach, lean):
    if count == 2:
        one = jax.random.randint(key, (), max(1, total - reach), min(reach, total - 1) + 1)
        return jnp.stack([one, total - one])
    sizes = jnp.asarray(length_profile(count, total, reach, lean), jnp.int32)
    pairs = (count - 1) // 2
    source_of, receiver = sizes[1:1 + 2 * pairs:2], sizes[2:2 + 2 * pairs:2]
    room = jnp.minimum(source_of - 1, reach - receiver)
    moved = jax.random.randint(jax.random.fold_in(key, 1), (pairs,), 0, 1 << 20) % (room + 1)
    sizes = sizes.at[1:1 + 2 * pairs:2].set(source_of - moved).at[2:2 + 2 * pairs:2].set(receiver + moved)
    return sizes[jax.random.permutation(jax.random.fold_in(key, 2), count)]


def normal_values(rng, dims, spread, bound, cuts=(), kind=jnp.bfloat16):
    drawn = jax.random.normal(rng, dims, jnp.float32) * spread
    if len(cuts) > 0:
        drawn = block_levels(rng, dims, cuts, -0.22, 0.18) * drawn
    return jnp.clip(drawn, min=-bound, max=bound).astype(kind)


def setup_inputs(seed: int = 0) -> dict:
    keys = jax.random.split(jax.random.key(seed), 9)
    tokens = normal_values(keys[0], (PROMPT_TOKENS, MODEL_WIDTH), 1.0, 6.0, ((0, 64),))
    new_token_states = draw_new_token_states(jax.random.fold_in(keys[8], 71), 0)
    w_query = draw_w_query(jax.random.fold_in(keys[8], 71), 0)
    key_matrix = draw_key_matrix(jax.random.fold_in(keys[8], 71), 0)
    value_matrix = normal_values(keys[4], (MODEL_WIDTH, KEY_VALUE_HEADS * HEAD_SIZE), MODEL_WIDTH ** -0.5, 0.09375, ((0, 64), (1, 8)))
    w_out = normal_values(keys[5], (QUERY_HEAD_COUNT * HEAD_SIZE, MODEL_WIDTH), (QUERY_HEAD_COUNT * HEAD_SIZE) ** -0.5, 0.125, ((0, 8), (1, 64)))
    lengths = ragged_sizes(keys[6], REQUEST_COUNT, PROMPT_TOKENS, LONGEST_PROMPT, 2).astype(jnp.int32)
    block_map = jax.random.permutation(keys[7], NBLOCKS).astype(jnp.int32)
    return dict(tokens=tokens, new_token_states=new_token_states, w_query=w_query, key_matrix=key_matrix, value_matrix=value_matrix, w_out=w_out, lengths=lengths, block_map=block_map)


def initial_positions(block_map, row_count):
    row_ids = jnp.arange(row_count, dtype=jnp.int32)
    return block_map[row_ids // BLOCK] * BLOCK + row_ids % BLOCK

def request_index(positions, lengths):
    request_ends = jnp.cumsum(lengths).astype(jnp.int32)
    return lax.optimization_barrier(jnp.sum((positions[:, None] >= request_ends[None, :]).astype(jnp.int32), axis=1))

def project_rows(inputs, weight):
    return jnp.dot(inputs, weight, preferred_element_type=jnp.float32).astype(jnp.bfloat16)

def round_weights(weights):
    rounded = weights.astype(jnp.bfloat16)
    rounded = lax.optimization_barrier(rounded)
    return rounded.astype(jnp.float32)

def reference(tokens, new_token_states, w_query, key_matrix, value_matrix, w_out, lengths, block_map):
    query_group_count = QUERY_HEAD_COUNT // KEY_VALUE_HEADS
    score_scale = 1.0 / math.sqrt(HEAD_SIZE)
    queries = project_rows(tokens, w_query).reshape(PROMPT_TOKENS, QUERY_HEAD_COUNT, HEAD_SIZE)
    projected_key_rows = project_rows(tokens, key_matrix).reshape(PROMPT_TOKENS, KEY_VALUE_HEADS, HEAD_SIZE)
    projected_value_rows = project_rows(tokens, value_matrix).reshape(PROMPT_TOKENS, KEY_VALUE_HEADS, HEAD_SIZE)
    positions = initial_positions(block_map, PROMPT_TOKENS)
    inverse = jnp.zeros((PROMPT_TOKENS,), jnp.int32).at[positions].set(jnp.arange(PROMPT_TOKENS, dtype=jnp.int32))
    query_orig = queries[inverse]
    key_baseline = projected_key_rows[inverse]
    value_baseline = projected_value_rows[inverse]
    request_orig = request_index(jnp.arange(PROMPT_TOKENS, dtype=jnp.int32), lengths)
    filled_key_cache = jnp.concatenate([jnp.zeros((LONGEST_PROMPT, KEY_VALUE_HEADS, HEAD_SIZE), jnp.bfloat16), key_baseline], axis=0)
    filled_value_cache = jnp.concatenate([jnp.zeros((LONGEST_PROMPT, KEY_VALUE_HEADS, HEAD_SIZE), jnp.bfloat16), value_baseline], axis=0)
    padded_request = jnp.concatenate([jnp.full((LONGEST_PROMPT,), -1, jnp.int32), request_orig], axis=0)
    block_rows = min(256, PROMPT_TOKENS)
    window = LONGEST_PROMPT + block_rows

    def attend_block(block_index):
        first_row = (block_index * block_rows).astype(jnp.int32)
        query_block = lax.dynamic_slice_in_dim(query_orig, first_row, block_rows, 0).astype(jnp.float32)
        key_block = lax.dynamic_slice_in_dim(filled_key_cache, first_row, window, 0).astype(jnp.float32)
        value_block = lax.dynamic_slice_in_dim(filled_value_cache, first_row, window, 0).astype(jnp.float32)
        request_query = lax.dynamic_slice_in_dim(request_orig, first_row, block_rows, 0)
        request_key = lax.dynamic_slice_in_dim(padded_request, first_row, window, 0)
        query_pos = first_row + jnp.arange(block_rows, dtype=jnp.int32)
        key_pos = first_row - LONGEST_PROMPT + jnp.arange(window, dtype=jnp.int32)
        allowed = (request_key[None, :] == request_query[:, None]) & (key_pos[None, :] <= query_pos[:, None])
        key_heads = jnp.repeat(key_block, query_group_count, axis=1)
        value_heads = jnp.repeat(value_block, query_group_count, axis=1)
        scores = jnp.einsum('qhd,khd->hqk', query_block, key_heads) * score_scale
        scores = jnp.where(allowed[None], scores, -jnp.inf)
        row_peak = lax.optimization_barrier(jnp.max(scores, axis=2, keepdims=True))
        weights = jnp.exp(scores - row_peak)
        denominator = lax.optimization_barrier(jnp.sum(weights, axis=2))
        mixed_sum = jnp.einsum('hqk,khd->qhd', round_weights(weights), value_heads)
        return (mixed_sum / denominator.T[:, :, None]).astype(jnp.bfloat16)
    attended = lax.map(attend_block, jnp.arange(PROMPT_TOKENS // block_rows, dtype=jnp.int32))
    attended = attended.reshape(PROMPT_TOKENS, QUERY_HEAD_COUNT * HEAD_SIZE)[positions]
    dec_query = project_rows(new_token_states, w_query).reshape(REQUEST_COUNT, QUERY_HEAD_COUNT, HEAD_SIZE).astype(jnp.float32)
    decode_key_rows = jnp.repeat(project_rows(new_token_states, key_matrix).reshape(REQUEST_COUNT, KEY_VALUE_HEADS, HEAD_SIZE).astype(jnp.float32), query_group_count, axis=1)
    decode_value_rows = jnp.repeat(project_rows(new_token_states, value_matrix).reshape(REQUEST_COUNT, KEY_VALUE_HEADS, HEAD_SIZE).astype(jnp.float32), query_group_count, axis=1)
    key_all = jnp.repeat(key_baseline.astype(jnp.float32), query_group_count, axis=1)
    value_all = jnp.repeat(value_baseline.astype(jnp.float32), query_group_count, axis=1)
    cache_scores = jnp.einsum('rhd,thd->rht', dec_query, key_all) * score_scale
    owned = request_orig[None, :] == jnp.arange(REQUEST_COUNT, dtype=jnp.int32)[:, None]
    cache_scores = jnp.where(owned[:, None, :], cache_scores, -jnp.inf)
    self_scores = lax.optimization_barrier(jnp.sum(dec_query * decode_key_rows, axis=2)) * score_scale
    row_peak = jnp.maximum(lax.optimization_barrier(jnp.max(cache_scores, axis=2)), self_scores)
    cache_weights = jnp.exp(cache_scores - row_peak[:, :, None])
    self_weights = jnp.exp(self_scores - row_peak)
    denominator = lax.optimization_barrier(jnp.sum(cache_weights, axis=2)) + self_weights
    mixed_sum = jnp.einsum('rht,thd->rhd', round_weights(cache_weights), value_all)
    mixed_sum = mixed_sum + round_weights(self_weights)[:, :, None] * decode_value_rows
    dec_attn = (mixed_sum / denominator[:, :, None]).astype(jnp.bfloat16).reshape(REQUEST_COUNT, QUERY_HEAD_COUNT * HEAD_SIZE)
    prefill_out = jnp.dot(attended, w_out, preferred_element_type=jnp.float32).astype(jnp.bfloat16)
    decode_out = jnp.dot(dec_attn, w_out, preferred_element_type=jnp.float32).astype(jnp.bfloat16)
    return (prefill_out, decode_out)
```

```python
import math

import jax
import jax.numpy as jnp
from jax import lax
from jax.sharding import PartitionSpec as P

HEAD_SIZE = 128


floor_value = -1e30


def initial_positions(block_map, first_row, row_count, block_rows):
    row_ids = first_row + jnp.arange(row_count, dtype=jnp.int32)
    block_ids = row_ids // block_rows
    table_ids = jnp.arange(block_map.shape[0], dtype=jnp.int32)
    mapped = jnp.sum(
        jnp.where(block_ids[:, None] == table_ids[None, :], block_map[None, :], 0), axis=1
    )
    return mapped * block_rows + row_ids % block_rows


def request_index(positions, request_ends):
    return jnp.sum((positions[:, None] >= request_ends[None, :]).astype(jnp.int32), axis=1)


def round_weights(weights):
    rounded = weights.astype(jnp.bfloat16)
    rounded = lax.optimization_barrier(rounded)
    return rounded.astype(jnp.float32)


def softmax_parts(
    dec_heads, projected_key_rows, projected_value_rows, owned, kv_heads, head_dim, score_scale
):
    row_count = projected_key_rows.shape[0]
    scores = (
        jnp.einsum(
            "rgjd,tgd->rgjt",
            dec_heads,
            projected_key_rows.reshape(row_count, kv_heads, head_dim),
            preferred_element_type=jnp.float32,
        )
        * score_scale
    )
    scores = jnp.where(owned, scores, floor_value)
    part_peak = jnp.max(scores, axis=3)
    weights = jnp.where(owned, jnp.exp(scores - part_peak[..., None]), 0.0)
    part_total = jnp.sum(weights, axis=3)
    part_mixed = jnp.einsum(
        "rgjt,tgd->rgjd",
        weights.astype(jnp.bfloat16),
        projected_value_rows.reshape(row_count, kv_heads, head_dim),
        preferred_element_type=jnp.float32,
    )
    return (part_peak, part_total, part_mixed)


def on_device(
    tokens, new_token_states, w_query, key_matrix, value_matrix, w_out, lengths, block_map
):
    local_rows = tokens.shape[0]
    block_rows = local_rows // 2
    request_count = new_token_states.shape[0]
    head_dim = HEAD_SIZE
    query_width = w_query.shape[1]
    kv_width = key_matrix.shape[1]
    kv_heads = kv_width // head_dim
    query_group_count = query_width // kv_width
    score_scale = 1.0 / math.sqrt(head_dim)
    device = lax.axis_index("ctx")
    request_ends = jnp.cumsum(lengths)
    inputs = jnp.concatenate([tokens, new_token_states], axis=0)
    joined = lax.all_gather(
        jnp.concatenate([w_query, key_matrix, value_matrix, w_out.T], axis=1),
        "ctx",
        axis=0,
        tiled=True,
    )
    qkv_width = query_width + 2 * kv_width
    projected_all = jnp.dot(
        inputs, joined[:, :qkv_width], preferred_element_type=jnp.float32
    ).astype(jnp.bfloat16)
    out_weight = joined[:, qkv_width:].T
    query_all = projected_all[:, :query_width]
    key_all = projected_all[:, query_width : query_width + kv_width]
    value_all = projected_all[:, query_width + kv_width :]
    local_query = query_all[:local_rows]
    local_keys = key_all[:local_rows]
    local_values = value_all[:local_rows]
    dec_query = query_all[local_rows:]
    decode_key_rows = key_all[local_rows:]
    decode_value_rows = value_all[local_rows:]
    token_pos = initial_positions(block_map, device * local_rows, local_rows, block_rows)
    token_request = request_index(token_pos, request_ends)
    query_heads = local_query.reshape(local_rows, kv_heads, query_group_count, head_dim)

    def attend(running, shard_pieces, first_row):
        peak_run, total_run, mixed_run = running
        key_piece, value_piece = shard_pieces
        row_count = key_piece.shape[0]
        key_pos = initial_positions(block_map, first_row, row_count, block_rows)
        key_request = request_index(key_pos, request_ends)
        allowed = (key_request[None, :] == token_request[:, None]) & (
            key_pos[None, :] <= token_pos[:, None]
        )
        scores = (
            jnp.einsum(
                "tgjd,kgd->gjtk",
                query_heads,
                key_piece.reshape(row_count, kv_heads, head_dim),
                preferred_element_type=jnp.float32,
            )
            * score_scale
        )
        scores = jnp.where(allowed, scores, floor_value)
        peak_new = jnp.maximum(peak_run, jnp.max(scores, axis=3))
        weights = jnp.where(allowed, jnp.exp(scores - peak_new[..., None]), 0.0)
        rescale = jnp.exp(peak_run - peak_new)
        total_new = total_run * rescale + jnp.sum(weights, axis=3)
        mixed_new = mixed_run * rescale[..., None] + jnp.einsum(
            "gjtk,kgd->gjtd",
            weights.astype(jnp.bfloat16),
            value_piece.reshape(row_count, kv_heads, head_dim),
            preferred_element_type=jnp.float32,
        )
        return (peak_new, total_new, mixed_new)

    start_state = (
        jnp.full((kv_heads, query_group_count, local_rows), floor_value, jnp.float32),
        jnp.zeros((kv_heads, query_group_count, local_rows), jnp.float32),
        jnp.zeros((kv_heads, query_group_count, local_rows, head_dim), jnp.float32),
    )
    dec_heads = dec_query.reshape(request_count, kv_heads, query_group_count, head_dim)
    request_ids = jnp.arange(request_count, dtype=jnp.int32)
    cache_both = lax.all_gather(
        jnp.concatenate([local_keys, local_values], axis=1), "ctx", axis=0, tiled=True
    )
    cache_keys = cache_both[:, :kv_width]
    cache_values = cache_both[:, kv_width:]
    total_rows = cache_keys.shape[0]
    shard_count = total_rows // local_rows
    limit = max(1, 1024 // local_rows)
    step_rows = local_rows * math.gcd(shard_count, 1 << limit.bit_length() - 1)

    def key_step(running, step_index):
        first_row = step_index * step_rows
        pieces = (
            lax.dynamic_slice_in_dim(cache_keys, first_row, step_rows, 0),
            lax.dynamic_slice_in_dim(cache_values, first_row, step_rows, 0),
        )
        return (attend(running, pieces, first_row), None)

    final_state, unused = lax.scan(
        key_step, start_state, jnp.arange(total_rows // step_rows, dtype=jnp.int32)
    )
    peak_run, total_run, mixed_run = final_state
    cache_pos = (
        block_map[:, None] * block_rows + jnp.arange(block_rows, dtype=jnp.int32)[None, :]
    ).reshape(total_rows)
    cache_request = request_index(cache_pos, request_ends)
    owned = (cache_request[None, :] == request_ids[:, None])[:, None, None, :]
    cache_peak, cache_total, cache_mixed = softmax_parts(
        dec_heads, cache_keys, cache_values, owned, kv_heads, head_dim, score_scale
    )
    attended = (
        (mixed_run / total_run[..., None]).transpose(2, 0, 1, 3).reshape(local_rows, query_width)
    )
    attended = attended.astype(jnp.bfloat16)
    own_keys = decode_key_rows.reshape(request_count, kv_heads, 1, head_dim).astype(jnp.float32)
    own_values = decode_value_rows.reshape(request_count, kv_heads, 1, head_dim).astype(jnp.float32)
    self_scores = jnp.sum(dec_heads.astype(jnp.float32) * own_keys, axis=3) * score_scale
    peak_all = jnp.maximum(cache_peak, self_scores)
    rescale = jnp.exp(cache_peak - peak_all)
    self_weights = jnp.exp(self_scores - peak_all)
    dec_total = cache_total * rescale + self_weights
    dec_mixed = (
        cache_mixed * rescale[..., None] + round_weights(self_weights)[..., None] * own_values
    )
    dec_attn = (
        (dec_mixed / dec_total[..., None]).reshape(request_count, query_width).astype(jnp.bfloat16)
    )
    attended_all = jnp.concatenate([attended, dec_attn], axis=0)
    projected = jnp.dot(
        attended_all,
        out_weight,
        preferred_element_type=jnp.float32,
    )
    summed_rows = lax.psum_scatter(
        projected.astype(jnp.bfloat16), "tp", scatter_dimension=1, tiled=True
    ).astype(jnp.float32)
    summed_rows = summed_rows.astype(jnp.bfloat16)
    return (summed_rows[:local_rows], summed_rows[local_rows:])


def solution(mesh):
    return jax.shard_map(
        on_device,
        mesh=mesh,
        in_specs=(
            P("ctx", None),
            P(),
            P("ctx", "tp"),
            P("ctx", "tp"),
            P("ctx", "tp"),
            P("tp", "ctx"),
            P(),
            P(),
        ),
        out_specs=(P("ctx", "tp"), P(None, "tp")),
        check_vma=False,
    )
```

```python
import functools
import math

import jax
import jax.numpy as jnp
from jax import lax
from jax.experimental import pallas as pl
from jax.experimental.pallas import tpu as pltpu
from jax.sharding import PartitionSpec as P

HEAD_SIZE = 128


floor_value = -1e30


def _gather_kernel(count, piece_ref, out_ref, send_sems, recv_sems, local_sem):
    me = lax.axis_index("ctx")
    mesh_ids = pl.DeviceIdType.MESH
    barrier = pltpu.get_barrier_semaphore()

    def greet(step, carry):
        peer = lax.rem(me + step, count)
        pl.semaphore_signal(barrier, 1, device_id={"ctx": peer}, device_id_type=mesh_ids)
        return carry

    lax.fori_loop(1, count, greet, 0)
    pl.semaphore_wait(barrier, count - 1)
    own = pltpu.make_async_copy(piece_ref, out_ref.at[me], local_sem)
    own.start()

    def remote(peer, slot):
        return pltpu.make_async_remote_copy(
            src_ref=piece_ref,
            dst_ref=out_ref.at[slot],
            send_sem=send_sems.at[peer],
            recv_sem=recv_sems.at[slot],
            device_id={"ctx": peer},
            device_id_type=mesh_ids,
        )

    def send(step, carry):
        remote(lax.rem(me + step, count), me).start()
        return carry

    lax.fori_loop(1, count, send, 0)

    def finish(step, carry):
        peer = lax.rem(me + step, count)
        remote(peer, me).wait_send()
        remote(peer, peer).wait_recv()
        return carry

    lax.fori_loop(1, count, finish, 0)
    own.wait()


def gather_ctx(piece, count, kernel_id):
    rows, cols = piece.shape
    gathered = pl.pallas_call(
        functools.partial(_gather_kernel, count),
        out_shape=jax.ShapeDtypeStruct((count, rows, cols), piece.dtype),
        in_specs=[pl.BlockSpec(memory_space=pl.ANY)],
        out_specs=pl.BlockSpec(memory_space=pl.ANY),
        scratch_shapes=[
            pltpu.SemaphoreType.DMA((count,)),
            pltpu.SemaphoreType.DMA((count,)),
            pltpu.SemaphoreType.DMA(()),
        ],
        compiler_params=pltpu.CompilerParams(collective_id=kernel_id, has_side_effects=True),
    )(piece)
    return gathered.reshape(count * rows, cols)


def initial_positions(block_map, first_row, row_count, block_rows):
    row_ids = first_row + jnp.arange(row_count, dtype=jnp.int32)
    block_ids = row_ids // block_rows
    table_ids = jnp.arange(block_map.shape[0], dtype=jnp.int32)
    mapped = jnp.sum(
        jnp.where(block_ids[:, None] == table_ids[None, :], block_map[None, :], 0), axis=1
    )
    return mapped * block_rows + row_ids % block_rows


def request_index(positions, request_ends):
    return jnp.sum((positions[:, None] >= request_ends[None, :]).astype(jnp.int32), axis=1)


def round_weights(weights):
    rounded = weights.astype(jnp.bfloat16)
    rounded = lax.optimization_barrier(rounded)
    return rounded.astype(jnp.float32)


def softmax_parts(
    dec_heads, projected_key_rows, projected_value_rows, owned, kv_heads, head_dim, score_scale
):
    row_count = projected_key_rows.shape[0]
    scores = (
        jnp.einsum(
            "rgjd,tgd->rgjt",
            dec_heads,
            projected_key_rows.reshape(row_count, kv_heads, head_dim),
            preferred_element_type=jnp.float32,
        )
        * score_scale
    )
    scores = jnp.where(owned, scores, floor_value)
    part_peak = jnp.max(scores, axis=3)
    weights = jnp.where(owned, jnp.exp(scores - part_peak[..., None]), 0.0)
    part_total = jnp.sum(weights, axis=3)
    part_mixed = jnp.einsum(
        "rgjt,tgd->rgjd",
        weights.astype(jnp.bfloat16),
        projected_value_rows.reshape(row_count, kv_heads, head_dim),
        preferred_element_type=jnp.float32,
    )
    return (part_peak, part_total, part_mixed)


def on_device(
    ctx_count, tokens, new_token_states, w_query, key_matrix, value_matrix, w_out, lengths, block_map
):
    local_rows = tokens.shape[0]
    block_rows = local_rows // 2
    request_count = new_token_states.shape[0]
    head_dim = HEAD_SIZE
    query_width = w_query.shape[1]
    kv_width = key_matrix.shape[1]
    kv_heads = kv_width // head_dim
    query_group_count = query_width // kv_width
    score_scale = 1.0 / math.sqrt(head_dim)
    device = lax.axis_index("ctx")
    request_ends = jnp.cumsum(lengths)
    inputs = jnp.concatenate([tokens, new_token_states], axis=0)
    joined = gather_ctx(
        jnp.concatenate([w_query, key_matrix, value_matrix, w_out.T], axis=1), ctx_count, 0
    )
    qkv_width = query_width + 2 * kv_width
    projected_all = jnp.dot(
        inputs, joined[:, :qkv_width], preferred_element_type=jnp.float32
    ).astype(jnp.bfloat16)
    out_weight = joined[:, qkv_width:].T
    query_all = projected_all[:, :query_width]
    key_all = projected_all[:, query_width : query_width + kv_width]
    value_all = projected_all[:, query_width + kv_width :]
    local_query = query_all[:local_rows]
    local_keys = key_all[:local_rows]
    local_values = value_all[:local_rows]
    dec_query = query_all[local_rows:]
    decode_key_rows = key_all[local_rows:]
    decode_value_rows = value_all[local_rows:]
    token_pos = initial_positions(block_map, device * local_rows, local_rows, block_rows)
    token_request = request_index(token_pos, request_ends)
    query_heads = local_query.reshape(local_rows, kv_heads, query_group_count, head_dim)

    def attend(running, shard_pieces, first_row):
        peak_run, total_run, mixed_run = running
        key_piece, value_piece = shard_pieces
        row_count = key_piece.shape[0]
        key_pos = initial_positions(block_map, first_row, row_count, block_rows)
        key_request = request_index(key_pos, request_ends)
        allowed = (key_request[None, :] == token_request[:, None]) & (
            key_pos[None, :] <= token_pos[:, None]
        )
        scores = (
            jnp.einsum(
                "tgjd,kgd->gjtk",
                query_heads,
                key_piece.reshape(row_count, kv_heads, head_dim),
                preferred_element_type=jnp.float32,
            )
            * score_scale
        )
        scores = jnp.where(allowed, scores, floor_value)
        peak_new = jnp.maximum(peak_run, jnp.max(scores, axis=3))
        weights = jnp.where(allowed, jnp.exp(scores - peak_new[..., None]), 0.0)
        rescale = jnp.exp(peak_run - peak_new)
        total_new = total_run * rescale + jnp.sum(weights, axis=3)
        mixed_new = mixed_run * rescale[..., None] + jnp.einsum(
            "gjtk,kgd->gjtd",
            weights.astype(jnp.bfloat16),
            value_piece.reshape(row_count, kv_heads, head_dim),
            preferred_element_type=jnp.float32,
        )
        return (peak_new, total_new, mixed_new)

    start_state = (
        jnp.full((kv_heads, query_group_count, local_rows), floor_value, jnp.float32),
        jnp.zeros((kv_heads, query_group_count, local_rows), jnp.float32),
        jnp.zeros((kv_heads, query_group_count, local_rows, head_dim), jnp.float32),
    )
    dec_heads = dec_query.reshape(request_count, kv_heads, query_group_count, head_dim)
    request_ids = jnp.arange(request_count, dtype=jnp.int32)
    cache_both = gather_ctx(
        jnp.concatenate([local_keys, local_values], axis=1), ctx_count, 1
    )
    cache_keys = cache_both[:, :kv_width]
    cache_values = cache_both[:, kv_width:]
    total_rows = cache_keys.shape[0]
    shard_count = total_rows // local_rows
    limit = max(1, 1024 // local_rows)
    step_rows = local_rows * math.gcd(shard_count, 1 << limit.bit_length() - 1)

    def key_step(running, step_index):
        first_row = step_index * step_rows
        pieces = (
            lax.dynamic_slice_in_dim(cache_keys, first_row, step_rows, 0),
            lax.dynamic_slice_in_dim(cache_values, first_row, step_rows, 0),
        )
        return (attend(running, pieces, first_row), None)

    final_state, unused = lax.scan(
        key_step, start_state, jnp.arange(total_rows // step_rows, dtype=jnp.int32)
    )
    peak_run, total_run, mixed_run = final_state
    cache_pos = (
        block_map[:, None] * block_rows + jnp.arange(block_rows, dtype=jnp.int32)[None, :]
    ).reshape(total_rows)
    cache_request = request_index(cache_pos, request_ends)
    owned = (cache_request[None, :] == request_ids[:, None])[:, None, None, :]
    cache_peak, cache_total, cache_mixed = softmax_parts(
        dec_heads, cache_keys, cache_values, owned, kv_heads, head_dim, score_scale
    )
    attended = (
        (mixed_run / total_run[..., None]).transpose(2, 0, 1, 3).reshape(local_rows, query_width)
    )
    attended = attended.astype(jnp.bfloat16)
    own_keys = decode_key_rows.reshape(request_count, kv_heads, 1, head_dim).astype(jnp.float32)
    own_values = decode_value_rows.reshape(request_count, kv_heads, 1, head_dim).astype(jnp.float32)
    self_scores = jnp.sum(dec_heads.astype(jnp.float32) * own_keys, axis=3) * score_scale
    peak_all = jnp.maximum(cache_peak, self_scores)
    rescale = jnp.exp(cache_peak - peak_all)
    self_weights = jnp.exp(self_scores - peak_all)
    dec_total = cache_total * rescale + self_weights
    dec_mixed = (
        cache_mixed * rescale[..., None] + round_weights(self_weights)[..., None] * own_values
    )
    dec_attn = (
        (dec_mixed / dec_total[..., None]).reshape(request_count, query_width).astype(jnp.bfloat16)
    )
    attended_all = jnp.concatenate([attended, dec_attn], axis=0)
    projected = jnp.dot(
        attended_all,
        out_weight,
        preferred_element_type=jnp.float32,
    )
    summed_rows = lax.psum_scatter(
        projected.astype(jnp.bfloat16), "tp", scatter_dimension=1, tiled=True
    ).astype(jnp.float32)
    summed_rows = summed_rows.astype(jnp.bfloat16)
    return (summed_rows[:local_rows], summed_rows[local_rows:])


def solution(mesh):
    return jax.shard_map(
        functools.partial(on_device, mesh.shape["ctx"]),
        mesh=mesh,
        in_specs=(
            P("ctx", None),
            P(),
            P("ctx", "tp"),
            P("ctx", "tp"),
            P("ctx", "tp"),
            P("tp", "ctx"),
            P(),
            P(),
        ),
        out_specs=(P("ctx", "tp"), P(None, "tp")),
        check_vma=False,
    )
```

```python
import functools
import math

import jax
import jax.numpy as jnp
from jax import lax
from jax.experimental import pallas as pl
from jax.experimental.pallas import tpu as pltpu
from jax.sharding import PartitionSpec as P

HEAD_SIZE = 128


floor_value = -1e30


def _gather_kernel(
    z_count, p_count, piece_ref, out_ref, z_send, z_recv, p_send, p_recv, local_sem
):
    me = lax.axis_index("ctx")
    z_me = me // p_count
    p_me = lax.rem(me, p_count)
    mesh_ids = pl.DeviceIdType.MESH
    barrier = pltpu.get_barrier_semaphore()

    def z_peer(step):
        return lax.rem(z_me + step, z_count)

    def p_peer(step):
        return lax.rem(p_me + step, p_count)

    def greet_z(step, carry):
        target = z_peer(step) * p_count + p_me
        pl.semaphore_signal(barrier, 1, device_id={"ctx": target}, device_id_type=mesh_ids)
        return carry

    def greet_p(step, carry):
        target = z_me * p_count + p_peer(step)
        pl.semaphore_signal(barrier, 1, device_id={"ctx": target}, device_id_type=mesh_ids)
        return carry

    lax.fori_loop(1, z_count, greet_z, 0)
    lax.fori_loop(1, p_count, greet_p, 0)
    pl.semaphore_wait(barrier, z_count + p_count - 2)
    own = pltpu.make_async_copy(piece_ref, out_ref.at[p_me, z_me], local_sem)
    own.start()

    def z_copy(peer, slot):
        return pltpu.make_async_remote_copy(
            src_ref=piece_ref,
            dst_ref=out_ref.at[p_me, slot],
            send_sem=z_send.at[peer],
            recv_sem=z_recv.at[slot],
            device_id={"ctx": peer * p_count + p_me},
            device_id_type=mesh_ids,
        )

    def z_start(step, carry):
        z_copy(z_peer(step), z_me).start()
        return carry

    def z_finish(step, carry):
        peer = z_peer(step)
        z_copy(peer, z_me).wait_send()
        z_copy(peer, peer).wait_recv()
        return carry

    lax.fori_loop(1, z_count, z_start, 0)
    lax.fori_loop(1, z_count, z_finish, 0)
    own.wait()

    def p_copy(peer, slot):
        return pltpu.make_async_remote_copy(
            src_ref=out_ref.at[slot],
            dst_ref=out_ref.at[slot],
            send_sem=p_send.at[peer],
            recv_sem=p_recv.at[slot],
            device_id={"ctx": z_me * p_count + peer},
            device_id_type=mesh_ids,
        )

    def p_start(step, carry):
        p_copy(p_peer(step), p_me).start()
        return carry

    def p_finish(step, carry):
        peer = p_peer(step)
        p_copy(peer, p_me).wait_send()
        p_copy(peer, peer).wait_recv()
        return carry

    lax.fori_loop(1, p_count, p_start, 0)
    lax.fori_loop(1, p_count, p_finish, 0)


def gather_ctx(piece, layout, kernel_id):
    z_count, p_count = layout
    rows, cols = piece.shape
    gathered = pl.pallas_call(
        functools.partial(_gather_kernel, z_count, p_count),
        out_shape=jax.ShapeDtypeStruct((p_count, z_count, rows, cols), piece.dtype),
        in_specs=[pl.BlockSpec(memory_space=pl.ANY)],
        out_specs=pl.BlockSpec(memory_space=pl.ANY),
        scratch_shapes=[
            pltpu.SemaphoreType.DMA((z_count,)),
            pltpu.SemaphoreType.DMA((z_count,)),
            pltpu.SemaphoreType.DMA((p_count,)),
            pltpu.SemaphoreType.DMA((p_count,)),
            pltpu.SemaphoreType.DMA(()),
        ],
        compiler_params=pltpu.CompilerParams(collective_id=kernel_id, has_side_effects=True),
    )(piece)
    return gathered.transpose(1, 0, 2, 3).reshape(z_count * p_count * rows, cols)


def ctx_layout(mesh):
    count = mesh.shape["ctx"]
    column = mesh.devices.transpose(
        mesh.axis_names.index("ctx"), mesh.axis_names.index("tp")
    )[:, 0]
    try:
        planes = [device.coords[2] for device in column]
    except (AttributeError, IndexError, TypeError):
        return (count, 1)
    p_count = 1
    while p_count < count and planes[p_count] == planes[0]:
        p_count += 1
    if count % p_count:
        return (count, 1)
    for index in range(count):
        if planes[index] != planes[(index // p_count) * p_count]:
            return (count, 1)
    return (count // p_count, p_count)


def initial_positions(block_map, first_row, row_count, block_rows):
    row_ids = first_row + jnp.arange(row_count, dtype=jnp.int32)
    block_ids = row_ids // block_rows
    table_ids = jnp.arange(block_map.shape[0], dtype=jnp.int32)
    mapped = jnp.sum(
        jnp.where(block_ids[:, None] == table_ids[None, :], block_map[None, :], 0), axis=1
    )
    return mapped * block_rows + row_ids % block_rows


def request_index(positions, request_ends):
    return jnp.sum((positions[:, None] >= request_ends[None, :]).astype(jnp.int32), axis=1)


def round_weights(weights):
    rounded = weights.astype(jnp.bfloat16)
    rounded = lax.optimization_barrier(rounded)
    return rounded.astype(jnp.float32)


def softmax_parts(
    dec_heads, projected_key_rows, projected_value_rows, owned, kv_heads, head_dim, score_scale
):
    row_count = projected_key_rows.shape[0]
    scores = (
        jnp.einsum(
            "rgjd,tgd->rgjt",
            dec_heads,
            projected_key_rows.reshape(row_count, kv_heads, head_dim),
            preferred_element_type=jnp.float32,
        )
        * score_scale
    )
    scores = jnp.where(owned, scores, floor_value)
    part_peak = jnp.max(scores, axis=3)
    weights = jnp.where(owned, jnp.exp(scores - part_peak[..., None]), 0.0)
    part_total = jnp.sum(weights, axis=3)
    part_mixed = jnp.einsum(
        "rgjt,tgd->rgjd",
        weights.astype(jnp.bfloat16),
        projected_value_rows.reshape(row_count, kv_heads, head_dim),
        preferred_element_type=jnp.float32,
    )
    return (part_peak, part_total, part_mixed)


def on_device(
    layout, tokens, new_token_states, w_query, key_matrix, value_matrix, w_out, lengths, block_map
):
    local_rows = tokens.shape[0]
    block_rows = local_rows // 2
    request_count = new_token_states.shape[0]
    head_dim = HEAD_SIZE
    query_width = w_query.shape[1]
    kv_width = key_matrix.shape[1]
    kv_heads = kv_width // head_dim
    query_group_count = query_width // kv_width
    score_scale = 1.0 / math.sqrt(head_dim)
    device = lax.axis_index("ctx")
    request_ends = jnp.cumsum(lengths)
    inputs = jnp.concatenate([tokens, new_token_states], axis=0)
    joined = gather_ctx(
        jnp.concatenate([w_query, key_matrix, value_matrix, w_out.T], axis=1), layout, 0
    )
    qkv_width = query_width + 2 * kv_width
    projected_all = jnp.dot(
        inputs, joined[:, :qkv_width], preferred_element_type=jnp.float32
    ).astype(jnp.bfloat16)
    out_weight = joined[:, qkv_width:].T
    query_all = projected_all[:, :query_width]
    key_all = projected_all[:, query_width : query_width + kv_width]
    value_all = projected_all[:, query_width + kv_width :]
    local_query = query_all[:local_rows]
    local_keys = key_all[:local_rows]
    local_values = value_all[:local_rows]
    dec_query = query_all[local_rows:]
    decode_key_rows = key_all[local_rows:]
    decode_value_rows = value_all[local_rows:]
    token_pos = initial_positions(block_map, device * local_rows, local_rows, block_rows)
    token_request = request_index(token_pos, request_ends)
    query_heads = local_query.reshape(local_rows, kv_heads, query_group_count, head_dim)

    def attend(running, shard_pieces, first_row):
        peak_run, total_run, mixed_run = running
        key_piece, value_piece = shard_pieces
        row_count = key_piece.shape[0]
        key_pos = initial_positions(block_map, first_row, row_count, block_rows)
        key_request = request_index(key_pos, request_ends)
        allowed = (key_request[None, :] == token_request[:, None]) & (
            key_pos[None, :] <= token_pos[:, None]
        )
        scores = (
            jnp.einsum(
                "tgjd,kgd->gjtk",
                query_heads,
                key_piece.reshape(row_count, kv_heads, head_dim),
                preferred_element_type=jnp.float32,
            )
            * score_scale
        )
        scores = jnp.where(allowed, scores, floor_value)
        peak_new = jnp.maximum(peak_run, jnp.max(scores, axis=3))
        weights = jnp.where(allowed, jnp.exp(scores - peak_new[..., None]), 0.0)
        rescale = jnp.exp(peak_run - peak_new)
        total_new = total_run * rescale + jnp.sum(weights, axis=3)
        mixed_new = mixed_run * rescale[..., None] + jnp.einsum(
            "gjtk,kgd->gjtd",
            weights.astype(jnp.bfloat16),
            value_piece.reshape(row_count, kv_heads, head_dim),
            preferred_element_type=jnp.float32,
        )
        return (peak_new, total_new, mixed_new)

    start_state = (
        jnp.full((kv_heads, query_group_count, local_rows), floor_value, jnp.float32),
        jnp.zeros((kv_heads, query_group_count, local_rows), jnp.float32),
        jnp.zeros((kv_heads, query_group_count, local_rows, head_dim), jnp.float32),
    )
    dec_heads = dec_query.reshape(request_count, kv_heads, query_group_count, head_dim)
    request_ids = jnp.arange(request_count, dtype=jnp.int32)
    cache_both = gather_ctx(
        jnp.concatenate([local_keys, local_values], axis=1), layout, 1
    )
    cache_keys = cache_both[:, :kv_width]
    cache_values = cache_both[:, kv_width:]
    total_rows = cache_keys.shape[0]
    shard_count = total_rows // local_rows
    limit = max(1, 1024 // local_rows)
    step_rows = local_rows * math.gcd(shard_count, 1 << limit.bit_length() - 1)

    def key_step(running, step_index):
        first_row = step_index * step_rows
        pieces = (
            lax.dynamic_slice_in_dim(cache_keys, first_row, step_rows, 0),
            lax.dynamic_slice_in_dim(cache_values, first_row, step_rows, 0),
        )
        return (attend(running, pieces, first_row), None)

    final_state, unused = lax.scan(
        key_step, start_state, jnp.arange(total_rows // step_rows, dtype=jnp.int32)
    )
    peak_run, total_run, mixed_run = final_state
    cache_pos = (
        block_map[:, None] * block_rows + jnp.arange(block_rows, dtype=jnp.int32)[None, :]
    ).reshape(total_rows)
    cache_request = request_index(cache_pos, request_ends)
    owned = (cache_request[None, :] == request_ids[:, None])[:, None, None, :]
    cache_peak, cache_total, cache_mixed = softmax_parts(
        dec_heads, cache_keys, cache_values, owned, kv_heads, head_dim, score_scale
    )
    attended = (
        (mixed_run / total_run[..., None]).transpose(2, 0, 1, 3).reshape(local_rows, query_width)
    )
    attended = attended.astype(jnp.bfloat16)
    own_keys = decode_key_rows.reshape(request_count, kv_heads, 1, head_dim).astype(jnp.float32)
    own_values = decode_value_rows.reshape(request_count, kv_heads, 1, head_dim).astype(jnp.float32)
    self_scores = jnp.sum(dec_heads.astype(jnp.float32) * own_keys, axis=3) * score_scale
    peak_all = jnp.maximum(cache_peak, self_scores)
    rescale = jnp.exp(cache_peak - peak_all)
    self_weights = jnp.exp(self_scores - peak_all)
    dec_total = cache_total * rescale + self_weights
    dec_mixed = (
        cache_mixed * rescale[..., None] + round_weights(self_weights)[..., None] * own_values
    )
    dec_attn = (
        (dec_mixed / dec_total[..., None]).reshape(request_count, query_width).astype(jnp.bfloat16)
    )
    attended_all = jnp.concatenate([attended, dec_attn], axis=0)
    projected = jnp.dot(
        attended_all,
        out_weight,
        preferred_element_type=jnp.float32,
    )
    summed_rows = lax.psum_scatter(
        projected.astype(jnp.bfloat16), "tp", scatter_dimension=1, tiled=True
    ).astype(jnp.float32)
    summed_rows = summed_rows.astype(jnp.bfloat16)
    return (summed_rows[:local_rows], summed_rows[local_rows:])


def solution(mesh):
    return jax.shard_map(
        functools.partial(on_device, ctx_layout(mesh)),
        mesh=mesh,
        in_specs=(
            P("ctx", None),
            P(),
            P("ctx", "tp"),
            P("ctx", "tp"),
            P("ctx", "tp"),
            P("tp", "ctx"),
            P(),
            P(),
        ),
        out_specs=(P("ctx", "tp"), P(None, "tp")),
        check_vma=False,
    )
```

```python
import functools
import math

import jax
import jax.numpy as jnp
from jax import lax
from jax.experimental import pallas as pl
from jax.experimental.pallas import tpu as pltpu
from jax.sharding import PartitionSpec as P

HEAD_SIZE = 128


floor_value = -1e30


def _gather_kernel(
    z_count, p_count, piece_ref, out_ref, z_send, z_recv, p_send, p_recv, local_sem
):
    me = lax.axis_index("ctx")
    z_me = me // p_count
    p_me = lax.rem(me, p_count)
    mesh_ids = pl.DeviceIdType.MESH
    barrier = pltpu.get_barrier_semaphore()

    def z_peer(step):
        return lax.rem(z_me + step, z_count)

    def p_peer(step):
        return lax.rem(p_me + step, p_count)

    def greet_z(step, carry):
        target = z_peer(step) * p_count + p_me
        pl.semaphore_signal(barrier, 1, device_id={"ctx": target}, device_id_type=mesh_ids)
        return carry

    def greet_p(step, carry):
        target = z_me * p_count + p_peer(step)
        pl.semaphore_signal(barrier, 1, device_id={"ctx": target}, device_id_type=mesh_ids)
        return carry

    lax.fori_loop(1, z_count, greet_z, 0)
    lax.fori_loop(1, p_count, greet_p, 0)
    pl.semaphore_wait(barrier, z_count + p_count - 2)
    own = pltpu.make_async_copy(piece_ref, out_ref.at[p_me, z_me], local_sem)
    own.start()

    def z_copy(peer, slot):
        return pltpu.make_async_remote_copy(
            src_ref=piece_ref,
            dst_ref=out_ref.at[p_me, slot],
            send_sem=z_send.at[peer],
            recv_sem=z_recv.at[slot],
            device_id={"ctx": peer * p_count + p_me},
            device_id_type=mesh_ids,
        )

    def z_start(step, carry):
        z_copy(z_peer(step), z_me).start()
        return carry

    def z_finish(step, carry):
        peer = z_peer(step)
        z_copy(peer, z_me).wait_send()
        z_copy(peer, peer).wait_recv()
        return carry

    lax.fori_loop(1, z_count, z_start, 0)
    lax.fori_loop(1, z_count, z_finish, 0)
    own.wait()

    def p_copy(peer, slot):
        return pltpu.make_async_remote_copy(
            src_ref=out_ref.at[slot],
            dst_ref=out_ref.at[slot],
            send_sem=p_send.at[peer],
            recv_sem=p_recv.at[slot],
            device_id={"ctx": z_me * p_count + peer},
            device_id_type=mesh_ids,
        )

    def p_start(step, carry):
        p_copy(p_peer(step), p_me).start()
        return carry

    def p_finish(step, carry):
        peer = p_peer(step)
        p_copy(peer, p_me).wait_send()
        p_copy(peer, peer).wait_recv()
        return carry

    lax.fori_loop(1, p_count, p_start, 0)
    lax.fori_loop(1, p_count, p_finish, 0)


def gather_ctx(piece, layout, kernel_id):
    z_count, p_count = layout
    rows, cols = piece.shape
    gathered = pl.pallas_call(
        functools.partial(_gather_kernel, z_count, p_count),
        out_shape=jax.ShapeDtypeStruct((p_count, z_count, rows, cols), piece.dtype),
        in_specs=[pl.BlockSpec(memory_space=pl.ANY)],
        out_specs=pl.BlockSpec(memory_space=pl.ANY),
        scratch_shapes=[
            pltpu.SemaphoreType.DMA((z_count,)),
            pltpu.SemaphoreType.DMA((z_count,)),
            pltpu.SemaphoreType.DMA((p_count,)),
            pltpu.SemaphoreType.DMA((p_count,)),
            pltpu.SemaphoreType.DMA(()),
        ],
        compiler_params=pltpu.CompilerParams(collective_id=kernel_id, has_side_effects=True),
    )(piece)
    return gathered.transpose(1, 0, 2, 3).reshape(z_count * p_count * rows, cols)


def _scatter_kernel(count, part_ref, out_ref, send_sems, recv_sems, local_sem):
    me = lax.axis_index("tp")
    width = out_ref.shape[2]
    mesh_ids = pl.DeviceIdType.MESH
    barrier = pltpu.get_barrier_semaphore()

    def greet(step, carry):
        peer = lax.rem(me + step, count)
        pl.semaphore_signal(barrier, 1, device_id={"tp": peer}, device_id_type=mesh_ids)
        return carry

    lax.fori_loop(1, count, greet, 0)
    pl.semaphore_wait(barrier, count - 1)

    def columns(index):
        return pl.ds(pl.multiple_of(index * width, width), width)

    own = pltpu.make_async_copy(part_ref.at[:, columns(me)], out_ref.at[me], local_sem)
    own.start()

    def remote(peer, slot):
        return pltpu.make_async_remote_copy(
            src_ref=part_ref.at[:, columns(peer)],
            dst_ref=out_ref.at[slot],
            send_sem=send_sems.at[peer],
            recv_sem=recv_sems.at[slot],
            device_id={"tp": peer},
            device_id_type=mesh_ids,
        )

    def send(step, carry):
        remote(lax.rem(me + step, count), me).start()
        return carry

    def finish(step, carry):
        peer = lax.rem(me + step, count)
        remote(peer, me).wait_send()
        remote(peer, peer).wait_recv()
        return carry

    lax.fori_loop(1, count, send, 0)
    lax.fori_loop(1, count, finish, 0)
    own.wait()


def scatter_sum_tp(part, count, kernel_id):
    rows, cols = part.shape
    pieces = pl.pallas_call(
        functools.partial(_scatter_kernel, count),
        out_shape=jax.ShapeDtypeStruct((count, rows, cols // count), part.dtype),
        in_specs=[pl.BlockSpec(memory_space=pl.ANY)],
        out_specs=pl.BlockSpec(memory_space=pl.ANY),
        scratch_shapes=[
            pltpu.SemaphoreType.DMA((count,)),
            pltpu.SemaphoreType.DMA((count,)),
            pltpu.SemaphoreType.DMA(()),
        ],
        compiler_params=pltpu.CompilerParams(collective_id=kernel_id, has_side_effects=True),
    )(part)
    return jnp.sum(pieces.astype(jnp.float32), axis=0)


def ctx_layout(mesh):
    count = mesh.shape["ctx"]
    column = mesh.devices.transpose(
        mesh.axis_names.index("ctx"), mesh.axis_names.index("tp")
    )[:, 0]
    try:
        planes = [device.coords[2] for device in column]
    except (AttributeError, IndexError, TypeError):
        return (count, 1)
    p_count = 1
    while p_count < count and planes[p_count] == planes[0]:
        p_count += 1
    if count % p_count:
        return (count, 1)
    for index in range(count):
        if planes[index] != planes[(index // p_count) * p_count]:
            return (count, 1)
    return (count // p_count, p_count)


def initial_positions(block_map, first_row, row_count, block_rows):
    row_ids = first_row + jnp.arange(row_count, dtype=jnp.int32)
    block_ids = row_ids // block_rows
    table_ids = jnp.arange(block_map.shape[0], dtype=jnp.int32)
    mapped = jnp.sum(
        jnp.where(block_ids[:, None] == table_ids[None, :], block_map[None, :], 0), axis=1
    )
    return mapped * block_rows + row_ids % block_rows


def request_index(positions, request_ends):
    return jnp.sum((positions[:, None] >= request_ends[None, :]).astype(jnp.int32), axis=1)


def round_weights(weights):
    rounded = weights.astype(jnp.bfloat16)
    rounded = lax.optimization_barrier(rounded)
    return rounded.astype(jnp.float32)


def softmax_parts(
    dec_heads, projected_key_rows, projected_value_rows, owned, kv_heads, head_dim, score_scale
):
    row_count = projected_key_rows.shape[0]
    scores = (
        jnp.einsum(
            "rgjd,tgd->rgjt",
            dec_heads,
            projected_key_rows.reshape(row_count, kv_heads, head_dim),
            preferred_element_type=jnp.float32,
        )
        * score_scale
    )
    scores = jnp.where(owned, scores, floor_value)
    part_peak = jnp.max(scores, axis=3)
    weights = jnp.where(owned, jnp.exp(scores - part_peak[..., None]), 0.0)
    part_total = jnp.sum(weights, axis=3)
    part_mixed = jnp.einsum(
        "rgjt,tgd->rgjd",
        weights.astype(jnp.bfloat16),
        projected_value_rows.reshape(row_count, kv_heads, head_dim),
        preferred_element_type=jnp.float32,
    )
    return (part_peak, part_total, part_mixed)


def on_device(
    layout, tp_count, tokens, new_token_states, w_query, key_matrix, value_matrix, w_out, lengths, block_map
):
    local_rows = tokens.shape[0]
    block_rows = local_rows // 2
    request_count = new_token_states.shape[0]
    head_dim = HEAD_SIZE
    query_width = w_query.shape[1]
    kv_width = key_matrix.shape[1]
    kv_heads = kv_width // head_dim
    query_group_count = query_width // kv_width
    score_scale = 1.0 / math.sqrt(head_dim)
    device = lax.axis_index("ctx")
    request_ends = jnp.cumsum(lengths)
    inputs = jnp.concatenate([tokens, new_token_states], axis=0)
    joined = gather_ctx(
        jnp.concatenate([w_query, key_matrix, value_matrix, w_out.T], axis=1), layout, 0
    )
    qkv_width = query_width + 2 * kv_width
    projected_all = jnp.dot(
        inputs, joined[:, :qkv_width], preferred_element_type=jnp.float32
    ).astype(jnp.bfloat16)
    out_weight = joined[:, qkv_width:].T
    query_all = projected_all[:, :query_width]
    key_all = projected_all[:, query_width : query_width + kv_width]
    value_all = projected_all[:, query_width + kv_width :]
    local_query = query_all[:local_rows]
    local_keys = key_all[:local_rows]
    local_values = value_all[:local_rows]
    dec_query = query_all[local_rows:]
    decode_key_rows = key_all[local_rows:]
    decode_value_rows = value_all[local_rows:]
    token_pos = initial_positions(block_map, device * local_rows, local_rows, block_rows)
    token_request = request_index(token_pos, request_ends)
    query_heads = local_query.reshape(local_rows, kv_heads, query_group_count, head_dim)

    def attend(running, shard_pieces, first_row):
        peak_run, total_run, mixed_run = running
        key_piece, value_piece = shard_pieces
        row_count = key_piece.shape[0]
        key_pos = initial_positions(block_map, first_row, row_count, block_rows)
        key_request = request_index(key_pos, request_ends)
        allowed = (key_request[None, :] == token_request[:, None]) & (
            key_pos[None, :] <= token_pos[:, None]
        )
        scores = (
            jnp.einsum(
                "tgjd,kgd->gjtk",
                query_heads,
                key_piece.reshape(row_count, kv_heads, head_dim),
                preferred_element_type=jnp.float32,
            )
            * score_scale
        )
        scores = jnp.where(allowed, scores, floor_value)
        peak_new = jnp.maximum(peak_run, jnp.max(scores, axis=3))
        weights = jnp.where(allowed, jnp.exp(scores - peak_new[..., None]), 0.0)
        rescale = jnp.exp(peak_run - peak_new)
        total_new = total_run * rescale + jnp.sum(weights, axis=3)
        mixed_new = mixed_run * rescale[..., None] + jnp.einsum(
            "gjtk,kgd->gjtd",
            weights.astype(jnp.bfloat16),
            value_piece.reshape(row_count, kv_heads, head_dim),
            preferred_element_type=jnp.float32,
        )
        return (peak_new, total_new, mixed_new)

    start_state = (
        jnp.full((kv_heads, query_group_count, local_rows), floor_value, jnp.float32),
        jnp.zeros((kv_heads, query_group_count, local_rows), jnp.float32),
        jnp.zeros((kv_heads, query_group_count, local_rows, head_dim), jnp.float32),
    )
    dec_heads = dec_query.reshape(request_count, kv_heads, query_group_count, head_dim)
    request_ids = jnp.arange(request_count, dtype=jnp.int32)
    cache_both = gather_ctx(
        jnp.concatenate([local_keys, local_values], axis=1), layout, 1
    )
    cache_keys = cache_both[:, :kv_width]
    cache_values = cache_both[:, kv_width:]
    total_rows = cache_keys.shape[0]
    shard_count = total_rows // local_rows
    limit = max(1, 1024 // local_rows)
    step_rows = local_rows * math.gcd(shard_count, 1 << limit.bit_length() - 1)

    def key_step(running, step_index):
        first_row = step_index * step_rows
        pieces = (
            lax.dynamic_slice_in_dim(cache_keys, first_row, step_rows, 0),
            lax.dynamic_slice_in_dim(cache_values, first_row, step_rows, 0),
        )
        return (attend(running, pieces, first_row), None)

    final_state, unused = lax.scan(
        key_step, start_state, jnp.arange(total_rows // step_rows, dtype=jnp.int32)
    )
    peak_run, total_run, mixed_run = final_state
    cache_pos = (
        block_map[:, None] * block_rows + jnp.arange(block_rows, dtype=jnp.int32)[None, :]
    ).reshape(total_rows)
    cache_request = request_index(cache_pos, request_ends)
    owned = (cache_request[None, :] == request_ids[:, None])[:, None, None, :]
    cache_peak, cache_total, cache_mixed = softmax_parts(
        dec_heads, cache_keys, cache_values, owned, kv_heads, head_dim, score_scale
    )
    attended = (
        (mixed_run / total_run[..., None]).transpose(2, 0, 1, 3).reshape(local_rows, query_width)
    )
    attended = attended.astype(jnp.bfloat16)
    own_keys = decode_key_rows.reshape(request_count, kv_heads, 1, head_dim).astype(jnp.float32)
    own_values = decode_value_rows.reshape(request_count, kv_heads, 1, head_dim).astype(jnp.float32)
    self_scores = jnp.sum(dec_heads.astype(jnp.float32) * own_keys, axis=3) * score_scale
    peak_all = jnp.maximum(cache_peak, self_scores)
    rescale = jnp.exp(cache_peak - peak_all)
    self_weights = jnp.exp(self_scores - peak_all)
    dec_total = cache_total * rescale + self_weights
    dec_mixed = (
        cache_mixed * rescale[..., None] + round_weights(self_weights)[..., None] * own_values
    )
    dec_attn = (
        (dec_mixed / dec_total[..., None]).reshape(request_count, query_width).astype(jnp.bfloat16)
    )
    attended_all = jnp.concatenate([attended, dec_attn], axis=0)
    projected = jnp.dot(
        attended_all,
        out_weight,
        preferred_element_type=jnp.float32,
    )
    summed_rows = scatter_sum_tp(projected.astype(jnp.bfloat16), tp_count, 2)
    summed_rows = summed_rows.astype(jnp.bfloat16)
    return (summed_rows[:local_rows], summed_rows[local_rows:])


def solution(mesh):
    return jax.shard_map(
        functools.partial(on_device, ctx_layout(mesh), mesh.shape["tp"]),
        mesh=mesh,
        in_specs=(
            P("ctx", None),
            P(),
            P("ctx", "tp"),
            P("ctx", "tp"),
            P("ctx", "tp"),
            P("tp", "ctx"),
            P(),
            P(),
        ),
        out_specs=(P("ctx", "tp"), P(None, "tp")),
        check_vma=False,
    )
```

```python
import functools
import math

import jax
import jax.numpy as jnp
from jax import lax
from jax.experimental import pallas as pl
from jax.experimental.pallas import tpu as pltpu
from jax.sharding import PartitionSpec as P

HEAD_SIZE = 128


floor_value = -1e30


def _gather_kernel(
    z_count,
    p_count,
    first_ref,
    second_ref,
    first_out,
    second_out,
    first_z,
    first_p,
    second_p,
    second_z,
    local_sems,
):
    me = lax.axis_index("ctx")
    z_me = me // p_count
    p_me = lax.rem(me, p_count)
    mesh_ids = pl.DeviceIdType.MESH
    barrier = pltpu.get_barrier_semaphore()

    def z_peer(step):
        return lax.rem(z_me + step, z_count)

    def p_peer(step):
        return lax.rem(p_me + step, p_count)

    def z_target(peer):
        return peer * p_count + p_me

    def p_target(peer):
        return z_me * p_count + peer

    def greet(peer_of, target_of):
        def body(step, carry):
            pl.semaphore_signal(
                barrier, 1, device_id={"ctx": target_of(peer_of(step))}, device_id_type=mesh_ids
            )
            return carry

        return body

    lax.fori_loop(1, z_count, greet(z_peer, z_target), 0)
    lax.fori_loop(1, p_count, greet(p_peer, p_target), 0)
    pl.semaphore_wait(barrier, z_count + p_count - 2)

    def exchange(count, peer_of, target_of, own_slot, src_of, dst_of, sems):
        send_sems, recv_sems = sems

        def copy(peer, slot):
            return pltpu.make_async_remote_copy(
                src_ref=src_of(slot),
                dst_ref=dst_of(slot),
                send_sem=send_sems.at[peer],
                recv_sem=recv_sems.at[slot],
                device_id={"ctx": target_of(peer)},
                device_id_type=mesh_ids,
            )

        def start(step, carry):
            copy(peer_of(step), own_slot).start()
            return carry

        def finish(step, carry):
            peer = peer_of(step)
            copy(peer, own_slot).wait_send()
            copy(peer, peer).wait_recv()
            return carry

        return (lambda: lax.fori_loop(1, count, start, 0), lambda: lax.fori_loop(1, count, finish, 0))

    first_own = pltpu.make_async_copy(first_ref, first_out.at[p_me, z_me], local_sems.at[0])
    second_own = pltpu.make_async_copy(second_ref, second_out.at[z_me, p_me], local_sems.at[1])
    first_own.start()
    second_own.start()
    first_one = exchange(
        z_count, z_peer, z_target, z_me,
        lambda slot: first_ref, lambda slot: first_out.at[p_me, slot], first_z,
    )
    second_one = exchange(
        p_count, p_peer, p_target, p_me,
        lambda slot: second_ref, lambda slot: second_out.at[z_me, slot], second_p,
    )
    first_two = exchange(
        p_count, p_peer, p_target, p_me,
        lambda slot: first_out.at[slot], lambda slot: first_out.at[slot], first_p,
    )
    second_two = exchange(
        z_count, z_peer, z_target, z_me,
        lambda slot: second_out.at[slot], lambda slot: second_out.at[slot], second_z,
    )
    first_one[0]()
    second_one[0]()
    first_one[1]()
    first_own.wait()
    first_two[0]()
    second_one[1]()
    second_own.wait()
    second_two[0]()
    first_two[1]()
    second_two[1]()


def gather_ctx(piece, layout, kernel_id):
    z_count, p_count = layout
    rows, cols = piece.shape
    half = cols // 2
    dma_pairs = [
        pltpu.SemaphoreType.DMA((z_count,)),
        pltpu.SemaphoreType.DMA((z_count,)),
        pltpu.SemaphoreType.DMA((p_count,)),
        pltpu.SemaphoreType.DMA((p_count,)),
    ]

    def kernel(first_ref, second_ref, first_out, second_out, *sems):
        _gather_kernel(
            z_count, p_count, first_ref, second_ref, first_out, second_out,
            (sems[0], sems[1]), (sems[2], sems[3]), (sems[4], sems[5]), (sems[6], sems[7]),
            sems[8],
        )

    first, second = pl.pallas_call(
        kernel,
        out_shape=(
            jax.ShapeDtypeStruct((p_count, z_count, rows, half), piece.dtype),
            jax.ShapeDtypeStruct((z_count, p_count, rows, cols - half), piece.dtype),
        ),
        in_specs=[pl.BlockSpec(memory_space=pl.ANY)] * 2,
        out_specs=(pl.BlockSpec(memory_space=pl.ANY),) * 2,
        scratch_shapes=dma_pairs + [dma_pairs[2], dma_pairs[3], dma_pairs[0], dma_pairs[1]]
        + [pltpu.SemaphoreType.DMA((2,))],
        compiler_params=pltpu.CompilerParams(collective_id=kernel_id, has_side_effects=True),
    )(piece[:, :half], piece[:, half:])
    total = z_count * p_count * rows
    return jnp.concatenate(
        [
            first.transpose(1, 0, 2, 3).reshape(total, half),
            second.reshape(total, cols - half),
        ],
        axis=1,
    )


def _scatter_kernel(count, part_ref, out_ref, send_sems, recv_sems, local_sem):
    me = lax.axis_index("tp")
    width = out_ref.shape[2]
    mesh_ids = pl.DeviceIdType.MESH
    barrier = pltpu.get_barrier_semaphore()

    def greet(step, carry):
        peer = lax.rem(me + step, count)
        pl.semaphore_signal(barrier, 1, device_id={"tp": peer}, device_id_type=mesh_ids)
        return carry

    lax.fori_loop(1, count, greet, 0)
    pl.semaphore_wait(barrier, count - 1)

    def columns(index):
        return pl.ds(pl.multiple_of(index * width, width), width)

    own = pltpu.make_async_copy(part_ref.at[:, columns(me)], out_ref.at[me], local_sem)
    own.start()

    def remote(peer, slot):
        return pltpu.make_async_remote_copy(
            src_ref=part_ref.at[:, columns(peer)],
            dst_ref=out_ref.at[slot],
            send_sem=send_sems.at[peer],
            recv_sem=recv_sems.at[slot],
            device_id={"tp": peer},
            device_id_type=mesh_ids,
        )

    def send(step, carry):
        remote(lax.rem(me + step, count), me).start()
        return carry

    def finish(step, carry):
        peer = lax.rem(me + step, count)
        remote(peer, me).wait_send()
        remote(peer, peer).wait_recv()
        return carry

    lax.fori_loop(1, count, send, 0)
    lax.fori_loop(1, count, finish, 0)
    own.wait()


def scatter_sum_tp(part, count, kernel_id):
    rows, cols = part.shape
    pieces = pl.pallas_call(
        functools.partial(_scatter_kernel, count),
        out_shape=jax.ShapeDtypeStruct((count, rows, cols // count), part.dtype),
        in_specs=[pl.BlockSpec(memory_space=pl.ANY)],
        out_specs=pl.BlockSpec(memory_space=pl.ANY),
        scratch_shapes=[
            pltpu.SemaphoreType.DMA((count,)),
            pltpu.SemaphoreType.DMA((count,)),
            pltpu.SemaphoreType.DMA(()),
        ],
        compiler_params=pltpu.CompilerParams(collective_id=kernel_id, has_side_effects=True),
    )(part)
    return jnp.sum(pieces.astype(jnp.float32), axis=0)


def ctx_layout(mesh):
    count = mesh.shape["ctx"]
    column = mesh.devices.transpose(
        mesh.axis_names.index("ctx"), mesh.axis_names.index("tp")
    )[:, 0]
    try:
        planes = [device.coords[2] for device in column]
    except (AttributeError, IndexError, TypeError):
        return (count, 1)
    p_count = 1
    while p_count < count and planes[p_count] == planes[0]:
        p_count += 1
    if count % p_count:
        return (count, 1)
    for index in range(count):
        if planes[index] != planes[(index // p_count) * p_count]:
            return (count, 1)
    return (count // p_count, p_count)


def initial_positions(block_map, first_row, row_count, block_rows):
    row_ids = first_row + jnp.arange(row_count, dtype=jnp.int32)
    block_ids = row_ids // block_rows
    table_ids = jnp.arange(block_map.shape[0], dtype=jnp.int32)
    mapped = jnp.sum(
        jnp.where(block_ids[:, None] == table_ids[None, :], block_map[None, :], 0), axis=1
    )
    return mapped * block_rows + row_ids % block_rows


def request_index(positions, request_ends):
    return jnp.sum((positions[:, None] >= request_ends[None, :]).astype(jnp.int32), axis=1)


def round_weights(weights):
    rounded = weights.astype(jnp.bfloat16)
    rounded = lax.optimization_barrier(rounded)
    return rounded.astype(jnp.float32)


def softmax_parts(
    dec_heads, projected_key_rows, projected_value_rows, owned, kv_heads, head_dim, score_scale
):
    row_count = projected_key_rows.shape[0]
    scores = (
        jnp.einsum(
            "rgjd,tgd->rgjt",
            dec_heads,
            projected_key_rows.reshape(row_count, kv_heads, head_dim),
            preferred_element_type=jnp.float32,
        )
        * score_scale
    )
    scores = jnp.where(owned, scores, floor_value)
    part_peak = jnp.max(scores, axis=3)
    weights = jnp.where(owned, jnp.exp(scores - part_peak[..., None]), 0.0)
    part_total = jnp.sum(weights, axis=3)
    part_mixed = jnp.einsum(
        "rgjt,tgd->rgjd",
        weights.astype(jnp.bfloat16),
        projected_value_rows.reshape(row_count, kv_heads, head_dim),
        preferred_element_type=jnp.float32,
    )
    return (part_peak, part_total, part_mixed)


def on_device(
    layout, tp_count, tokens, new_token_states, w_query, key_matrix, value_matrix, w_out, lengths, block_map
):
    local_rows = tokens.shape[0]
    block_rows = local_rows // 2
    request_count = new_token_states.shape[0]
    head_dim = HEAD_SIZE
    query_width = w_query.shape[1]
    kv_width = key_matrix.shape[1]
    kv_heads = kv_width // head_dim
    query_group_count = query_width // kv_width
    score_scale = 1.0 / math.sqrt(head_dim)
    device = lax.axis_index("ctx")
    request_ends = jnp.cumsum(lengths)
    inputs = jnp.concatenate([tokens, new_token_states], axis=0)
    joined = gather_ctx(
        jnp.concatenate([w_query, key_matrix, value_matrix, w_out.T], axis=1), layout, 0
    )
    qkv_width = query_width + 2 * kv_width
    projected_all = jnp.dot(
        inputs, joined[:, :qkv_width], preferred_element_type=jnp.float32
    ).astype(jnp.bfloat16)
    out_weight = joined[:, qkv_width:].T
    query_all = projected_all[:, :query_width]
    key_all = projected_all[:, query_width : query_width + kv_width]
    value_all = projected_all[:, query_width + kv_width :]
    local_query = query_all[:local_rows]
    local_keys = key_all[:local_rows]
    local_values = value_all[:local_rows]
    dec_query = query_all[local_rows:]
    decode_key_rows = key_all[local_rows:]
    decode_value_rows = value_all[local_rows:]
    token_pos = initial_positions(block_map, device * local_rows, local_rows, block_rows)
    token_request = request_index(token_pos, request_ends)
    query_heads = local_query.reshape(local_rows, kv_heads, query_group_count, head_dim)

    def attend(running, shard_pieces, first_row):
        peak_run, total_run, mixed_run = running
        key_piece, value_piece = shard_pieces
        row_count = key_piece.shape[0]
        key_pos = initial_positions(block_map, first_row, row_count, block_rows)
        key_request = request_index(key_pos, request_ends)
        allowed = (key_request[None, :] == token_request[:, None]) & (
            key_pos[None, :] <= token_pos[:, None]
        )
        scores = (
            jnp.einsum(
                "tgjd,kgd->gjtk",
                query_heads,
                key_piece.reshape(row_count, kv_heads, head_dim),
                preferred_element_type=jnp.float32,
            )
            * score_scale
        )
        scores = jnp.where(allowed, scores, floor_value)
        peak_new = jnp.maximum(peak_run, jnp.max(scores, axis=3))
        weights = jnp.where(allowed, jnp.exp(scores - peak_new[..., None]), 0.0)
        rescale = jnp.exp(peak_run - peak_new)
        total_new = total_run * rescale + jnp.sum(weights, axis=3)
        mixed_new = mixed_run * rescale[..., None] + jnp.einsum(
            "gjtk,kgd->gjtd",
            weights.astype(jnp.bfloat16),
            value_piece.reshape(row_count, kv_heads, head_dim),
            preferred_element_type=jnp.float32,
        )
        return (peak_new, total_new, mixed_new)

    start_state = (
        jnp.full((kv_heads, query_group_count, local_rows), floor_value, jnp.float32),
        jnp.zeros((kv_heads, query_group_count, local_rows), jnp.float32),
        jnp.zeros((kv_heads, query_group_count, local_rows, head_dim), jnp.float32),
    )
    dec_heads = dec_query.reshape(request_count, kv_heads, query_group_count, head_dim)
    request_ids = jnp.arange(request_count, dtype=jnp.int32)
    cache_both = gather_ctx(
        jnp.concatenate([local_keys, local_values], axis=1), layout, 1
    )
    cache_keys = cache_both[:, :kv_width]
    cache_values = cache_both[:, kv_width:]
    total_rows = cache_keys.shape[0]
    shard_count = total_rows // local_rows
    limit = max(1, 1024 // local_rows)
    step_rows = local_rows * math.gcd(shard_count, 1 << limit.bit_length() - 1)

    def key_step(running, step_index):
        first_row = step_index * step_rows
        pieces = (
            lax.dynamic_slice_in_dim(cache_keys, first_row, step_rows, 0),
            lax.dynamic_slice_in_dim(cache_values, first_row, step_rows, 0),
        )
        return (attend(running, pieces, first_row), None)

    final_state, unused = lax.scan(
        key_step, start_state, jnp.arange(total_rows // step_rows, dtype=jnp.int32)
    )
    peak_run, total_run, mixed_run = final_state
    cache_pos = (
        block_map[:, None] * block_rows + jnp.arange(block_rows, dtype=jnp.int32)[None, :]
    ).reshape(total_rows)
    cache_request = request_index(cache_pos, request_ends)
    owned = (cache_request[None, :] == request_ids[:, None])[:, None, None, :]
    cache_peak, cache_total, cache_mixed = softmax_parts(
        dec_heads, cache_keys, cache_values, owned, kv_heads, head_dim, score_scale
    )
    attended = (
        (mixed_run / total_run[..., None]).transpose(2, 0, 1, 3).reshape(local_rows, query_width)
    )
    attended = attended.astype(jnp.bfloat16)
    own_keys = decode_key_rows.reshape(request_count, kv_heads, 1, head_dim).astype(jnp.float32)
    own_values = decode_value_rows.reshape(request_count, kv_heads, 1, head_dim).astype(jnp.float32)
    self_scores = jnp.sum(dec_heads.astype(jnp.float32) * own_keys, axis=3) * score_scale
    peak_all = jnp.maximum(cache_peak, self_scores)
    rescale = jnp.exp(cache_peak - peak_all)
    self_weights = jnp.exp(self_scores - peak_all)
    dec_total = cache_total * rescale + self_weights
    dec_mixed = (
        cache_mixed * rescale[..., None] + round_weights(self_weights)[..., None] * own_values
    )
    dec_attn = (
        (dec_mixed / dec_total[..., None]).reshape(request_count, query_width).astype(jnp.bfloat16)
    )
    attended_all = jnp.concatenate([attended, dec_attn], axis=0)
    projected = jnp.dot(
        attended_all,
        out_weight,
        preferred_element_type=jnp.float32,
    )
    summed_rows = scatter_sum_tp(projected.astype(jnp.bfloat16), tp_count, 2)
    summed_rows = summed_rows.astype(jnp.bfloat16)
    return (summed_rows[:local_rows], summed_rows[local_rows:])


def solution(mesh):
    return jax.shard_map(
        functools.partial(on_device, ctx_layout(mesh), mesh.shape["tp"]),
        mesh=mesh,
        in_specs=(
            P("ctx", None),
            P(),
            P("ctx", "tp"),
            P("ctx", "tp"),
            P("ctx", "tp"),
            P("tp", "ctx"),
            P(),
            P(),
        ),
        out_specs=(P("ctx", "tp"), P(None, "tp")),
        check_vma=False,
    )
```

```python
import functools
import math

import jax
import jax.numpy as jnp
from jax import lax
from jax.experimental import pallas as pl
from jax.experimental.pallas import tpu as pltpu
from jax.sharding import PartitionSpec as P

HEAD_SIZE = 128


floor_value = -1e30


def _gather_kernel(
    z_count,
    p_count,
    first_ref,
    second_ref,
    first_out,
    second_out,
    first_z,
    first_p,
    second_p,
    second_z,
    local_sems,
):
    me = lax.axis_index("ctx")
    z_me = me // p_count
    p_me = lax.rem(me, p_count)
    mesh_ids = pl.DeviceIdType.MESH
    barrier = pltpu.get_barrier_semaphore()

    def z_peer(step):
        return lax.rem(z_me + step, z_count)

    def p_peer(step):
        return lax.rem(p_me + step, p_count)

    def z_target(peer):
        return peer * p_count + p_me

    def p_target(peer):
        return z_me * p_count + peer

    def greet(peer_of, target_of):
        def body(step, carry):
            pl.semaphore_signal(
                barrier, 1, device_id={"ctx": target_of(peer_of(step))}, device_id_type=mesh_ids
            )
            return carry

        return body

    lax.fori_loop(1, z_count, greet(z_peer, z_target), 0)
    lax.fori_loop(1, p_count, greet(p_peer, p_target), 0)
    pl.semaphore_wait(barrier, z_count + p_count - 2)

    def exchange(count, peer_of, target_of, own_slot, src_of, dst_of, sems):
        send_sems, recv_sems = sems

        def copy(peer, slot):
            return pltpu.make_async_remote_copy(
                src_ref=src_of(slot),
                dst_ref=dst_of(slot),
                send_sem=send_sems.at[peer],
                recv_sem=recv_sems.at[slot],
                device_id={"ctx": target_of(peer)},
                device_id_type=mesh_ids,
            )

        def start(step, carry):
            copy(peer_of(step), own_slot).start()
            return carry

        def finish(step, carry):
            peer = peer_of(step)
            copy(peer, own_slot).wait_send()
            copy(peer, peer).wait_recv()
            return carry

        return (lambda: lax.fori_loop(1, count, start, 0), lambda: lax.fori_loop(1, count, finish, 0))

    first_own = pltpu.make_async_copy(first_ref, first_out.at[p_me, z_me], local_sems.at[0])
    second_own = pltpu.make_async_copy(second_ref, second_out.at[z_me, p_me], local_sems.at[1])
    first_own.start()
    second_own.start()
    first_one = exchange(
        z_count, z_peer, z_target, z_me,
        lambda slot: first_ref, lambda slot: first_out.at[p_me, slot], first_z,
    )
    second_one = exchange(
        p_count, p_peer, p_target, p_me,
        lambda slot: second_ref, lambda slot: second_out.at[z_me, slot], second_p,
    )
    first_two = exchange(
        p_count, p_peer, p_target, p_me,
        lambda slot: first_out.at[slot], lambda slot: first_out.at[slot], first_p,
    )
    second_two = exchange(
        z_count, z_peer, z_target, z_me,
        lambda slot: second_out.at[slot], lambda slot: second_out.at[slot], second_z,
    )
    first_one[0]()
    second_one[0]()
    first_one[1]()
    first_own.wait()
    first_two[0]()
    second_one[1]()
    second_own.wait()
    second_two[0]()
    first_two[1]()
    second_two[1]()


def gather_ctx(piece, layout, kernel_id):
    z_count, p_count = layout
    rows, cols = piece.shape
    half = cols // 2
    dma_pairs = [
        pltpu.SemaphoreType.DMA((z_count,)),
        pltpu.SemaphoreType.DMA((z_count,)),
        pltpu.SemaphoreType.DMA((p_count,)),
        pltpu.SemaphoreType.DMA((p_count,)),
    ]

    def kernel(first_ref, second_ref, first_out, second_out, *sems):
        _gather_kernel(
            z_count, p_count, first_ref, second_ref, first_out, second_out,
            (sems[0], sems[1]), (sems[2], sems[3]), (sems[4], sems[5]), (sems[6], sems[7]),
            sems[8],
        )

    first, second = pl.pallas_call(
        kernel,
        out_shape=(
            jax.ShapeDtypeStruct((p_count, z_count, rows, half), piece.dtype),
            jax.ShapeDtypeStruct((z_count, p_count, rows, cols - half), piece.dtype),
        ),
        in_specs=[pl.BlockSpec(memory_space=pl.ANY)] * 2,
        out_specs=(pl.BlockSpec(memory_space=pl.ANY),) * 2,
        scratch_shapes=dma_pairs + [dma_pairs[2], dma_pairs[3], dma_pairs[0], dma_pairs[1]]
        + [pltpu.SemaphoreType.DMA((2,))],
        compiler_params=pltpu.CompilerParams(collective_id=kernel_id, has_side_effects=True),
    )(piece[:, :half], piece[:, half:])
    total = z_count * p_count * rows
    return jnp.concatenate(
        [
            first.transpose(1, 0, 2, 3).reshape(total, half),
            second.reshape(total, cols - half),
        ],
        axis=1,
    )


def _scatter_kernel(count, part_ref, out_ref, send_sems, recv_sems, local_sem):
    me = lax.axis_index("tp")
    width = out_ref.shape[2]
    mesh_ids = pl.DeviceIdType.MESH
    barrier = pltpu.get_barrier_semaphore()

    def greet(step, carry):
        peer = lax.rem(me + step, count)
        pl.semaphore_signal(barrier, 1, device_id={"tp": peer}, device_id_type=mesh_ids)
        return carry

    lax.fori_loop(1, count, greet, 0)
    pl.semaphore_wait(barrier, count - 1)

    def columns(index):
        return pl.ds(pl.multiple_of(index * width, width), width)

    own = pltpu.make_async_copy(part_ref.at[:, columns(me)], out_ref.at[me], local_sem)
    own.start()

    def remote(peer, slot):
        return pltpu.make_async_remote_copy(
            src_ref=part_ref.at[:, columns(peer)],
            dst_ref=out_ref.at[slot],
            send_sem=send_sems.at[peer],
            recv_sem=recv_sems.at[slot],
            device_id={"tp": peer},
            device_id_type=mesh_ids,
        )

    def send(step, carry):
        remote(lax.rem(me + step, count), me).start()
        return carry

    def finish(step, carry):
        peer = lax.rem(me + step, count)
        remote(peer, me).wait_send()
        remote(peer, peer).wait_recv()
        return carry

    lax.fori_loop(1, count, send, 0)
    lax.fori_loop(1, count, finish, 0)
    own.wait()


def scatter_sum_tp(part, count, kernel_id):
    rows, cols = part.shape
    pieces = pl.pallas_call(
        functools.partial(_scatter_kernel, count),
        out_shape=jax.ShapeDtypeStruct((count, rows, cols // count), part.dtype),
        in_specs=[pl.BlockSpec(memory_space=pl.ANY)],
        out_specs=pl.BlockSpec(memory_space=pl.ANY),
        scratch_shapes=[
            pltpu.SemaphoreType.DMA((count,)),
            pltpu.SemaphoreType.DMA((count,)),
            pltpu.SemaphoreType.DMA(()),
        ],
        compiler_params=pltpu.CompilerParams(collective_id=kernel_id, has_side_effects=True),
    )(part)
    return jnp.sum(pieces.astype(jnp.float32), axis=0)


def ctx_layout(mesh):
    count = mesh.shape["ctx"]
    column = mesh.devices.transpose(
        mesh.axis_names.index("ctx"), mesh.axis_names.index("tp")
    )[:, 0]
    try:
        planes = [device.coords[2] for device in column]
    except (AttributeError, IndexError, TypeError):
        return (count, 1)
    p_count = 1
    while p_count < count and planes[p_count] == planes[0]:
        p_count += 1
    if count % p_count:
        return (count, 1)
    for index in range(count):
        if planes[index] != planes[(index // p_count) * p_count]:
            return (count, 1)
    return (count // p_count, p_count)


def initial_positions(block_map, first_row, row_count, block_rows):
    row_ids = first_row + jnp.arange(row_count, dtype=jnp.int32)
    block_ids = row_ids // block_rows
    table_ids = jnp.arange(block_map.shape[0], dtype=jnp.int32)
    mapped = jnp.sum(
        jnp.where(block_ids[:, None] == table_ids[None, :], block_map[None, :], 0), axis=1
    )
    return mapped * block_rows + row_ids % block_rows


def request_index(positions, request_ends):
    return jnp.sum((positions[:, None] >= request_ends[None, :]).astype(jnp.int32), axis=1)


def round_weights(weights):
    rounded = weights.astype(jnp.bfloat16)
    rounded = lax.optimization_barrier(rounded)
    return rounded.astype(jnp.float32)


def softmax_parts(
    dec_heads, projected_key_rows, projected_value_rows, owned, kv_heads, head_dim, score_scale
):
    row_count = projected_key_rows.shape[0]
    scores = (
        jnp.einsum(
            "rgjd,tgd->rgjt",
            dec_heads,
            projected_key_rows.reshape(row_count, kv_heads, head_dim),
            preferred_element_type=jnp.float32,
        )
        * score_scale
    )
    scores = jnp.where(owned, scores, floor_value)
    part_peak = jnp.max(scores, axis=3)
    weights = jnp.where(owned, jnp.exp(scores - part_peak[..., None]), 0.0)
    part_total = jnp.sum(weights, axis=3)
    part_mixed = jnp.einsum(
        "rgjt,tgd->rgjd",
        weights.astype(jnp.bfloat16),
        projected_value_rows.reshape(row_count, kv_heads, head_dim),
        preferred_element_type=jnp.float32,
    )
    return (part_peak, part_total, part_mixed)


def on_device(
    layout, tp_count, tokens, new_token_states, w_query, key_matrix, value_matrix, w_out, lengths, block_map
):
    local_rows = tokens.shape[0]
    block_rows = local_rows // 2
    request_count = new_token_states.shape[0]
    head_dim = HEAD_SIZE
    query_width = w_query.shape[1]
    kv_width = key_matrix.shape[1]
    kv_heads = kv_width // head_dim
    query_group_count = query_width // kv_width
    score_scale = 1.0 / math.sqrt(head_dim)
    device = lax.axis_index("ctx")
    request_ends = jnp.cumsum(lengths)
    inputs = jnp.concatenate([tokens, new_token_states], axis=0)
    joined = gather_ctx(
        jnp.concatenate([w_query, key_matrix, value_matrix, w_out.T], axis=1), layout, 0
    )
    qkv_width = query_width + 2 * kv_width
    projected_all = jnp.dot(
        inputs, joined[:, :qkv_width], preferred_element_type=jnp.float32
    ).astype(jnp.bfloat16)
    out_weight = joined[:, qkv_width:].T
    query_all = projected_all[:, :query_width]
    key_all = projected_all[:, query_width : query_width + kv_width]
    value_all = projected_all[:, query_width + kv_width :]
    local_query = query_all[:local_rows]
    local_keys = key_all[:local_rows]
    local_values = value_all[:local_rows]
    dec_query = query_all[local_rows:]
    decode_key_rows = key_all[local_rows:]
    decode_value_rows = value_all[local_rows:]
    token_pos = initial_positions(block_map, device * local_rows, local_rows, block_rows)
    token_request = request_index(token_pos, request_ends)
    query_heads = local_query.reshape(local_rows, kv_heads, query_group_count, head_dim)

    def attend(running, shard_pieces, first_row):
        peak_run, total_run, mixed_run = running
        key_piece, value_piece = shard_pieces
        row_count = key_piece.shape[0]
        key_pos = lax.dynamic_slice_in_dim(cache_pos, first_row, row_count, 0)
        key_request = lax.dynamic_slice_in_dim(cache_request, first_row, row_count, 0)
        allowed = (key_request[None, :] == token_request[:, None]) & (
            key_pos[None, :] <= token_pos[:, None]
        )
        scores = (
            jnp.einsum(
                "tgjd,kgd->gjtk",
                query_heads,
                key_piece.reshape(row_count, kv_heads, head_dim),
                preferred_element_type=jnp.float32,
            )
            * score_scale
        )
        scores = jnp.where(allowed, scores, floor_value)
        peak_new = jnp.maximum(peak_run, jnp.max(scores, axis=3))
        weights = jnp.where(allowed, jnp.exp(scores - peak_new[..., None]), 0.0)
        rescale = jnp.exp(peak_run - peak_new)
        total_new = total_run * rescale + jnp.sum(weights, axis=3)
        mixed_new = mixed_run * rescale[..., None] + jnp.einsum(
            "gjtk,kgd->gjtd",
            weights.astype(jnp.bfloat16),
            value_piece.reshape(row_count, kv_heads, head_dim),
            preferred_element_type=jnp.float32,
        )
        return (peak_new, total_new, mixed_new)

    start_state = (
        jnp.full((kv_heads, query_group_count, local_rows), floor_value, jnp.float32),
        jnp.zeros((kv_heads, query_group_count, local_rows), jnp.float32),
        jnp.zeros((kv_heads, query_group_count, local_rows, head_dim), jnp.float32),
    )
    dec_heads = dec_query.reshape(request_count, kv_heads, query_group_count, head_dim)
    request_ids = jnp.arange(request_count, dtype=jnp.int32)
    cache_both = gather_ctx(
        jnp.concatenate([local_keys, local_values], axis=1), layout, 1
    )
    cache_keys = cache_both[:, :kv_width]
    cache_values = cache_both[:, kv_width:]
    total_rows = cache_keys.shape[0]
    step_rows = total_rows
    cache_pos = (
        block_map[:, None] * block_rows + jnp.arange(block_rows, dtype=jnp.int32)[None, :]
    ).reshape(total_rows)
    cache_request = request_index(cache_pos, request_ends)

    def key_step(running, step_index):
        first_row = step_index * step_rows
        pieces = (
            lax.dynamic_slice_in_dim(cache_keys, first_row, step_rows, 0),
            lax.dynamic_slice_in_dim(cache_values, first_row, step_rows, 0),
        )
        return (attend(running, pieces, first_row), None)

    final_state, unused = lax.scan(
        key_step, start_state, jnp.arange(total_rows // step_rows, dtype=jnp.int32)
    )
    peak_run, total_run, mixed_run = final_state
    owned = (cache_request[None, :] == request_ids[:, None])[:, None, None, :]
    cache_peak, cache_total, cache_mixed = softmax_parts(
        dec_heads, cache_keys, cache_values, owned, kv_heads, head_dim, score_scale
    )
    attended = (
        (mixed_run / total_run[..., None]).transpose(2, 0, 1, 3).reshape(local_rows, query_width)
    )
    attended = attended.astype(jnp.bfloat16)
    own_keys = decode_key_rows.reshape(request_count, kv_heads, 1, head_dim).astype(jnp.float32)
    own_values = decode_value_rows.reshape(request_count, kv_heads, 1, head_dim).astype(jnp.float32)
    self_scores = jnp.sum(dec_heads.astype(jnp.float32) * own_keys, axis=3) * score_scale
    peak_all = jnp.maximum(cache_peak, self_scores)
    rescale = jnp.exp(cache_peak - peak_all)
    self_weights = jnp.exp(self_scores - peak_all)
    dec_total = cache_total * rescale + self_weights
    dec_mixed = (
        cache_mixed * rescale[..., None] + round_weights(self_weights)[..., None] * own_values
    )
    dec_attn = (
        (dec_mixed / dec_total[..., None]).reshape(request_count, query_width).astype(jnp.bfloat16)
    )
    attended_all = jnp.concatenate([attended, dec_attn], axis=0)
    projected = jnp.dot(
        attended_all,
        out_weight,
        preferred_element_type=jnp.float32,
    )
    summed_rows = scatter_sum_tp(projected.astype(jnp.bfloat16), tp_count, 2)
    summed_rows = summed_rows.astype(jnp.bfloat16)
    return (summed_rows[:local_rows], summed_rows[local_rows:])


def solution(mesh):
    return jax.shard_map(
        functools.partial(on_device, ctx_layout(mesh), mesh.shape["tp"]),
        mesh=mesh,
        in_specs=(
            P("ctx", None),
            P(),
            P("ctx", "tp"),
            P("ctx", "tp"),
            P("ctx", "tp"),
            P("tp", "ctx"),
            P(),
            P(),
        ),
        out_specs=(P("ctx", "tp"), P(None, "tp")),
        check_vma=False,
    )
```

```python
import functools
import math

import jax
import jax.numpy as jnp
from jax import lax
from jax.experimental import pallas as pl
from jax.experimental.pallas import tpu as pltpu
from jax.sharding import PartitionSpec as P

HEAD_SIZE = 128


floor_value = -1e30


def _gather_kernel(
    z_count,
    p_count,
    first_ref,
    second_ref,
    first_out,
    second_out,
    first_z,
    first_p,
    second_p,
    second_z,
    local_sems,
):
    me = lax.axis_index("ctx")
    z_me = me // p_count
    p_me = lax.rem(me, p_count)
    mesh_ids = pl.DeviceIdType.MESH
    barrier = pltpu.get_barrier_semaphore()

    def z_peer(step):
        return lax.rem(z_me + step, z_count)

    def p_peer(step):
        return lax.rem(p_me + step, p_count)

    def z_target(peer):
        return peer * p_count + p_me

    def p_target(peer):
        return z_me * p_count + peer

    def greet(peer_of, target_of):
        def body(step, carry):
            pl.semaphore_signal(
                barrier, 1, device_id={"ctx": target_of(peer_of(step))}, device_id_type=mesh_ids
            )
            return carry

        return body

    lax.fori_loop(1, z_count, greet(z_peer, z_target), 0)
    lax.fori_loop(1, p_count, greet(p_peer, p_target), 0)
    pl.semaphore_wait(barrier, z_count + p_count - 2)

    def exchange(count, peer_of, target_of, own_slot, src_of, dst_of, sems):
        send_sems, recv_sems = sems

        def copy(peer, slot):
            return pltpu.make_async_remote_copy(
                src_ref=src_of(slot),
                dst_ref=dst_of(slot),
                send_sem=send_sems.at[peer],
                recv_sem=recv_sems.at[slot],
                device_id={"ctx": target_of(peer)},
                device_id_type=mesh_ids,
            )

        def start(step, carry):
            copy(peer_of(step), own_slot).start()
            return carry

        def finish(step, carry):
            peer = peer_of(step)
            copy(peer, own_slot).wait_send()
            copy(peer, peer).wait_recv()
            return carry

        return (lambda: lax.fori_loop(1, count, start, 0), lambda: lax.fori_loop(1, count, finish, 0))

    first_own = pltpu.make_async_copy(first_ref, first_out.at[p_me, z_me], local_sems.at[0])
    second_own = pltpu.make_async_copy(second_ref, second_out.at[z_me, p_me], local_sems.at[1])
    first_own.start()
    second_own.start()
    first_one = exchange(
        z_count, z_peer, z_target, z_me,
        lambda slot: first_ref, lambda slot: first_out.at[p_me, slot], first_z,
    )
    second_one = exchange(
        p_count, p_peer, p_target, p_me,
        lambda slot: second_ref, lambda slot: second_out.at[z_me, slot], second_p,
    )
    first_two = exchange(
        p_count, p_peer, p_target, p_me,
        lambda slot: first_out.at[slot], lambda slot: first_out.at[slot], first_p,
    )
    second_two = exchange(
        z_count, z_peer, z_target, z_me,
        lambda slot: second_out.at[slot], lambda slot: second_out.at[slot], second_z,
    )
    first_one[0]()
    second_one[0]()
    first_one[1]()
    first_own.wait()
    first_two[0]()
    second_one[1]()
    second_own.wait()
    second_two[0]()
    first_two[1]()
    second_two[1]()


def gather_ctx(piece, layout, kernel_id):
    z_count, p_count = layout
    rows, cols = piece.shape
    tile = 16
    head = min(rows - tile, max(tile, round(rows * 2 / (3 * tile)) * tile))
    tail = rows - head
    dma_pairs = [
        pltpu.SemaphoreType.DMA((z_count,)),
        pltpu.SemaphoreType.DMA((z_count,)),
        pltpu.SemaphoreType.DMA((p_count,)),
        pltpu.SemaphoreType.DMA((p_count,)),
    ]

    def kernel(first_ref, second_ref, first_out, second_out, *sems):
        _gather_kernel(
            z_count, p_count, first_ref, second_ref, first_out, second_out,
            (sems[0], sems[1]), (sems[2], sems[3]), (sems[4], sems[5]), (sems[6], sems[7]),
            sems[8],
        )

    first, second = pl.pallas_call(
        kernel,
        out_shape=(
            jax.ShapeDtypeStruct((p_count, z_count, head, cols), piece.dtype),
            jax.ShapeDtypeStruct((z_count, p_count, tail, cols), piece.dtype),
        ),
        in_specs=[pl.BlockSpec(memory_space=pl.ANY)] * 2,
        out_specs=(pl.BlockSpec(memory_space=pl.ANY),) * 2,
        scratch_shapes=dma_pairs + [dma_pairs[2], dma_pairs[3], dma_pairs[0], dma_pairs[1]]
        + [pltpu.SemaphoreType.DMA((2,))],
        compiler_params=pltpu.CompilerParams(collective_id=kernel_id, has_side_effects=True),
    )(piece[:head], piece[head:])
    joined = jnp.concatenate([first.transpose(1, 0, 2, 3), second], axis=2)
    return joined.reshape(z_count * p_count * rows, cols)


def _scatter_kernel(count, part_ref, out_ref, send_sems, recv_sems, local_sem):
    me = lax.axis_index("tp")
    width = out_ref.shape[2]
    mesh_ids = pl.DeviceIdType.MESH
    barrier = pltpu.get_barrier_semaphore()

    def greet(step, carry):
        peer = lax.rem(me + step, count)
        pl.semaphore_signal(barrier, 1, device_id={"tp": peer}, device_id_type=mesh_ids)
        return carry

    lax.fori_loop(1, count, greet, 0)
    pl.semaphore_wait(barrier, count - 1)

    def columns(index):
        return pl.ds(pl.multiple_of(index * width, width), width)

    own = pltpu.make_async_copy(part_ref.at[:, columns(me)], out_ref.at[me], local_sem)
    own.start()

    def remote(peer, slot):
        return pltpu.make_async_remote_copy(
            src_ref=part_ref.at[:, columns(peer)],
            dst_ref=out_ref.at[slot],
            send_sem=send_sems.at[peer],
            recv_sem=recv_sems.at[slot],
            device_id={"tp": peer},
            device_id_type=mesh_ids,
        )

    def send(step, carry):
        remote(lax.rem(me + step, count), me).start()
        return carry

    def finish(step, carry):
        peer = lax.rem(me + step, count)
        remote(peer, me).wait_send()
        remote(peer, peer).wait_recv()
        return carry

    lax.fori_loop(1, count, send, 0)
    lax.fori_loop(1, count, finish, 0)
    own.wait()


def scatter_sum_tp(part, count, kernel_id):
    rows, cols = part.shape
    pieces = pl.pallas_call(
        functools.partial(_scatter_kernel, count),
        out_shape=jax.ShapeDtypeStruct((count, rows, cols // count), part.dtype),
        in_specs=[pl.BlockSpec(memory_space=pl.ANY)],
        out_specs=pl.BlockSpec(memory_space=pl.ANY),
        scratch_shapes=[
            pltpu.SemaphoreType.DMA((count,)),
            pltpu.SemaphoreType.DMA((count,)),
            pltpu.SemaphoreType.DMA(()),
        ],
        compiler_params=pltpu.CompilerParams(collective_id=kernel_id, has_side_effects=True),
    )(part)
    return jnp.sum(pieces.astype(jnp.float32), axis=0)


def ctx_layout(mesh):
    count = mesh.shape["ctx"]
    column = mesh.devices.transpose(
        mesh.axis_names.index("ctx"), mesh.axis_names.index("tp")
    )[:, 0]
    try:
        planes = [device.coords[2] for device in column]
    except (AttributeError, IndexError, TypeError):
        return (count, 1)
    p_count = 1
    while p_count < count and planes[p_count] == planes[0]:
        p_count += 1
    if count % p_count:
        return (count, 1)
    for index in range(count):
        if planes[index] != planes[(index // p_count) * p_count]:
            return (count, 1)
    return (count // p_count, p_count)


def initial_positions(block_map, first_row, row_count, block_rows):
    row_ids = first_row + jnp.arange(row_count, dtype=jnp.int32)
    block_ids = row_ids // block_rows
    table_ids = jnp.arange(block_map.shape[0], dtype=jnp.int32)
    mapped = jnp.sum(
        jnp.where(block_ids[:, None] == table_ids[None, :], block_map[None, :], 0), axis=1
    )
    return mapped * block_rows + row_ids % block_rows


def request_index(positions, request_ends):
    return jnp.sum((positions[:, None] >= request_ends[None, :]).astype(jnp.int32), axis=1)


def round_weights(weights):
    rounded = weights.astype(jnp.bfloat16)
    rounded = lax.optimization_barrier(rounded)
    return rounded.astype(jnp.float32)


def softmax_parts(
    dec_heads, projected_key_rows, projected_value_rows, owned, kv_heads, head_dim, score_scale
):
    row_count = projected_key_rows.shape[0]
    scores = (
        jnp.einsum(
            "rgjd,tgd->rgjt",
            dec_heads,
            projected_key_rows.reshape(row_count, kv_heads, head_dim),
            preferred_element_type=jnp.float32,
        )
        * score_scale
    )
    scores = jnp.where(owned, scores, floor_value)
    part_peak = jnp.max(scores, axis=3)
    weights = jnp.where(owned, jnp.exp(scores - part_peak[..., None]), 0.0)
    part_total = jnp.sum(weights, axis=3)
    part_mixed = jnp.einsum(
        "rgjt,tgd->rgjd",
        weights.astype(jnp.bfloat16),
        projected_value_rows.reshape(row_count, kv_heads, head_dim),
        preferred_element_type=jnp.float32,
    )
    return (part_peak, part_total, part_mixed)


def on_device(
    layout, tp_count, tokens, new_token_states, w_query, key_matrix, value_matrix, w_out, lengths, block_map
):
    local_rows = tokens.shape[0]
    block_rows = local_rows // 2
    request_count = new_token_states.shape[0]
    head_dim = HEAD_SIZE
    query_width = w_query.shape[1]
    kv_width = key_matrix.shape[1]
    kv_heads = kv_width // head_dim
    query_group_count = query_width // kv_width
    score_scale = 1.0 / math.sqrt(head_dim)
    device = lax.axis_index("ctx")
    request_ends = jnp.cumsum(lengths)
    inputs = jnp.concatenate([tokens, new_token_states], axis=0)
    joined = gather_ctx(
        jnp.concatenate([w_query, key_matrix, value_matrix, w_out.T], axis=1), layout, 0
    )
    qkv_width = query_width + 2 * kv_width
    projected_all = jnp.dot(
        inputs, joined[:, :qkv_width], preferred_element_type=jnp.float32
    ).astype(jnp.bfloat16)
    out_weight = joined[:, qkv_width:].T
    query_all = projected_all[:, :query_width]
    key_all = projected_all[:, query_width : query_width + kv_width]
    value_all = projected_all[:, query_width + kv_width :]
    local_query = query_all[:local_rows]
    local_keys = key_all[:local_rows]
    local_values = value_all[:local_rows]
    dec_query = query_all[local_rows:]
    decode_key_rows = key_all[local_rows:]
    decode_value_rows = value_all[local_rows:]
    token_pos = initial_positions(block_map, device * local_rows, local_rows, block_rows)
    token_request = request_index(token_pos, request_ends)
    query_heads = local_query.reshape(local_rows, kv_heads, query_group_count, head_dim)

    def attend(running, shard_pieces, first_row):
        peak_run, total_run, mixed_run = running
        key_piece, value_piece = shard_pieces
        row_count = key_piece.shape[0]
        key_pos = lax.dynamic_slice_in_dim(cache_pos, first_row, row_count, 0)
        key_request = lax.dynamic_slice_in_dim(cache_request, first_row, row_count, 0)
        allowed = (key_request[None, :] == token_request[:, None]) & (
            key_pos[None, :] <= token_pos[:, None]
        )
        scores = (
            jnp.einsum(
                "tgjd,kgd->gjtk",
                query_heads,
                key_piece.reshape(row_count, kv_heads, head_dim),
                preferred_element_type=jnp.float32,
            )
            * score_scale
        )
        scores = jnp.where(allowed, scores, floor_value)
        peak_new = jnp.maximum(peak_run, jnp.max(scores, axis=3))
        weights = jnp.where(allowed, jnp.exp(scores - peak_new[..., None]), 0.0)
        rescale = jnp.exp(peak_run - peak_new)
        total_new = total_run * rescale + jnp.sum(weights, axis=3)
        mixed_new = mixed_run * rescale[..., None] + jnp.einsum(
            "gjtk,kgd->gjtd",
            weights.astype(jnp.bfloat16),
            value_piece.reshape(row_count, kv_heads, head_dim),
            preferred_element_type=jnp.float32,
        )
        return (peak_new, total_new, mixed_new)

    start_state = (
        jnp.full((kv_heads, query_group_count, local_rows), floor_value, jnp.float32),
        jnp.zeros((kv_heads, query_group_count, local_rows), jnp.float32),
        jnp.zeros((kv_heads, query_group_count, local_rows, head_dim), jnp.float32),
    )
    dec_heads = dec_query.reshape(request_count, kv_heads, query_group_count, head_dim)
    request_ids = jnp.arange(request_count, dtype=jnp.int32)
    cache_both = gather_ctx(
        jnp.concatenate([local_keys, local_values], axis=1), layout, 1
    )
    cache_keys = cache_both[:, :kv_width]
    cache_values = cache_both[:, kv_width:]
    total_rows = cache_keys.shape[0]
    step_rows = total_rows
    cache_pos = (
        block_map[:, None] * block_rows + jnp.arange(block_rows, dtype=jnp.int32)[None, :]
    ).reshape(total_rows)
    cache_request = request_index(cache_pos, request_ends)

    def key_step(running, step_index):
        first_row = step_index * step_rows
        pieces = (
            lax.dynamic_slice_in_dim(cache_keys, first_row, step_rows, 0),
            lax.dynamic_slice_in_dim(cache_values, first_row, step_rows, 0),
        )
        return (attend(running, pieces, first_row), None)

    final_state, unused = lax.scan(
        key_step, start_state, jnp.arange(total_rows // step_rows, dtype=jnp.int32)
    )
    peak_run, total_run, mixed_run = final_state
    owned = (cache_request[None, :] == request_ids[:, None])[:, None, None, :]
    cache_peak, cache_total, cache_mixed = softmax_parts(
        dec_heads, cache_keys, cache_values, owned, kv_heads, head_dim, score_scale
    )
    attended = (
        (mixed_run / total_run[..., None]).transpose(2, 0, 1, 3).reshape(local_rows, query_width)
    )
    attended = attended.astype(jnp.bfloat16)
    own_keys = decode_key_rows.reshape(request_count, kv_heads, 1, head_dim).astype(jnp.float32)
    own_values = decode_value_rows.reshape(request_count, kv_heads, 1, head_dim).astype(jnp.float32)
    self_scores = jnp.sum(dec_heads.astype(jnp.float32) * own_keys, axis=3) * score_scale
    peak_all = jnp.maximum(cache_peak, self_scores)
    rescale = jnp.exp(cache_peak - peak_all)
    self_weights = jnp.exp(self_scores - peak_all)
    dec_total = cache_total * rescale + self_weights
    dec_mixed = (
        cache_mixed * rescale[..., None] + round_weights(self_weights)[..., None] * own_values
    )
    dec_attn = (
        (dec_mixed / dec_total[..., None]).reshape(request_count, query_width).astype(jnp.bfloat16)
    )
    attended_all = jnp.concatenate([attended, dec_attn], axis=0)
    projected = jnp.dot(
        attended_all,
        out_weight,
        preferred_element_type=jnp.float32,
    )
    summed_rows = scatter_sum_tp(projected.astype(jnp.bfloat16), tp_count, 2)
    summed_rows = summed_rows.astype(jnp.bfloat16)
    return (summed_rows[:local_rows], summed_rows[local_rows:])


def solution(mesh):
    return jax.shard_map(
        functools.partial(on_device, ctx_layout(mesh), mesh.shape["tp"]),
        mesh=mesh,
        in_specs=(
            P("ctx", None),
            P(),
            P("ctx", "tp"),
            P("ctx", "tp"),
            P("ctx", "tp"),
            P("tp", "ctx"),
            P(),
            P(),
        ),
        out_specs=(P("ctx", "tp"), P(None, "tp")),
        check_vma=False,
    )
```

```python
import functools
import math

import jax
import jax.numpy as jnp
from jax import lax
from jax.experimental import pallas as pl
from jax.experimental.pallas import tpu as pltpu
from jax.sharding import PartitionSpec as P

HEAD_SIZE = 128


floor_value = -1e30


def _gather_kernel(
    z_count,
    p_count,
    first_ref,
    second_ref,
    first_out,
    second_out,
    first_z,
    first_p,
    second_p,
    second_z,
    local_sems,
):
    me = lax.axis_index("ctx")
    z_me = me // p_count
    p_me = lax.rem(me, p_count)
    mesh_ids = pl.DeviceIdType.MESH
    barrier = pltpu.get_barrier_semaphore()

    def z_peer(step):
        return lax.rem(z_me + step, z_count)

    def p_peer(step):
        return lax.rem(p_me + step, p_count)

    def z_target(peer):
        return peer * p_count + p_me

    def p_target(peer):
        return z_me * p_count + peer

    def greet(peer_of, target_of):
        def body(step, carry):
            pl.semaphore_signal(
                barrier, 1, device_id={"ctx": target_of(peer_of(step))}, device_id_type=mesh_ids
            )
            return carry

        return body

    lax.fori_loop(1, z_count, greet(z_peer, z_target), 0)
    lax.fori_loop(1, p_count, greet(p_peer, p_target), 0)
    pl.semaphore_wait(barrier, z_count + p_count - 2)

    def remote(src, dst, send_sem, recv_sem, target):
        return pltpu.make_async_remote_copy(
            src_ref=src,
            dst_ref=dst,
            send_sem=send_sem,
            recv_sem=recv_sem,
            device_id={"ctx": target},
            device_id_type=mesh_ids,
        )

    def first_one(peer, slot):
        return remote(
            first_ref, first_out.at[p_me, slot], first_z[0].at[peer], first_z[1].at[slot],
            z_target(peer),
        )

    def second_one(peer, slot):
        return remote(
            second_ref, second_out.at[z_me, slot], second_p[0].at[peer], second_p[1].at[slot],
            p_target(peer),
        )

    def first_two(peer, row, slot):
        return remote(
            first_out.at[row, slot], first_out.at[row, slot], first_p[0].at[peer],
            first_p[1].at[row], p_target(peer),
        )

    def second_two(peer, row, slot):
        return remote(
            second_out.at[row, slot], second_out.at[row, slot], second_z[0].at[peer],
            second_z[1].at[row], z_target(peer),
        )

    def first_rows(peer, row):
        return remote(
            first_out.at[row], first_out.at[row], first_p[0].at[peer], first_p[1].at[row],
            p_target(peer),
        )

    def second_rows(peer, row):
        return remote(
            second_out.at[row], second_out.at[row], second_z[0].at[peer], second_z[1].at[row],
            z_target(peer),
        )

    first_own = pltpu.make_async_copy(first_ref, first_out.at[p_me, z_me], local_sems.at[0])
    second_own = pltpu.make_async_copy(second_ref, second_out.at[z_me, p_me], local_sems.at[1])
    first_own.start()
    second_own.start()

    def start_one(step, carry):
        @pl.when(step < z_count)
        def _():
            first_one(z_peer(step), z_me).start()

        @pl.when(step < p_count)
        def _():
            second_one(p_peer(step), p_me).start()

        return carry

    rounds = max(z_count, p_count)
    lax.fori_loop(1, rounds, start_one, 0)

    def forward_first(slot):
        def body(step, carry):
            first_two(p_peer(step), p_me, slot).start()
            return carry

        lax.fori_loop(1, p_count, body, 0)

    def forward_second(slot):
        def body(step, carry):
            second_two(z_peer(step), z_me, slot).start()
            return carry

        lax.fori_loop(1, z_count, body, 0)

    first_own.wait()
    forward_first(z_me)
    second_own.wait()
    forward_second(p_me)

    def relay(step, carry):
        @pl.when(step < z_count)
        def _():
            slot = z_peer(step)
            first_one(slot, slot).wait_recv()
            forward_first(slot)

        @pl.when(step < p_count)
        def _():
            slot = p_peer(step)
            second_one(slot, slot).wait_recv()
            forward_second(slot)

        return carry

    lax.fori_loop(1, rounds, relay, 0)

    def drain(step, carry):
        @pl.when(step < z_count)
        def _():
            peer = z_peer(step)
            first_one(peer, z_me).wait_send()
            second_rows(peer, z_me).wait_send()
            second_rows(peer, peer).wait_recv()

        @pl.when(step < p_count)
        def _():
            peer = p_peer(step)
            second_one(peer, p_me).wait_send()
            first_rows(peer, p_me).wait_send()
            first_rows(peer, peer).wait_recv()

        return carry

    lax.fori_loop(1, rounds, drain, 0)


def gather_ctx(piece, layout, kernel_id):
    z_count, p_count = layout
    rows, cols = piece.shape
    tile = 16
    head = min(rows - tile, max(tile, round(rows * 2 / (3 * tile)) * tile))
    tail = rows - head
    dma_pairs = [
        pltpu.SemaphoreType.DMA((z_count,)),
        pltpu.SemaphoreType.DMA((z_count,)),
        pltpu.SemaphoreType.DMA((p_count,)),
        pltpu.SemaphoreType.DMA((p_count,)),
    ]

    def kernel(first_ref, second_ref, first_out, second_out, *sems):
        _gather_kernel(
            z_count, p_count, first_ref, second_ref, first_out, second_out,
            (sems[0], sems[1]), (sems[2], sems[3]), (sems[4], sems[5]), (sems[6], sems[7]),
            sems[8],
        )

    first, second = pl.pallas_call(
        kernel,
        out_shape=(
            jax.ShapeDtypeStruct((p_count, z_count, head, cols), piece.dtype),
            jax.ShapeDtypeStruct((z_count, p_count, tail, cols), piece.dtype),
        ),
        in_specs=[pl.BlockSpec(memory_space=pl.ANY)] * 2,
        out_specs=(pl.BlockSpec(memory_space=pl.ANY),) * 2,
        scratch_shapes=dma_pairs + [dma_pairs[2], dma_pairs[3], dma_pairs[0], dma_pairs[1]]
        + [pltpu.SemaphoreType.DMA((2,))],
        compiler_params=pltpu.CompilerParams(collective_id=kernel_id, has_side_effects=True),
    )(piece[:head], piece[head:])
    joined = jnp.concatenate([first.transpose(1, 0, 2, 3), second], axis=2)
    return joined.reshape(z_count * p_count * rows, cols)


def _scatter_kernel(count, part_ref, out_ref, send_sems, recv_sems, local_sem):
    me = lax.axis_index("tp")
    width = out_ref.shape[2]
    mesh_ids = pl.DeviceIdType.MESH
    barrier = pltpu.get_barrier_semaphore()

    def greet(step, carry):
        peer = lax.rem(me + step, count)
        pl.semaphore_signal(barrier, 1, device_id={"tp": peer}, device_id_type=mesh_ids)
        return carry

    lax.fori_loop(1, count, greet, 0)
    pl.semaphore_wait(barrier, count - 1)

    def columns(index):
        return pl.ds(pl.multiple_of(index * width, width), width)

    own = pltpu.make_async_copy(part_ref.at[:, columns(me)], out_ref.at[me], local_sem)
    own.start()

    def remote(peer, slot):
        return pltpu.make_async_remote_copy(
            src_ref=part_ref.at[:, columns(peer)],
            dst_ref=out_ref.at[slot],
            send_sem=send_sems.at[peer],
            recv_sem=recv_sems.at[slot],
            device_id={"tp": peer},
            device_id_type=mesh_ids,
        )

    def send(step, carry):
        remote(lax.rem(me + step, count), me).start()
        return carry

    def finish(step, carry):
        peer = lax.rem(me + step, count)
        remote(peer, me).wait_send()
        remote(peer, peer).wait_recv()
        return carry

    lax.fori_loop(1, count, send, 0)
    lax.fori_loop(1, count, finish, 0)
    own.wait()


def scatter_sum_tp(part, count, kernel_id):
    rows, cols = part.shape
    pieces = pl.pallas_call(
        functools.partial(_scatter_kernel, count),
        out_shape=jax.ShapeDtypeStruct((count, rows, cols // count), part.dtype),
        in_specs=[pl.BlockSpec(memory_space=pl.ANY)],
        out_specs=pl.BlockSpec(memory_space=pl.ANY),
        scratch_shapes=[
            pltpu.SemaphoreType.DMA((count,)),
            pltpu.SemaphoreType.DMA((count,)),
            pltpu.SemaphoreType.DMA(()),
        ],
        compiler_params=pltpu.CompilerParams(collective_id=kernel_id, has_side_effects=True),
    )(part)
    return jnp.sum(pieces.astype(jnp.float32), axis=0)


def ctx_layout(mesh):
    count = mesh.shape["ctx"]
    column = mesh.devices.transpose(
        mesh.axis_names.index("ctx"), mesh.axis_names.index("tp")
    )[:, 0]
    try:
        planes = [device.coords[2] for device in column]
    except (AttributeError, IndexError, TypeError):
        return (count, 1)
    p_count = 1
    while p_count < count and planes[p_count] == planes[0]:
        p_count += 1
    if count % p_count:
        return (count, 1)
    for index in range(count):
        if planes[index] != planes[(index // p_count) * p_count]:
            return (count, 1)
    return (count // p_count, p_count)


def initial_positions(block_map, first_row, row_count, block_rows):
    row_ids = first_row + jnp.arange(row_count, dtype=jnp.int32)
    block_ids = row_ids // block_rows
    table_ids = jnp.arange(block_map.shape[0], dtype=jnp.int32)
    mapped = jnp.sum(
        jnp.where(block_ids[:, None] == table_ids[None, :], block_map[None, :], 0), axis=1
    )
    return mapped * block_rows + row_ids % block_rows


def request_index(positions, request_ends):
    return jnp.sum((positions[:, None] >= request_ends[None, :]).astype(jnp.int32), axis=1)


def round_weights(weights):
    rounded = weights.astype(jnp.bfloat16)
    rounded = lax.optimization_barrier(rounded)
    return rounded.astype(jnp.float32)


def softmax_parts(
    dec_heads, projected_key_rows, projected_value_rows, owned, kv_heads, head_dim, score_scale
):
    row_count = projected_key_rows.shape[0]
    scores = (
        jnp.einsum(
            "rgjd,tgd->rgjt",
            dec_heads,
            projected_key_rows.reshape(row_count, kv_heads, head_dim),
            preferred_element_type=jnp.float32,
        )
        * score_scale
    )
    scores = jnp.where(owned, scores, floor_value)
    part_peak = jnp.max(scores, axis=3)
    weights = jnp.where(owned, jnp.exp(scores - part_peak[..., None]), 0.0)
    part_total = jnp.sum(weights, axis=3)
    part_mixed = jnp.einsum(
        "rgjt,tgd->rgjd",
        weights.astype(jnp.bfloat16),
        projected_value_rows.reshape(row_count, kv_heads, head_dim),
        preferred_element_type=jnp.float32,
    )
    return (part_peak, part_total, part_mixed)


def on_device(
    layout, tp_count, tokens, new_token_states, w_query, key_matrix, value_matrix, w_out, lengths, block_map
):
    local_rows = tokens.shape[0]
    block_rows = local_rows // 2
    request_count = new_token_states.shape[0]
    head_dim = HEAD_SIZE
    query_width = w_query.shape[1]
    kv_width = key_matrix.shape[1]
    kv_heads = kv_width // head_dim
    query_group_count = query_width // kv_width
    score_scale = 1.0 / math.sqrt(head_dim)
    device = lax.axis_index("ctx")
    request_ends = jnp.cumsum(lengths)
    inputs = jnp.concatenate([tokens, new_token_states], axis=0)
    joined = gather_ctx(
        jnp.concatenate([w_query, key_matrix, value_matrix, w_out.T], axis=1), layout, 0
    )
    qkv_width = query_width + 2 * kv_width
    projected_all = jnp.dot(
        inputs, joined[:, :qkv_width], preferred_element_type=jnp.float32
    ).astype(jnp.bfloat16)
    out_weight = joined[:, qkv_width:].T
    query_all = projected_all[:, :query_width]
    key_all = projected_all[:, query_width : query_width + kv_width]
    value_all = projected_all[:, query_width + kv_width :]
    local_query = query_all[:local_rows]
    local_keys = key_all[:local_rows]
    local_values = value_all[:local_rows]
    dec_query = query_all[local_rows:]
    decode_key_rows = key_all[local_rows:]
    decode_value_rows = value_all[local_rows:]
    token_pos = initial_positions(block_map, device * local_rows, local_rows, block_rows)
    token_request = request_index(token_pos, request_ends)
    query_heads = local_query.reshape(local_rows, kv_heads, query_group_count, head_dim)

    def attend(running, shard_pieces, first_row):
        peak_run, total_run, mixed_run = running
        key_piece, value_piece = shard_pieces
        row_count = key_piece.shape[0]
        key_pos = lax.dynamic_slice_in_dim(cache_pos, first_row, row_count, 0)
        key_request = lax.dynamic_slice_in_dim(cache_request, first_row, row_count, 0)
        allowed = (key_request[None, :] == token_request[:, None]) & (
            key_pos[None, :] <= token_pos[:, None]
        )
        scores = (
            jnp.einsum(
                "tgjd,kgd->gjtk",
                query_heads,
                key_piece.reshape(row_count, kv_heads, head_dim),
                preferred_element_type=jnp.float32,
            )
            * score_scale
        )
        scores = jnp.where(allowed, scores, floor_value)
        peak_new = jnp.maximum(peak_run, jnp.max(scores, axis=3))
        weights = jnp.where(allowed, jnp.exp(scores - peak_new[..., None]), 0.0)
        rescale = jnp.exp(peak_run - peak_new)
        total_new = total_run * rescale + jnp.sum(weights, axis=3)
        mixed_new = mixed_run * rescale[..., None] + jnp.einsum(
            "gjtk,kgd->gjtd",
            weights.astype(jnp.bfloat16),
            value_piece.reshape(row_count, kv_heads, head_dim),
            preferred_element_type=jnp.float32,
        )
        return (peak_new, total_new, mixed_new)

    start_state = (
        jnp.full((kv_heads, query_group_count, local_rows), floor_value, jnp.float32),
        jnp.zeros((kv_heads, query_group_count, local_rows), jnp.float32),
        jnp.zeros((kv_heads, query_group_count, local_rows, head_dim), jnp.float32),
    )
    dec_heads = dec_query.reshape(request_count, kv_heads, query_group_count, head_dim)
    request_ids = jnp.arange(request_count, dtype=jnp.int32)
    cache_both = gather_ctx(
        jnp.concatenate([local_keys, local_values], axis=1), layout, 1
    )
    cache_keys = cache_both[:, :kv_width]
    cache_values = cache_both[:, kv_width:]
    total_rows = cache_keys.shape[0]
    step_rows = total_rows
    cache_pos = (
        block_map[:, None] * block_rows + jnp.arange(block_rows, dtype=jnp.int32)[None, :]
    ).reshape(total_rows)
    cache_request = request_index(cache_pos, request_ends)

    def key_step(running, step_index):
        first_row = step_index * step_rows
        pieces = (
            lax.dynamic_slice_in_dim(cache_keys, first_row, step_rows, 0),
            lax.dynamic_slice_in_dim(cache_values, first_row, step_rows, 0),
        )
        return (attend(running, pieces, first_row), None)

    final_state, unused = lax.scan(
        key_step, start_state, jnp.arange(total_rows // step_rows, dtype=jnp.int32)
    )
    peak_run, total_run, mixed_run = final_state
    owned = (cache_request[None, :] == request_ids[:, None])[:, None, None, :]
    cache_peak, cache_total, cache_mixed = softmax_parts(
        dec_heads, cache_keys, cache_values, owned, kv_heads, head_dim, score_scale
    )
    attended = (
        (mixed_run / total_run[..., None]).transpose(2, 0, 1, 3).reshape(local_rows, query_width)
    )
    attended = attended.astype(jnp.bfloat16)
    own_keys = decode_key_rows.reshape(request_count, kv_heads, 1, head_dim).astype(jnp.float32)
    own_values = decode_value_rows.reshape(request_count, kv_heads, 1, head_dim).astype(jnp.float32)
    self_scores = jnp.sum(dec_heads.astype(jnp.float32) * own_keys, axis=3) * score_scale
    peak_all = jnp.maximum(cache_peak, self_scores)
    rescale = jnp.exp(cache_peak - peak_all)
    self_weights = jnp.exp(self_scores - peak_all)
    dec_total = cache_total * rescale + self_weights
    dec_mixed = (
        cache_mixed * rescale[..., None] + round_weights(self_weights)[..., None] * own_values
    )
    dec_attn = (
        (dec_mixed / dec_total[..., None]).reshape(request_count, query_width).astype(jnp.bfloat16)
    )
    attended_all = jnp.concatenate([attended, dec_attn], axis=0)
    projected = jnp.dot(
        attended_all,
        out_weight,
        preferred_element_type=jnp.float32,
    )
    summed_rows = scatter_sum_tp(projected.astype(jnp.bfloat16), tp_count, 2)
    summed_rows = summed_rows.astype(jnp.bfloat16)
    return (summed_rows[:local_rows], summed_rows[local_rows:])


def solution(mesh):
    return jax.shard_map(
        functools.partial(on_device, ctx_layout(mesh), mesh.shape["tp"]),
        mesh=mesh,
        in_specs=(
            P("ctx", None),
            P(),
            P("ctx", "tp"),
            P("ctx", "tp"),
            P("ctx", "tp"),
            P("tp", "ctx"),
            P(),
            P(),
        ),
        out_specs=(P("ctx", "tp"), P(None, "tp")),
        check_vma=False,
    )
```

```python
import functools
import math

import jax
import jax.numpy as jnp
from jax import lax
from jax.experimental import pallas as pl
from jax.experimental.pallas import tpu as pltpu
from jax.sharding import PartitionSpec as P

HEAD_SIZE = 128


floor_value = -1e30


def _gather_kernel(
    z_count,
    p_count,
    first_ref,
    second_ref,
    first_out,
    second_out,
    first_z,
    first_p,
    second_p,
    second_z,
    local_sems,
):
    me = lax.axis_index("ctx")
    z_me = me // p_count
    p_me = lax.rem(me, p_count)
    mesh_ids = pl.DeviceIdType.MESH
    barrier = pltpu.get_barrier_semaphore()

    def z_peer(step):
        return lax.rem(z_me + step, z_count)

    def p_peer(step):
        return lax.rem(p_me + step, p_count)

    def z_target(peer):
        return peer * p_count + p_me

    def p_target(peer):
        return z_me * p_count + peer

    def greet(peer_of, target_of):
        def body(step, carry):
            pl.semaphore_signal(
                barrier, 1, device_id={"ctx": target_of(peer_of(step))}, device_id_type=mesh_ids
            )
            return carry

        return body

    lax.fori_loop(1, z_count, greet(z_peer, z_target), 0)
    lax.fori_loop(1, p_count, greet(p_peer, p_target), 0)
    pl.semaphore_wait(barrier, z_count + p_count - 2)

    def remote(src, dst, send_sem, recv_sem, target):
        return pltpu.make_async_remote_copy(
            src_ref=src,
            dst_ref=dst,
            send_sem=send_sem,
            recv_sem=recv_sem,
            device_id={"ctx": target},
            device_id_type=mesh_ids,
        )

    def first_one(peer, slot):
        return remote(
            first_ref, first_out.at[p_me, slot], first_z[0].at[peer], first_z[1].at[slot],
            z_target(peer),
        )

    def second_one(peer, slot):
        return remote(
            second_ref, second_out.at[z_me, slot], second_p[0].at[peer], second_p[1].at[slot],
            p_target(peer),
        )

    def first_two(peer, row, slot):
        return remote(
            first_out.at[row, slot], first_out.at[row, slot], first_p[0].at[peer],
            first_p[1].at[row], p_target(peer),
        )

    def second_two(peer, row, slot):
        return remote(
            second_out.at[row, slot], second_out.at[row, slot], second_z[0].at[peer],
            second_z[1].at[row], z_target(peer),
        )

    def first_rows(peer, row):
        return remote(
            first_out.at[row], first_out.at[row], first_p[0].at[peer], first_p[1].at[row],
            p_target(peer),
        )

    def second_rows(peer, row):
        return remote(
            second_out.at[row], second_out.at[row], second_z[0].at[peer], second_z[1].at[row],
            z_target(peer),
        )

    first_own = pltpu.make_async_copy(first_ref, first_out.at[p_me, z_me], local_sems.at[0])
    second_own = pltpu.make_async_copy(second_ref, second_out.at[z_me, p_me], local_sems.at[1])
    first_own.start()
    second_own.start()

    def start_one(step, carry):
        @pl.when(step < z_count)
        def _():
            first_one(z_peer(step), z_me).start()

        @pl.when(step < p_count)
        def _():
            second_one(p_peer(step), p_me).start()

        return carry

    rounds = max(z_count, p_count)
    lax.fori_loop(1, rounds, start_one, 0)

    def forward_first(slot):
        def body(step, carry):
            first_two(p_peer(step), p_me, slot).start()
            return carry

        lax.fori_loop(1, p_count, body, 0)

    def forward_second(slot):
        def body(step, carry):
            second_two(z_peer(step), z_me, slot).start()
            return carry

        lax.fori_loop(1, z_count, body, 0)

    first_own.wait()
    forward_first(z_me)
    second_own.wait()
    forward_second(p_me)

    def relay(step, carry):
        @pl.when(step < z_count)
        def _():
            slot = z_peer(step)
            first_one(slot, slot).wait_recv()
            forward_first(slot)

        @pl.when(step < p_count)
        def _():
            slot = p_peer(step)
            second_one(slot, slot).wait_recv()
            forward_second(slot)

        return carry

    lax.fori_loop(1, rounds, relay, 0)

    def drain(step, carry):
        @pl.when(step < z_count)
        def _():
            peer = z_peer(step)
            first_one(peer, z_me).wait_send()
            second_rows(peer, z_me).wait_send()
            second_rows(peer, peer).wait_recv()

        @pl.when(step < p_count)
        def _():
            peer = p_peer(step)
            second_one(peer, p_me).wait_send()
            first_rows(peer, p_me).wait_send()
            first_rows(peer, peer).wait_recv()

        return carry

    lax.fori_loop(1, rounds, drain, 0)


def gather_ctx(piece, layout, kernel_id):
    z_count, p_count = layout
    rows, cols = piece.shape
    lane = 128
    by_columns = cols % (3 * lane) == 0
    if by_columns:
        head = 2 * cols // 3
        shapes = ((rows, head), (rows, cols - head))
        pieces = (piece[:, :head], piece[:, head:])
    else:
        tile = 16
        head = min(rows - tile, max(tile, round(rows * 2 / (3 * tile)) * tile))
        shapes = ((head, cols), (rows - head, cols))
        pieces = (piece[:head], piece[head:])
    dma_pairs = [
        pltpu.SemaphoreType.DMA((z_count,)),
        pltpu.SemaphoreType.DMA((z_count,)),
        pltpu.SemaphoreType.DMA((p_count,)),
        pltpu.SemaphoreType.DMA((p_count,)),
    ]

    def kernel(first_ref, second_ref, first_out, second_out, *sems):
        _gather_kernel(
            z_count, p_count, first_ref, second_ref, first_out, second_out,
            (sems[0], sems[1]), (sems[2], sems[3]), (sems[4], sems[5]), (sems[6], sems[7]),
            sems[8],
        )

    first, second = pl.pallas_call(
        kernel,
        out_shape=(
            jax.ShapeDtypeStruct((p_count, z_count) + shapes[0], piece.dtype),
            jax.ShapeDtypeStruct((z_count, p_count) + shapes[1], piece.dtype),
        ),
        in_specs=[pl.BlockSpec(memory_space=pl.ANY)] * 2,
        out_specs=(pl.BlockSpec(memory_space=pl.ANY),) * 2,
        scratch_shapes=dma_pairs + [dma_pairs[2], dma_pairs[3], dma_pairs[0], dma_pairs[1]]
        + [pltpu.SemaphoreType.DMA((2,))],
        compiler_params=pltpu.CompilerParams(collective_id=kernel_id, has_side_effects=True),
    )(*pieces)
    joined = jnp.concatenate([first.transpose(1, 0, 2, 3), second], axis=3 if by_columns else 2)
    return joined.reshape(z_count * p_count * rows, cols)


def _scatter_kernel(count, part_ref, out_ref, send_sems, recv_sems, local_sem):
    me = lax.axis_index("tp")
    width = out_ref.shape[2]
    mesh_ids = pl.DeviceIdType.MESH
    barrier = pltpu.get_barrier_semaphore()

    def greet(step, carry):
        peer = lax.rem(me + step, count)
        pl.semaphore_signal(barrier, 1, device_id={"tp": peer}, device_id_type=mesh_ids)
        return carry

    lax.fori_loop(1, count, greet, 0)
    pl.semaphore_wait(barrier, count - 1)

    def columns(index):
        return pl.ds(pl.multiple_of(index * width, width), width)

    own = pltpu.make_async_copy(part_ref.at[:, columns(me)], out_ref.at[me], local_sem)
    own.start()

    def remote(peer, slot):
        return pltpu.make_async_remote_copy(
            src_ref=part_ref.at[:, columns(peer)],
            dst_ref=out_ref.at[slot],
            send_sem=send_sems.at[peer],
            recv_sem=recv_sems.at[slot],
            device_id={"tp": peer},
            device_id_type=mesh_ids,
        )

    def send(step, carry):
        remote(lax.rem(me + step, count), me).start()
        return carry

    def finish(step, carry):
        peer = lax.rem(me + step, count)
        remote(peer, me).wait_send()
        remote(peer, peer).wait_recv()
        return carry

    lax.fori_loop(1, count, send, 0)
    lax.fori_loop(1, count, finish, 0)
    own.wait()


def scatter_sum_tp(part, count, kernel_id):
    rows, cols = part.shape
    pieces = pl.pallas_call(
        functools.partial(_scatter_kernel, count),
        out_shape=jax.ShapeDtypeStruct((count, rows, cols // count), part.dtype),
        in_specs=[pl.BlockSpec(memory_space=pl.ANY)],
        out_specs=pl.BlockSpec(memory_space=pl.ANY),
        scratch_shapes=[
            pltpu.SemaphoreType.DMA((count,)),
            pltpu.SemaphoreType.DMA((count,)),
            pltpu.SemaphoreType.DMA(()),
        ],
        compiler_params=pltpu.CompilerParams(collective_id=kernel_id, has_side_effects=True),
    )(part)
    return jnp.sum(pieces.astype(jnp.float32), axis=0)


def ctx_layout(mesh):
    count = mesh.shape["ctx"]
    column = mesh.devices.transpose(
        mesh.axis_names.index("ctx"), mesh.axis_names.index("tp")
    )[:, 0]
    try:
        planes = [device.coords[2] for device in column]
    except (AttributeError, IndexError, TypeError):
        return (count, 1)
    p_count = 1
    while p_count < count and planes[p_count] == planes[0]:
        p_count += 1
    if count % p_count:
        return (count, 1)
    for index in range(count):
        if planes[index] != planes[(index // p_count) * p_count]:
            return (count, 1)
    return (count // p_count, p_count)


def initial_positions(block_map, first_row, row_count, block_rows):
    row_ids = first_row + jnp.arange(row_count, dtype=jnp.int32)
    block_ids = row_ids // block_rows
    table_ids = jnp.arange(block_map.shape[0], dtype=jnp.int32)
    mapped = jnp.sum(
        jnp.where(block_ids[:, None] == table_ids[None, :], block_map[None, :], 0), axis=1
    )
    return mapped * block_rows + row_ids % block_rows


def request_index(positions, request_ends):
    return jnp.sum((positions[:, None] >= request_ends[None, :]).astype(jnp.int32), axis=1)


def round_weights(weights):
    rounded = weights.astype(jnp.bfloat16)
    rounded = lax.optimization_barrier(rounded)
    return rounded.astype(jnp.float32)


def softmax_parts(
    dec_heads, projected_key_rows, projected_value_rows, owned, kv_heads, head_dim, score_scale
):
    row_count = projected_key_rows.shape[0]
    scores = (
        jnp.einsum(
            "rgjd,tgd->rgjt",
            dec_heads,
            projected_key_rows.reshape(row_count, kv_heads, head_dim),
            preferred_element_type=jnp.float32,
        )
        * score_scale
    )
    scores = jnp.where(owned, scores, floor_value)
    part_peak = jnp.max(scores, axis=3)
    weights = jnp.where(owned, jnp.exp(scores - part_peak[..., None]), 0.0)
    part_total = jnp.sum(weights, axis=3)
    part_mixed = jnp.einsum(
        "rgjt,tgd->rgjd",
        weights.astype(jnp.bfloat16),
        projected_value_rows.reshape(row_count, kv_heads, head_dim),
        preferred_element_type=jnp.float32,
    )
    return (part_peak, part_total, part_mixed)


def on_device(
    layout, tp_count, tokens, new_token_states, w_query, key_matrix, value_matrix, w_out, lengths, block_map
):
    local_rows = tokens.shape[0]
    block_rows = local_rows // 2
    request_count = new_token_states.shape[0]
    head_dim = HEAD_SIZE
    query_width = w_query.shape[1]
    kv_width = key_matrix.shape[1]
    kv_heads = kv_width // head_dim
    query_group_count = query_width // kv_width
    score_scale = 1.0 / math.sqrt(head_dim)
    device = lax.axis_index("ctx")
    request_ends = jnp.cumsum(lengths)
    inputs = jnp.concatenate([tokens, new_token_states], axis=0)
    joined = gather_ctx(
        jnp.concatenate([w_query, key_matrix, value_matrix, w_out.T], axis=1), layout, 0
    )
    qkv_width = query_width + 2 * kv_width
    projected_all = jnp.dot(
        inputs, joined[:, :qkv_width], preferred_element_type=jnp.float32
    ).astype(jnp.bfloat16)
    out_weight = joined[:, qkv_width:].T
    query_all = projected_all[:, :query_width]
    key_all = projected_all[:, query_width : query_width + kv_width]
    value_all = projected_all[:, query_width + kv_width :]
    local_query = query_all[:local_rows]
    local_keys = key_all[:local_rows]
    local_values = value_all[:local_rows]
    dec_query = query_all[local_rows:]
    decode_key_rows = key_all[local_rows:]
    decode_value_rows = value_all[local_rows:]
    token_pos = initial_positions(block_map, device * local_rows, local_rows, block_rows)
    token_request = request_index(token_pos, request_ends)
    query_heads = local_query.reshape(local_rows, kv_heads, query_group_count, head_dim)

    def attend(running, shard_pieces, first_row):
        peak_run, total_run, mixed_run = running
        key_piece, value_piece = shard_pieces
        row_count = key_piece.shape[0]
        key_pos = lax.dynamic_slice_in_dim(cache_pos, first_row, row_count, 0)
        key_request = lax.dynamic_slice_in_dim(cache_request, first_row, row_count, 0)
        allowed = (key_request[None, :] == token_request[:, None]) & (
            key_pos[None, :] <= token_pos[:, None]
        )
        scores = (
            jnp.einsum(
                "tgjd,kgd->gjtk",
                query_heads,
                key_piece.reshape(row_count, kv_heads, head_dim),
                preferred_element_type=jnp.float32,
            )
            * score_scale
        )
        scores = jnp.where(allowed, scores, floor_value)
        peak_new = jnp.maximum(peak_run, jnp.max(scores, axis=3))
        weights = jnp.where(allowed, jnp.exp(scores - peak_new[..., None]), 0.0)
        rescale = jnp.exp(peak_run - peak_new)
        total_new = total_run * rescale + jnp.sum(weights, axis=3)
        mixed_new = mixed_run * rescale[..., None] + jnp.einsum(
            "gjtk,kgd->gjtd",
            weights.astype(jnp.bfloat16),
            value_piece.reshape(row_count, kv_heads, head_dim),
            preferred_element_type=jnp.float32,
        )
        return (peak_new, total_new, mixed_new)

    start_state = (
        jnp.full((kv_heads, query_group_count, local_rows), floor_value, jnp.float32),
        jnp.zeros((kv_heads, query_group_count, local_rows), jnp.float32),
        jnp.zeros((kv_heads, query_group_count, local_rows, head_dim), jnp.float32),
    )
    dec_heads = dec_query.reshape(request_count, kv_heads, query_group_count, head_dim)
    request_ids = jnp.arange(request_count, dtype=jnp.int32)
    cache_both = gather_ctx(
        jnp.concatenate([local_keys, local_values], axis=1), layout, 1
    )
    cache_keys = cache_both[:, :kv_width]
    cache_values = cache_both[:, kv_width:]
    total_rows = cache_keys.shape[0]
    step_rows = total_rows
    cache_pos = (
        block_map[:, None] * block_rows + jnp.arange(block_rows, dtype=jnp.int32)[None, :]
    ).reshape(total_rows)
    cache_request = request_index(cache_pos, request_ends)

    def key_step(running, step_index):
        first_row = step_index * step_rows
        pieces = (
            lax.dynamic_slice_in_dim(cache_keys, first_row, step_rows, 0),
            lax.dynamic_slice_in_dim(cache_values, first_row, step_rows, 0),
        )
        return (attend(running, pieces, first_row), None)

    final_state, unused = lax.scan(
        key_step, start_state, jnp.arange(total_rows // step_rows, dtype=jnp.int32)
    )
    peak_run, total_run, mixed_run = final_state
    owned = (cache_request[None, :] == request_ids[:, None])[:, None, None, :]
    cache_peak, cache_total, cache_mixed = softmax_parts(
        dec_heads, cache_keys, cache_values, owned, kv_heads, head_dim, score_scale
    )
    attended = (
        (mixed_run / total_run[..., None]).transpose(2, 0, 1, 3).reshape(local_rows, query_width)
    )
    attended = attended.astype(jnp.bfloat16)
    own_keys = decode_key_rows.reshape(request_count, kv_heads, 1, head_dim).astype(jnp.float32)
    own_values = decode_value_rows.reshape(request_count, kv_heads, 1, head_dim).astype(jnp.float32)
    self_scores = jnp.sum(dec_heads.astype(jnp.float32) * own_keys, axis=3) * score_scale
    peak_all = jnp.maximum(cache_peak, self_scores)
    rescale = jnp.exp(cache_peak - peak_all)
    self_weights = jnp.exp(self_scores - peak_all)
    dec_total = cache_total * rescale + self_weights
    dec_mixed = (
        cache_mixed * rescale[..., None] + round_weights(self_weights)[..., None] * own_values
    )
    dec_attn = (
        (dec_mixed / dec_total[..., None]).reshape(request_count, query_width).astype(jnp.bfloat16)
    )
    attended_all = jnp.concatenate([attended, dec_attn], axis=0)
    projected = jnp.dot(
        attended_all,
        out_weight,
        preferred_element_type=jnp.float32,
    )
    summed_rows = scatter_sum_tp(projected.astype(jnp.bfloat16), tp_count, 2)
    summed_rows = summed_rows.astype(jnp.bfloat16)
    return (summed_rows[:local_rows], summed_rows[local_rows:])


def solution(mesh):
    return jax.shard_map(
        functools.partial(on_device, ctx_layout(mesh), mesh.shape["tp"]),
        mesh=mesh,
        in_specs=(
            P("ctx", None),
            P(),
            P("ctx", "tp"),
            P("ctx", "tp"),
            P("ctx", "tp"),
            P("tp", "ctx"),
            P(),
            P(),
        ),
        out_specs=(P("ctx", "tp"), P(None, "tp")),
        check_vma=False,
    )
```

```python
import functools
import math

import jax
import jax.numpy as jnp
from jax import lax
from jax.experimental import pallas as pl
from jax.experimental.pallas import tpu as pltpu
from jax.sharding import PartitionSpec as P

HEAD_SIZE = 128


floor_value = -1e30


def _gather_kernel(
    z_count,
    p_count,
    first_ref,
    second_ref,
    first_out,
    second_out,
    first_z,
    first_p,
    second_p,
    second_z,
    local_sems,
):
    me = lax.axis_index("ctx")
    z_me = me // p_count
    p_me = lax.rem(me, p_count)
    mesh_ids = pl.DeviceIdType.MESH
    barrier = pltpu.get_barrier_semaphore()

    def z_peer(step):
        return lax.rem(z_me + step, z_count)

    def p_peer(step):
        return lax.rem(p_me + step, p_count)

    def z_target(peer):
        return peer * p_count + p_me

    def p_target(peer):
        return z_me * p_count + peer

    def greet(peer_of, target_of):
        def body(step, carry):
            pl.semaphore_signal(
                barrier, 1, device_id={"ctx": target_of(peer_of(step))}, device_id_type=mesh_ids
            )
            return carry

        return body

    lax.fori_loop(1, z_count, greet(z_peer, z_target), 0)
    lax.fori_loop(1, p_count, greet(p_peer, p_target), 0)
    pl.semaphore_wait(barrier, z_count + p_count - 2)

    def remote(src, dst, send_sem, recv_sem, target):
        return pltpu.make_async_remote_copy(
            src_ref=src,
            dst_ref=dst,
            send_sem=send_sem,
            recv_sem=recv_sem,
            device_id={"ctx": target},
            device_id_type=mesh_ids,
        )

    def first_one(peer, slot):
        return remote(
            first_ref, first_out.at[p_me, slot], first_z[0].at[peer], first_z[1].at[slot],
            z_target(peer),
        )

    def second_one(peer, slot):
        return remote(
            second_ref, second_out.at[z_me, slot], second_p[0].at[peer], second_p[1].at[slot],
            p_target(peer),
        )

    def first_two(peer, row, slot):
        return remote(
            first_out.at[row, slot], first_out.at[row, slot], first_p[0].at[peer],
            first_p[1].at[row], p_target(peer),
        )

    def second_two(peer, row, slot):
        return remote(
            second_out.at[row, slot], second_out.at[row, slot], second_z[0].at[peer],
            second_z[1].at[row], z_target(peer),
        )

    def first_rows(peer, row):
        return remote(
            first_out.at[row], first_out.at[row], first_p[0].at[peer], first_p[1].at[row],
            p_target(peer),
        )

    def second_rows(peer, row):
        return remote(
            second_out.at[row], second_out.at[row], second_z[0].at[peer], second_z[1].at[row],
            z_target(peer),
        )

    first_own = pltpu.make_async_copy(first_ref, first_out.at[p_me, z_me], local_sems.at[0])
    second_own = pltpu.make_async_copy(second_ref, second_out.at[z_me, p_me], local_sems.at[1])
    first_own.start()
    second_own.start()

    def start_one(step, carry):
        @pl.when(step < z_count)
        def _():
            first_one(z_peer(step), z_me).start()

        @pl.when(step < p_count)
        def _():
            second_one(p_peer(step), p_me).start()

        return carry

    rounds = max(z_count, p_count)
    lax.fori_loop(1, rounds, start_one, 0)

    def forward_first(slot):
        def body(step, carry):
            first_two(p_peer(step), p_me, slot).start()
            return carry

        lax.fori_loop(1, p_count, body, 0)

    def forward_second(slot):
        def body(step, carry):
            second_two(z_peer(step), z_me, slot).start()
            return carry

        lax.fori_loop(1, z_count, body, 0)

    first_own.wait()
    forward_first(z_me)
    second_own.wait()
    forward_second(p_me)

    def relay(step, carry):
        @pl.when(step < z_count)
        def _():
            slot = z_peer(step)
            first_one(slot, slot).wait_recv()
            forward_first(slot)

        @pl.when(step < p_count)
        def _():
            slot = p_peer(step)
            second_one(slot, slot).wait_recv()
            forward_second(slot)

        return carry

    lax.fori_loop(1, rounds, relay, 0)

    def drain(step, carry):
        @pl.when(step < z_count)
        def _():
            peer = z_peer(step)
            first_one(peer, z_me).wait_send()
            second_rows(peer, z_me).wait_send()
            second_rows(peer, peer).wait_recv()

        @pl.when(step < p_count)
        def _():
            peer = p_peer(step)
            second_one(peer, p_me).wait_send()
            first_rows(peer, p_me).wait_send()
            first_rows(peer, peer).wait_recv()

        return carry

    lax.fori_loop(1, rounds, drain, 0)


def gather_ctx(piece, layout, kernel_id):
    z_count, p_count = layout
    rows, cols = piece.shape
    lane = 128
    by_columns = cols % (3 * lane) == 0
    if by_columns:
        head = 2 * cols // 3
        shapes = ((rows, head), (rows, cols - head))
        pieces = (piece[:, :head], piece[:, head:])
    else:
        tile = 16
        head = min(rows - tile, max(tile, round(rows * 2 / (3 * tile)) * tile))
        shapes = ((head, cols), (rows - head, cols))
        pieces = (piece[:head], piece[head:])
    dma_pairs = [
        pltpu.SemaphoreType.DMA((z_count,)),
        pltpu.SemaphoreType.DMA((z_count,)),
        pltpu.SemaphoreType.DMA((p_count,)),
        pltpu.SemaphoreType.DMA((p_count,)),
    ]

    def kernel(first_ref, second_ref, first_out, second_out, *sems):
        _gather_kernel(
            z_count, p_count, first_ref, second_ref, first_out, second_out,
            (sems[0], sems[1]), (sems[2], sems[3]), (sems[4], sems[5]), (sems[6], sems[7]),
            sems[8],
        )

    first, second = pl.pallas_call(
        kernel,
        out_shape=(
            jax.ShapeDtypeStruct((p_count, z_count) + shapes[0], piece.dtype),
            jax.ShapeDtypeStruct((z_count, p_count) + shapes[1], piece.dtype),
        ),
        in_specs=[pl.BlockSpec(memory_space=pl.ANY)] * 2,
        out_specs=(pl.BlockSpec(memory_space=pl.ANY),) * 2,
        scratch_shapes=dma_pairs + [dma_pairs[2], dma_pairs[3], dma_pairs[0], dma_pairs[1]]
        + [pltpu.SemaphoreType.DMA((2,))],
        compiler_params=pltpu.CompilerParams(collective_id=kernel_id, has_side_effects=True),
    )(*pieces)
    joined = jnp.concatenate([first.transpose(1, 0, 2, 3), second], axis=3 if by_columns else 2)
    return joined.reshape(z_count * p_count * rows, cols)


def _scatter_kernel(count, part_ref, out_ref, send_sems, recv_sems, local_sem):
    me = lax.axis_index("tp")
    width = out_ref.shape[2]
    mesh_ids = pl.DeviceIdType.MESH
    barrier = pltpu.get_barrier_semaphore()

    def greet(step, carry):
        peer = lax.rem(me + step, count)
        pl.semaphore_signal(barrier, 1, device_id={"tp": peer}, device_id_type=mesh_ids)
        return carry

    lax.fori_loop(1, count, greet, 0)
    pl.semaphore_wait(barrier, count - 1)

    def columns(index):
        return pl.ds(pl.multiple_of(index * width, width), width)

    own = pltpu.make_async_copy(part_ref.at[:, columns(me)], out_ref.at[me], local_sem)
    own.start()

    def remote(peer, slot):
        return pltpu.make_async_remote_copy(
            src_ref=part_ref.at[:, columns(peer)],
            dst_ref=out_ref.at[slot],
            send_sem=send_sems.at[peer],
            recv_sem=recv_sems.at[slot],
            device_id={"tp": peer},
            device_id_type=mesh_ids,
        )

    def send(step, carry):
        remote(lax.rem(me + step, count), me).start()
        return carry

    def finish(step, carry):
        peer = lax.rem(me + step, count)
        remote(peer, me).wait_send()
        remote(peer, peer).wait_recv()
        return carry

    lax.fori_loop(1, count, send, 0)
    lax.fori_loop(1, count, finish, 0)
    own.wait()


def scatter_sum_tp(part, count, kernel_id):
    rows, cols = part.shape
    pieces = pl.pallas_call(
        functools.partial(_scatter_kernel, count),
        out_shape=jax.ShapeDtypeStruct((count, rows, cols // count), part.dtype),
        in_specs=[pl.BlockSpec(memory_space=pl.ANY)],
        out_specs=pl.BlockSpec(memory_space=pl.ANY),
        scratch_shapes=[
            pltpu.SemaphoreType.DMA((count,)),
            pltpu.SemaphoreType.DMA((count,)),
            pltpu.SemaphoreType.DMA(()),
        ],
        compiler_params=pltpu.CompilerParams(collective_id=kernel_id, has_side_effects=True),
    )(part)
    return jnp.sum(pieces.astype(jnp.float32), axis=0)


def _exchange_kernel(count, stride, part_ref, out_ref, send_sems, recv_sems, local_sem):
    me = lax.axis_index("tp")
    pos = lax.rem(me // stride, count)
    base = me - pos * stride
    mesh_ids = pl.DeviceIdType.MESH
    barrier = pltpu.get_barrier_semaphore()

    def peer_of(step):
        return lax.rem(pos + step, count)

    def greet(step, carry):
        target = base + peer_of(step) * stride
        pl.semaphore_signal(barrier, 1, device_id={"tp": target}, device_id_type=mesh_ids)
        return carry

    lax.fori_loop(1, count, greet, 0)
    pl.semaphore_wait(barrier, count - 1)
    own = pltpu.make_async_copy(part_ref.at[pos], out_ref.at[pos], local_sem)
    own.start()

    def remote(peer, slot):
        return pltpu.make_async_remote_copy(
            src_ref=part_ref.at[peer],
            dst_ref=out_ref.at[slot],
            send_sem=send_sems.at[peer],
            recv_sem=recv_sems.at[slot],
            device_id={"tp": base + peer * stride},
            device_id_type=mesh_ids,
        )

    def send(step, carry):
        remote(peer_of(step), pos).start()
        return carry

    def finish(step, carry):
        peer = peer_of(step)
        remote(peer, pos).wait_send()
        remote(peer, peer).wait_recv()
        return carry

    lax.fori_loop(1, count, send, 0)
    lax.fori_loop(1, count, finish, 0)
    own.wait()


def exchange_tp(part, count, stride, kernel_id):
    return pl.pallas_call(
        functools.partial(_exchange_kernel, count, stride),
        out_shape=jax.ShapeDtypeStruct(part.shape, part.dtype),
        in_specs=[pl.BlockSpec(memory_space=pl.ANY)],
        out_specs=pl.BlockSpec(memory_space=pl.ANY),
        scratch_shapes=[
            pltpu.SemaphoreType.DMA((count,)),
            pltpu.SemaphoreType.DMA((count,)),
            pltpu.SemaphoreType.DMA(()),
        ],
        compiler_params=pltpu.CompilerParams(collective_id=kernel_id, has_side_effects=True),
    )(part)


def scatter_sum_pairs(part, count):
    rows, cols = part.shape
    width = cols // count
    outer = count // 2
    pieces = part.reshape(rows, outer, 2, width).transpose(2, 1, 0, 3)
    pieces = pieces.reshape(2, outer * rows, width)
    paired = exchange_tp(pieces, 2, 1, 2)
    paired = jnp.sum(paired.astype(jnp.float32), axis=0).astype(part.dtype)
    spread = exchange_tp(paired.reshape(outer, rows, width), outer, 2, 3)
    return jnp.sum(spread.astype(jnp.float32), axis=0)


def tp_paired(mesh):
    count = mesh.shape["tp"]
    row = mesh.devices.transpose(
        mesh.axis_names.index("ctx"), mesh.axis_names.index("tp")
    )[0, :]
    if count % 2 or count < 4:
        return False
    try:
        chips = [tuple(device.coords) for device in row]
    except (AttributeError, TypeError):
        return False
    return all(chips[index] == chips[index + 1] for index in range(0, count, 2))


def ctx_layout(mesh):
    count = mesh.shape["ctx"]
    column = mesh.devices.transpose(
        mesh.axis_names.index("ctx"), mesh.axis_names.index("tp")
    )[:, 0]
    try:
        planes = [device.coords[2] for device in column]
    except (AttributeError, IndexError, TypeError):
        return (count, 1)
    p_count = 1
    while p_count < count and planes[p_count] == planes[0]:
        p_count += 1
    if count % p_count:
        return (count, 1)
    for index in range(count):
        if planes[index] != planes[(index // p_count) * p_count]:
            return (count, 1)
    return (count // p_count, p_count)


def initial_positions(block_map, first_row, row_count, block_rows):
    row_ids = first_row + jnp.arange(row_count, dtype=jnp.int32)
    block_ids = row_ids // block_rows
    table_ids = jnp.arange(block_map.shape[0], dtype=jnp.int32)
    mapped = jnp.sum(
        jnp.where(block_ids[:, None] == table_ids[None, :], block_map[None, :], 0), axis=1
    )
    return mapped * block_rows + row_ids % block_rows


def request_index(positions, request_ends):
    return jnp.sum((positions[:, None] >= request_ends[None, :]).astype(jnp.int32), axis=1)


def round_weights(weights):
    rounded = weights.astype(jnp.bfloat16)
    rounded = lax.optimization_barrier(rounded)
    return rounded.astype(jnp.float32)


def softmax_parts(
    dec_heads, projected_key_rows, projected_value_rows, owned, kv_heads, head_dim, score_scale
):
    row_count = projected_key_rows.shape[0]
    scores = (
        jnp.einsum(
            "rgjd,tgd->rgjt",
            dec_heads,
            projected_key_rows.reshape(row_count, kv_heads, head_dim),
            preferred_element_type=jnp.float32,
        )
        * score_scale
    )
    scores = jnp.where(owned, scores, floor_value)
    part_peak = jnp.max(scores, axis=3)
    weights = jnp.where(owned, jnp.exp(scores - part_peak[..., None]), 0.0)
    part_total = jnp.sum(weights, axis=3)
    part_mixed = jnp.einsum(
        "rgjt,tgd->rgjd",
        weights.astype(jnp.bfloat16),
        projected_value_rows.reshape(row_count, kv_heads, head_dim),
        preferred_element_type=jnp.float32,
    )
    return (part_peak, part_total, part_mixed)


def on_device(
    layout, tp_count, paired, tokens, new_token_states, w_query, key_matrix, value_matrix, w_out, lengths, block_map
):
    local_rows = tokens.shape[0]
    block_rows = local_rows // 2
    request_count = new_token_states.shape[0]
    head_dim = HEAD_SIZE
    query_width = w_query.shape[1]
    kv_width = key_matrix.shape[1]
    kv_heads = kv_width // head_dim
    query_group_count = query_width // kv_width
    score_scale = 1.0 / math.sqrt(head_dim)
    device = lax.axis_index("ctx")
    request_ends = jnp.cumsum(lengths)
    inputs = jnp.concatenate([tokens, new_token_states], axis=0)
    joined = gather_ctx(
        jnp.concatenate([w_query, key_matrix, value_matrix, w_out.T], axis=1), layout, 0
    )
    qkv_width = query_width + 2 * kv_width
    projected_all = jnp.dot(
        inputs, joined[:, :qkv_width], preferred_element_type=jnp.float32
    ).astype(jnp.bfloat16)
    out_weight = joined[:, qkv_width:].T
    query_all = projected_all[:, :query_width]
    key_all = projected_all[:, query_width : query_width + kv_width]
    value_all = projected_all[:, query_width + kv_width :]
    local_query = query_all[:local_rows]
    local_keys = key_all[:local_rows]
    local_values = value_all[:local_rows]
    dec_query = query_all[local_rows:]
    decode_key_rows = key_all[local_rows:]
    decode_value_rows = value_all[local_rows:]
    token_pos = initial_positions(block_map, device * local_rows, local_rows, block_rows)
    token_request = request_index(token_pos, request_ends)
    query_heads = local_query.reshape(local_rows, kv_heads, query_group_count, head_dim)

    def attend(running, shard_pieces, first_row):
        peak_run, total_run, mixed_run = running
        key_piece, value_piece = shard_pieces
        row_count = key_piece.shape[0]
        key_pos = lax.dynamic_slice_in_dim(cache_pos, first_row, row_count, 0)
        key_request = lax.dynamic_slice_in_dim(cache_request, first_row, row_count, 0)
        allowed = (key_request[None, :] == token_request[:, None]) & (
            key_pos[None, :] <= token_pos[:, None]
        )
        scores = (
            jnp.einsum(
                "tgjd,kgd->gjtk",
                query_heads,
                key_piece.reshape(row_count, kv_heads, head_dim),
                preferred_element_type=jnp.float32,
            )
            * score_scale
        )
        scores = jnp.where(allowed, scores, floor_value)
        peak_new = jnp.maximum(peak_run, jnp.max(scores, axis=3))
        weights = jnp.where(allowed, jnp.exp(scores - peak_new[..., None]), 0.0)
        rescale = jnp.exp(peak_run - peak_new)
        total_new = total_run * rescale + jnp.sum(weights, axis=3)
        mixed_new = mixed_run * rescale[..., None] + jnp.einsum(
            "gjtk,kgd->gjtd",
            weights.astype(jnp.bfloat16),
            value_piece.reshape(row_count, kv_heads, head_dim),
            preferred_element_type=jnp.float32,
        )
        return (peak_new, total_new, mixed_new)

    start_state = (
        jnp.full((kv_heads, query_group_count, local_rows), floor_value, jnp.float32),
        jnp.zeros((kv_heads, query_group_count, local_rows), jnp.float32),
        jnp.zeros((kv_heads, query_group_count, local_rows, head_dim), jnp.float32),
    )
    dec_heads = dec_query.reshape(request_count, kv_heads, query_group_count, head_dim)
    request_ids = jnp.arange(request_count, dtype=jnp.int32)
    cache_both = gather_ctx(
        jnp.concatenate([local_keys, local_values], axis=1), layout, 1
    )
    cache_keys = cache_both[:, :kv_width]
    cache_values = cache_both[:, kv_width:]
    total_rows = cache_keys.shape[0]
    step_rows = total_rows
    cache_pos = (
        block_map[:, None] * block_rows + jnp.arange(block_rows, dtype=jnp.int32)[None, :]
    ).reshape(total_rows)
    cache_request = request_index(cache_pos, request_ends)

    def key_step(running, step_index):
        first_row = step_index * step_rows
        pieces = (
            lax.dynamic_slice_in_dim(cache_keys, first_row, step_rows, 0),
            lax.dynamic_slice_in_dim(cache_values, first_row, step_rows, 0),
        )
        return (attend(running, pieces, first_row), None)

    final_state, unused = lax.scan(
        key_step, start_state, jnp.arange(total_rows // step_rows, dtype=jnp.int32)
    )
    peak_run, total_run, mixed_run = final_state
    owned = (cache_request[None, :] == request_ids[:, None])[:, None, None, :]
    cache_peak, cache_total, cache_mixed = softmax_parts(
        dec_heads, cache_keys, cache_values, owned, kv_heads, head_dim, score_scale
    )
    attended = (
        (mixed_run / total_run[..., None]).transpose(2, 0, 1, 3).reshape(local_rows, query_width)
    )
    attended = attended.astype(jnp.bfloat16)
    own_keys = decode_key_rows.reshape(request_count, kv_heads, 1, head_dim).astype(jnp.float32)
    own_values = decode_value_rows.reshape(request_count, kv_heads, 1, head_dim).astype(jnp.float32)
    self_scores = jnp.sum(dec_heads.astype(jnp.float32) * own_keys, axis=3) * score_scale
    peak_all = jnp.maximum(cache_peak, self_scores)
    rescale = jnp.exp(cache_peak - peak_all)
    self_weights = jnp.exp(self_scores - peak_all)
    dec_total = cache_total * rescale + self_weights
    dec_mixed = (
        cache_mixed * rescale[..., None] + round_weights(self_weights)[..., None] * own_values
    )
    dec_attn = (
        (dec_mixed / dec_total[..., None]).reshape(request_count, query_width).astype(jnp.bfloat16)
    )
    attended_all = jnp.concatenate([attended, dec_attn], axis=0)
    projected = jnp.dot(
        attended_all,
        out_weight,
        preferred_element_type=jnp.float32,
    )
    if paired:
        summed_rows = scatter_sum_pairs(projected.astype(jnp.bfloat16), tp_count)
    else:
        summed_rows = scatter_sum_tp(projected.astype(jnp.bfloat16), tp_count, 2)
    summed_rows = summed_rows.astype(jnp.bfloat16)
    return (summed_rows[:local_rows], summed_rows[local_rows:])


def solution(mesh):
    return jax.shard_map(
        functools.partial(on_device, ctx_layout(mesh), mesh.shape["tp"], tp_paired(mesh)),
        mesh=mesh,
        in_specs=(
            P("ctx", None),
            P(),
            P("ctx", "tp"),
            P("ctx", "tp"),
            P("ctx", "tp"),
            P("tp", "ctx"),
            P(),
            P(),
        ),
        out_specs=(P("ctx", "tp"), P(None, "tp")),
        check_vma=False,
    )
```

```python
import functools
import math

import jax
import jax.numpy as jnp
from jax import lax
from jax.experimental import pallas as pl
from jax.experimental.pallas import tpu as pltpu
from jax.sharding import PartitionSpec as P

HEAD_SIZE = 128


floor_value = -1e30


def _gather_kernel(
    z_count,
    p_count,
    first_ref,
    second_ref,
    first_out,
    second_out,
    first_z,
    first_p,
    second_p,
    second_z,
    local_sems,
):
    me = lax.axis_index("ctx")
    z_me = me // p_count
    p_me = lax.rem(me, p_count)
    mesh_ids = pl.DeviceIdType.MESH
    barrier = pltpu.get_barrier_semaphore()

    def z_peer(step):
        return lax.rem(z_me + step, z_count)

    def p_peer(step):
        return lax.rem(p_me + step, p_count)

    def z_target(peer):
        return peer * p_count + p_me

    def p_target(peer):
        return z_me * p_count + peer

    def greet(peer_of, target_of):
        def body(step, carry):
            pl.semaphore_signal(
                barrier, 1, device_id={"ctx": target_of(peer_of(step))}, device_id_type=mesh_ids
            )
            return carry

        return body

    lax.fori_loop(1, z_count, greet(z_peer, z_target), 0)
    lax.fori_loop(1, p_count, greet(p_peer, p_target), 0)
    pl.semaphore_wait(barrier, z_count + p_count - 2)

    def remote(src, dst, send_sem, recv_sem, target):
        return pltpu.make_async_remote_copy(
            src_ref=src,
            dst_ref=dst,
            send_sem=send_sem,
            recv_sem=recv_sem,
            device_id={"ctx": target},
            device_id_type=mesh_ids,
        )

    def first_one(peer, slot):
        return remote(
            first_ref, first_out.at[p_me, slot], first_z[0].at[peer], first_z[1].at[slot],
            z_target(peer),
        )

    def second_one(peer, slot):
        return remote(
            second_ref, second_out.at[z_me, slot], second_p[0].at[peer], second_p[1].at[slot],
            p_target(peer),
        )

    def first_two(peer, row, slot):
        return remote(
            first_out.at[row, slot], first_out.at[row, slot], first_p[0].at[peer],
            first_p[1].at[row], p_target(peer),
        )

    def second_two(peer, row, slot):
        return remote(
            second_out.at[row, slot], second_out.at[row, slot], second_z[0].at[peer],
            second_z[1].at[row], z_target(peer),
        )

    def first_rows(peer, row):
        return remote(
            first_out.at[row], first_out.at[row], first_p[0].at[peer], first_p[1].at[row],
            p_target(peer),
        )

    def second_rows(peer, row):
        return remote(
            second_out.at[row], second_out.at[row], second_z[0].at[peer], second_z[1].at[row],
            z_target(peer),
        )

    first_own = pltpu.make_async_copy(first_ref, first_out.at[p_me, z_me], local_sems.at[0])
    second_own = pltpu.make_async_copy(second_ref, second_out.at[z_me, p_me], local_sems.at[1])
    first_own.start()
    second_own.start()

    def start_one(step, carry):
        @pl.when(step < z_count)
        def _():
            first_one(z_peer(step), z_me).start()

        @pl.when(step < p_count)
        def _():
            second_one(p_peer(step), p_me).start()

        return carry

    rounds = max(z_count, p_count)
    lax.fori_loop(1, rounds, start_one, 0)

    def forward_first(slot):
        def body(step, carry):
            first_two(p_peer(step), p_me, slot).start()
            return carry

        lax.fori_loop(1, p_count, body, 0)

    def forward_second(slot):
        def body(step, carry):
            second_two(z_peer(step), z_me, slot).start()
            return carry

        lax.fori_loop(1, z_count, body, 0)

    first_own.wait()
    forward_first(z_me)
    second_own.wait()
    forward_second(p_me)

    def relay(step, carry):
        @pl.when(step < z_count)
        def _():
            slot = z_peer(step)
            first_one(slot, slot).wait_recv()
            forward_first(slot)

        @pl.when(step < p_count)
        def _():
            slot = p_peer(step)
            second_one(slot, slot).wait_recv()
            forward_second(slot)

        return carry

    lax.fori_loop(1, rounds, relay, 0)

    def drain(step, carry):
        @pl.when(step < z_count)
        def _():
            peer = z_peer(step)
            first_one(peer, z_me).wait_send()
            second_rows(peer, z_me).wait_send()
            second_rows(peer, peer).wait_recv()

        @pl.when(step < p_count)
        def _():
            peer = p_peer(step)
            second_one(peer, p_me).wait_send()
            first_rows(peer, p_me).wait_send()
            first_rows(peer, peer).wait_recv()

        return carry

    lax.fori_loop(1, rounds, drain, 0)


def gather_ctx(piece, layout, kernel_id):
    z_count, p_count = layout
    rows, cols = piece.shape
    lane = 128
    by_columns = cols % (3 * lane) == 0
    if by_columns:
        head = 2 * cols // 3
        shapes = ((rows, head), (rows, cols - head))
        pieces = (piece[:, :head], piece[:, head:])
    else:
        tile = 16
        flat = piece.reshape(rows * cols // lane, lane)
        count = flat.shape[0]
        head = min(count - tile, max(tile, round(count * 2 / (3 * tile)) * tile))
        shapes = ((head, lane), (count - head, lane))
        pieces = (flat[:head], flat[head:])
    dma_pairs = [
        pltpu.SemaphoreType.DMA((z_count,)),
        pltpu.SemaphoreType.DMA((z_count,)),
        pltpu.SemaphoreType.DMA((p_count,)),
        pltpu.SemaphoreType.DMA((p_count,)),
    ]

    def kernel(first_ref, second_ref, first_out, second_out, *sems):
        _gather_kernel(
            z_count, p_count, first_ref, second_ref, first_out, second_out,
            (sems[0], sems[1]), (sems[2], sems[3]), (sems[4], sems[5]), (sems[6], sems[7]),
            sems[8],
        )

    first, second = pl.pallas_call(
        kernel,
        out_shape=(
            jax.ShapeDtypeStruct((p_count, z_count) + shapes[0], piece.dtype),
            jax.ShapeDtypeStruct((z_count, p_count) + shapes[1], piece.dtype),
        ),
        in_specs=[pl.BlockSpec(memory_space=pl.ANY)] * 2,
        out_specs=(pl.BlockSpec(memory_space=pl.ANY),) * 2,
        scratch_shapes=dma_pairs + [dma_pairs[2], dma_pairs[3], dma_pairs[0], dma_pairs[1]]
        + [pltpu.SemaphoreType.DMA((2,))],
        compiler_params=pltpu.CompilerParams(collective_id=kernel_id, has_side_effects=True),
    )(*pieces)
    joined = jnp.concatenate([first.transpose(1, 0, 2, 3), second], axis=3 if by_columns else 2)
    joined = joined.reshape(z_count, p_count, rows, cols)
    return joined.reshape(z_count * p_count * rows, cols)


def _scatter_kernel(count, part_ref, out_ref, send_sems, recv_sems, local_sem):
    me = lax.axis_index("tp")
    width = out_ref.shape[2]
    mesh_ids = pl.DeviceIdType.MESH
    barrier = pltpu.get_barrier_semaphore()

    def greet(step, carry):
        peer = lax.rem(me + step, count)
        pl.semaphore_signal(barrier, 1, device_id={"tp": peer}, device_id_type=mesh_ids)
        return carry

    lax.fori_loop(1, count, greet, 0)
    pl.semaphore_wait(barrier, count - 1)

    def columns(index):
        return pl.ds(pl.multiple_of(index * width, width), width)

    own = pltpu.make_async_copy(part_ref.at[:, columns(me)], out_ref.at[me], local_sem)
    own.start()

    def remote(peer, slot):
        return pltpu.make_async_remote_copy(
            src_ref=part_ref.at[:, columns(peer)],
            dst_ref=out_ref.at[slot],
            send_sem=send_sems.at[peer],
            recv_sem=recv_sems.at[slot],
            device_id={"tp": peer},
            device_id_type=mesh_ids,
        )

    def send(step, carry):
        remote(lax.rem(me + step, count), me).start()
        return carry

    def finish(step, carry):
        peer = lax.rem(me + step, count)
        remote(peer, me).wait_send()
        remote(peer, peer).wait_recv()
        return carry

    lax.fori_loop(1, count, send, 0)
    lax.fori_loop(1, count, finish, 0)
    own.wait()


def scatter_sum_tp(part, count, kernel_id):
    rows, cols = part.shape
    pieces = pl.pallas_call(
        functools.partial(_scatter_kernel, count),
        out_shape=jax.ShapeDtypeStruct((count, rows, cols // count), part.dtype),
        in_specs=[pl.BlockSpec(memory_space=pl.ANY)],
        out_specs=pl.BlockSpec(memory_space=pl.ANY),
        scratch_shapes=[
            pltpu.SemaphoreType.DMA((count,)),
            pltpu.SemaphoreType.DMA((count,)),
            pltpu.SemaphoreType.DMA(()),
        ],
        compiler_params=pltpu.CompilerParams(collective_id=kernel_id, has_side_effects=True),
    )(part)
    return jnp.sum(pieces.astype(jnp.float32), axis=0)


def ctx_layout(mesh):
    count = mesh.shape["ctx"]
    column = mesh.devices.transpose(
        mesh.axis_names.index("ctx"), mesh.axis_names.index("tp")
    )[:, 0]
    try:
        planes = [device.coords[2] for device in column]
    except (AttributeError, IndexError, TypeError):
        return (count, 1)
    p_count = 1
    while p_count < count and planes[p_count] == planes[0]:
        p_count += 1
    if count % p_count:
        return (count, 1)
    for index in range(count):
        if planes[index] != planes[(index // p_count) * p_count]:
            return (count, 1)
    return (count // p_count, p_count)


def initial_positions(block_map, first_row, row_count, block_rows):
    row_ids = first_row + jnp.arange(row_count, dtype=jnp.int32)
    block_ids = row_ids // block_rows
    table_ids = jnp.arange(block_map.shape[0], dtype=jnp.int32)
    mapped = jnp.sum(
        jnp.where(block_ids[:, None] == table_ids[None, :], block_map[None, :], 0), axis=1
    )
    return mapped * block_rows + row_ids % block_rows


def request_index(positions, request_ends):
    return jnp.sum((positions[:, None] >= request_ends[None, :]).astype(jnp.int32), axis=1)


def round_weights(weights):
    rounded = weights.astype(jnp.bfloat16)
    rounded = lax.optimization_barrier(rounded)
    return rounded.astype(jnp.float32)


def softmax_parts(
    dec_heads, projected_key_rows, projected_value_rows, owned, kv_heads, head_dim, score_scale
):
    row_count = projected_key_rows.shape[0]
    scores = (
        jnp.einsum(
            "rgjd,tgd->rgjt",
            dec_heads,
            projected_key_rows.reshape(row_count, kv_heads, head_dim),
            preferred_element_type=jnp.float32,
        )
        * score_scale
    )
    scores = jnp.where(owned, scores, floor_value)
    part_peak = jnp.max(scores, axis=3)
    weights = jnp.where(owned, jnp.exp(scores - part_peak[..., None]), 0.0)
    part_total = jnp.sum(weights, axis=3)
    part_mixed = jnp.einsum(
        "rgjt,tgd->rgjd",
        weights.astype(jnp.bfloat16),
        projected_value_rows.reshape(row_count, kv_heads, head_dim),
        preferred_element_type=jnp.float32,
    )
    return (part_peak, part_total, part_mixed)


def on_device(
    layout, tp_count, tokens, new_token_states, w_query, key_matrix, value_matrix, w_out, lengths, block_map
):
    local_rows = tokens.shape[0]
    block_rows = local_rows // 2
    request_count = new_token_states.shape[0]
    head_dim = HEAD_SIZE
    query_width = w_query.shape[1]
    kv_width = key_matrix.shape[1]
    kv_heads = kv_width // head_dim
    query_group_count = query_width // kv_width
    score_scale = 1.0 / math.sqrt(head_dim)
    device = lax.axis_index("ctx")
    request_ends = jnp.cumsum(lengths)
    inputs = jnp.concatenate([tokens, new_token_states], axis=0)
    joined = gather_ctx(
        jnp.concatenate([w_query, key_matrix, value_matrix, w_out.T], axis=1), layout, 0
    )
    qkv_width = query_width + 2 * kv_width
    projected_all = jnp.dot(
        inputs, joined[:, :qkv_width], preferred_element_type=jnp.float32
    ).astype(jnp.bfloat16)
    out_weight = joined[:, qkv_width:].T
    query_all = projected_all[:, :query_width]
    key_all = projected_all[:, query_width : query_width + kv_width]
    value_all = projected_all[:, query_width + kv_width :]
    local_query = query_all[:local_rows]
    local_keys = key_all[:local_rows]
    local_values = value_all[:local_rows]
    dec_query = query_all[local_rows:]
    decode_key_rows = key_all[local_rows:]
    decode_value_rows = value_all[local_rows:]
    token_pos = initial_positions(block_map, device * local_rows, local_rows, block_rows)
    token_request = request_index(token_pos, request_ends)
    query_heads = local_query.reshape(local_rows, kv_heads, query_group_count, head_dim)

    def attend(running, shard_pieces, first_row):
        peak_run, total_run, mixed_run = running
        key_piece, value_piece = shard_pieces
        row_count = key_piece.shape[0]
        key_pos = lax.dynamic_slice_in_dim(cache_pos, first_row, row_count, 0)
        key_request = lax.dynamic_slice_in_dim(cache_request, first_row, row_count, 0)
        allowed = (key_request[None, :] == token_request[:, None]) & (
            key_pos[None, :] <= token_pos[:, None]
        )
        scores = (
            jnp.einsum(
                "tgjd,kgd->gjtk",
                query_heads,
                key_piece.reshape(row_count, kv_heads, head_dim),
                preferred_element_type=jnp.float32,
            )
            * score_scale
        )
        scores = jnp.where(allowed, scores, floor_value)
        peak_new = jnp.maximum(peak_run, jnp.max(scores, axis=3))
        weights = jnp.where(allowed, jnp.exp(scores - peak_new[..., None]), 0.0)
        rescale = jnp.exp(peak_run - peak_new)
        total_new = total_run * rescale + jnp.sum(weights, axis=3)
        mixed_new = mixed_run * rescale[..., None] + jnp.einsum(
            "gjtk,kgd->gjtd",
            weights.astype(jnp.bfloat16),
            value_piece.reshape(row_count, kv_heads, head_dim),
            preferred_element_type=jnp.float32,
        )
        return (peak_new, total_new, mixed_new)

    start_state = (
        jnp.full((kv_heads, query_group_count, local_rows), floor_value, jnp.float32),
        jnp.zeros((kv_heads, query_group_count, local_rows), jnp.float32),
        jnp.zeros((kv_heads, query_group_count, local_rows, head_dim), jnp.float32),
    )
    dec_heads = dec_query.reshape(request_count, kv_heads, query_group_count, head_dim)
    request_ids = jnp.arange(request_count, dtype=jnp.int32)
    cache_both = gather_ctx(
        jnp.concatenate([local_keys, local_values], axis=1), layout, 1
    )
    cache_keys = cache_both[:, :kv_width]
    cache_values = cache_both[:, kv_width:]
    total_rows = cache_keys.shape[0]
    step_rows = total_rows
    cache_pos = (
        block_map[:, None] * block_rows + jnp.arange(block_rows, dtype=jnp.int32)[None, :]
    ).reshape(total_rows)
    cache_request = request_index(cache_pos, request_ends)

    def key_step(running, step_index):
        first_row = step_index * step_rows
        pieces = (
            lax.dynamic_slice_in_dim(cache_keys, first_row, step_rows, 0),
            lax.dynamic_slice_in_dim(cache_values, first_row, step_rows, 0),
        )
        return (attend(running, pieces, first_row), None)

    final_state, unused = lax.scan(
        key_step, start_state, jnp.arange(total_rows // step_rows, dtype=jnp.int32)
    )
    peak_run, total_run, mixed_run = final_state
    owned = (cache_request[None, :] == request_ids[:, None])[:, None, None, :]
    cache_peak, cache_total, cache_mixed = softmax_parts(
        dec_heads, cache_keys, cache_values, owned, kv_heads, head_dim, score_scale
    )
    attended = (
        (mixed_run / total_run[..., None]).transpose(2, 0, 1, 3).reshape(local_rows, query_width)
    )
    attended = attended.astype(jnp.bfloat16)
    own_keys = decode_key_rows.reshape(request_count, kv_heads, 1, head_dim).astype(jnp.float32)
    own_values = decode_value_rows.reshape(request_count, kv_heads, 1, head_dim).astype(jnp.float32)
    self_scores = jnp.sum(dec_heads.astype(jnp.float32) * own_keys, axis=3) * score_scale
    peak_all = jnp.maximum(cache_peak, self_scores)
    rescale = jnp.exp(cache_peak - peak_all)
    self_weights = jnp.exp(self_scores - peak_all)
    dec_total = cache_total * rescale + self_weights
    dec_mixed = (
        cache_mixed * rescale[..., None] + round_weights(self_weights)[..., None] * own_values
    )
    dec_attn = (
        (dec_mixed / dec_total[..., None]).reshape(request_count, query_width).astype(jnp.bfloat16)
    )
    attended_all = jnp.concatenate([attended, dec_attn], axis=0)
    projected = jnp.dot(
        attended_all,
        out_weight,
        preferred_element_type=jnp.float32,
    )
    summed_rows = scatter_sum_tp(projected.astype(jnp.bfloat16), tp_count, 2)
    summed_rows = summed_rows.astype(jnp.bfloat16)
    return (summed_rows[:local_rows], summed_rows[local_rows:])


def solution(mesh):
    return jax.shard_map(
        functools.partial(on_device, ctx_layout(mesh), mesh.shape["tp"]),
        mesh=mesh,
        in_specs=(
            P("ctx", None),
            P(),
            P("ctx", "tp"),
            P("ctx", "tp"),
            P("ctx", "tp"),
            P("tp", "ctx"),
            P(),
            P(),
        ),
        out_specs=(P("ctx", "tp"), P(None, "tp")),
        check_vma=False,
    )
```

```python
import functools
import math

import jax
import jax.numpy as jnp
from jax import lax
from jax.experimental import pallas as pl
from jax.experimental.pallas import tpu as pltpu
from jax.sharding import PartitionSpec as P

HEAD_SIZE = 128


floor_value = -1e30


def _gather_kernel(
    z_count,
    p_count,
    first_ref,
    second_ref,
    first_out,
    second_out,
    first_z,
    first_p,
    second_p,
    second_z,
    local_sems,
):
    me = lax.axis_index("ctx")
    z_me = me // p_count
    p_me = lax.rem(me, p_count)
    mesh_ids = pl.DeviceIdType.MESH
    barrier = pltpu.get_barrier_semaphore()

    def z_peer(step):
        return lax.rem(z_me + step, z_count)

    def p_peer(step):
        return lax.rem(p_me + step, p_count)

    def z_target(peer):
        return peer * p_count + p_me

    def p_target(peer):
        return z_me * p_count + peer

    def greet(peer_of, target_of):
        def body(step, carry):
            pl.semaphore_signal(
                barrier, 1, device_id={"ctx": target_of(peer_of(step))}, device_id_type=mesh_ids
            )
            return carry

        return body

    lax.fori_loop(1, z_count, greet(z_peer, z_target), 0)
    lax.fori_loop(1, p_count, greet(p_peer, p_target), 0)
    pl.semaphore_wait(barrier, z_count + p_count - 2)

    def remote(src, dst, send_sem, recv_sem, target):
        return pltpu.make_async_remote_copy(
            src_ref=src,
            dst_ref=dst,
            send_sem=send_sem,
            recv_sem=recv_sem,
            device_id={"ctx": target},
            device_id_type=mesh_ids,
        )

    def first_one(peer, slot):
        return remote(
            first_ref, first_out.at[p_me, slot], first_z[0].at[peer], first_z[1].at[slot],
            z_target(peer),
        )

    def second_one(peer, slot):
        return remote(
            second_ref, second_out.at[z_me, slot], second_p[0].at[peer], second_p[1].at[slot],
            p_target(peer),
        )

    def first_two(peer, row, slot):
        return remote(
            first_out.at[row, slot], first_out.at[row, slot], first_p[0].at[peer],
            first_p[1].at[row], p_target(peer),
        )

    def second_two(peer, row, slot):
        return remote(
            second_out.at[row, slot], second_out.at[row, slot], second_z[0].at[peer],
            second_z[1].at[row], z_target(peer),
        )

    def first_rows(peer, row):
        return remote(
            first_out.at[row], first_out.at[row], first_p[0].at[peer], first_p[1].at[row],
            p_target(peer),
        )

    def second_rows(peer, row):
        return remote(
            second_out.at[row], second_out.at[row], second_z[0].at[peer], second_z[1].at[row],
            z_target(peer),
        )

    first_own = pltpu.make_async_copy(first_ref, first_out.at[p_me, z_me], local_sems.at[0])
    second_own = pltpu.make_async_copy(second_ref, second_out.at[z_me, p_me], local_sems.at[1])
    first_own.start()
    second_own.start()

    def start_one(step, carry):
        @pl.when(step < z_count)
        def _():
            first_one(z_peer(step), z_me).start()

        @pl.when(step < p_count)
        def _():
            second_one(p_peer(step), p_me).start()

        return carry

    rounds = max(z_count, p_count)
    lax.fori_loop(1, rounds, start_one, 0)

    def forward_first(slot):
        def body(step, carry):
            first_two(p_peer(step), p_me, slot).start()
            return carry

        lax.fori_loop(1, p_count, body, 0)

    def forward_second(slot):
        def body(step, carry):
            second_two(z_peer(step), z_me, slot).start()
            return carry

        lax.fori_loop(1, z_count, body, 0)

    first_own.wait()
    forward_first(z_me)
    second_own.wait()
    forward_second(p_me)

    def relay(step, carry):
        @pl.when(step < z_count)
        def _():
            slot = z_peer(step)
            first_one(slot, slot).wait_recv()
            forward_first(slot)

        @pl.when(step < p_count)
        def _():
            slot = p_peer(step)
            second_one(slot, slot).wait_recv()
            forward_second(slot)

        return carry

    lax.fori_loop(1, rounds, relay, 0)

    def drain(step, carry):
        @pl.when(step < z_count)
        def _():
            peer = z_peer(step)
            first_one(peer, z_me).wait_send()
            second_rows(peer, z_me).wait_send()
            second_rows(peer, peer).wait_recv()

        @pl.when(step < p_count)
        def _():
            peer = p_peer(step)
            second_one(peer, p_me).wait_send()
            first_rows(peer, p_me).wait_send()
            first_rows(peer, peer).wait_recv()

        return carry

    lax.fori_loop(1, rounds, drain, 0)


def gather_ctx(piece, layout, kernel_id, parts=False):
    z_count, p_count = layout
    rows, cols = piece.shape
    lane = 128
    by_columns = cols % (3 * lane) == 0
    if by_columns:
        head = 2 * cols // 3
        shapes = ((rows, head), (rows, cols - head))
        pieces = (piece[:, :head], piece[:, head:])
    else:
        tile = 16
        head = min(rows - tile, max(tile, round(rows * 2 / (3 * tile)) * tile))
        shapes = ((head, cols), (rows - head, cols))
        pieces = (piece[:head], piece[head:])
    dma_pairs = [
        pltpu.SemaphoreType.DMA((z_count,)),
        pltpu.SemaphoreType.DMA((z_count,)),
        pltpu.SemaphoreType.DMA((p_count,)),
        pltpu.SemaphoreType.DMA((p_count,)),
    ]

    def kernel(first_ref, second_ref, first_out, second_out, *sems):
        _gather_kernel(
            z_count, p_count, first_ref, second_ref, first_out, second_out,
            (sems[0], sems[1]), (sems[2], sems[3]), (sems[4], sems[5]), (sems[6], sems[7]),
            sems[8],
        )

    first, second = pl.pallas_call(
        kernel,
        out_shape=(
            jax.ShapeDtypeStruct((p_count, z_count) + shapes[0], piece.dtype),
            jax.ShapeDtypeStruct((z_count, p_count) + shapes[1], piece.dtype),
        ),
        in_specs=[pl.BlockSpec(memory_space=pl.ANY)] * 2,
        out_specs=(pl.BlockSpec(memory_space=pl.ANY),) * 2,
        scratch_shapes=dma_pairs + [dma_pairs[2], dma_pairs[3], dma_pairs[0], dma_pairs[1]]
        + [pltpu.SemaphoreType.DMA((2,))],
        compiler_params=pltpu.CompilerParams(collective_id=kernel_id, has_side_effects=True),
    )(*pieces)
    if parts:
        return first, second
    joined = jnp.concatenate([first.transpose(1, 0, 2, 3), second], axis=3 if by_columns else 2)
    return joined.reshape(z_count * p_count * rows, cols)


def _scatter_kernel(count, part_ref, out_ref, send_sems, recv_sems, local_sem):
    me = lax.axis_index("tp")
    width = out_ref.shape[2]
    mesh_ids = pl.DeviceIdType.MESH
    barrier = pltpu.get_barrier_semaphore()

    def greet(step, carry):
        peer = lax.rem(me + step, count)
        pl.semaphore_signal(barrier, 1, device_id={"tp": peer}, device_id_type=mesh_ids)
        return carry

    lax.fori_loop(1, count, greet, 0)
    pl.semaphore_wait(barrier, count - 1)

    def columns(index):
        return pl.ds(pl.multiple_of(index * width, width), width)

    own = pltpu.make_async_copy(part_ref.at[:, columns(me)], out_ref.at[me], local_sem)
    own.start()

    def remote(peer, slot):
        return pltpu.make_async_remote_copy(
            src_ref=part_ref.at[:, columns(peer)],
            dst_ref=out_ref.at[slot],
            send_sem=send_sems.at[peer],
            recv_sem=recv_sems.at[slot],
            device_id={"tp": peer},
            device_id_type=mesh_ids,
        )

    def send(step, carry):
        remote(lax.rem(me + step, count), me).start()
        return carry

    def finish(step, carry):
        peer = lax.rem(me + step, count)
        remote(peer, me).wait_send()
        remote(peer, peer).wait_recv()
        return carry

    lax.fori_loop(1, count, send, 0)
    lax.fori_loop(1, count, finish, 0)
    own.wait()


def scatter_sum_tp(part, count, kernel_id):
    rows, cols = part.shape
    pieces = pl.pallas_call(
        functools.partial(_scatter_kernel, count),
        out_shape=jax.ShapeDtypeStruct((count, rows, cols // count), part.dtype),
        in_specs=[pl.BlockSpec(memory_space=pl.ANY)],
        out_specs=pl.BlockSpec(memory_space=pl.ANY),
        scratch_shapes=[
            pltpu.SemaphoreType.DMA((count,)),
            pltpu.SemaphoreType.DMA((count,)),
            pltpu.SemaphoreType.DMA(()),
        ],
        compiler_params=pltpu.CompilerParams(collective_id=kernel_id, has_side_effects=True),
    )(part)
    return jnp.sum(pieces.astype(jnp.float32), axis=0)


def ctx_layout(mesh):
    count = mesh.shape["ctx"]
    column = mesh.devices.transpose(
        mesh.axis_names.index("ctx"), mesh.axis_names.index("tp")
    )[:, 0]
    try:
        planes = [device.coords[2] for device in column]
    except (AttributeError, IndexError, TypeError):
        return (count, 1)
    p_count = 1
    while p_count < count and planes[p_count] == planes[0]:
        p_count += 1
    if count % p_count:
        return (count, 1)
    for index in range(count):
        if planes[index] != planes[(index // p_count) * p_count]:
            return (count, 1)
    return (count // p_count, p_count)


def initial_positions(block_map, first_row, row_count, block_rows):
    row_ids = first_row + jnp.arange(row_count, dtype=jnp.int32)
    block_ids = row_ids // block_rows
    table_ids = jnp.arange(block_map.shape[0], dtype=jnp.int32)
    mapped = jnp.sum(
        jnp.where(block_ids[:, None] == table_ids[None, :], block_map[None, :], 0), axis=1
    )
    return mapped * block_rows + row_ids % block_rows


def request_index(positions, request_ends):
    return jnp.sum((positions[:, None] >= request_ends[None, :]).astype(jnp.int32), axis=1)


def round_weights(weights):
    rounded = weights.astype(jnp.bfloat16)
    rounded = lax.optimization_barrier(rounded)
    return rounded.astype(jnp.float32)


def softmax_parts(
    dec_heads, projected_key_rows, projected_value_rows, owned, kv_heads, head_dim, score_scale
):
    row_count = projected_key_rows.shape[0]
    scores = (
        jnp.einsum(
            "rgjd,tgd->rgjt",
            dec_heads,
            projected_key_rows.reshape(row_count, kv_heads, head_dim),
            preferred_element_type=jnp.float32,
        )
        * score_scale
    )
    scores = jnp.where(owned, scores, floor_value)
    part_peak = jnp.max(scores, axis=3)
    weights = jnp.where(owned, jnp.exp(scores - part_peak[..., None]), 0.0)
    part_total = jnp.sum(weights, axis=3)
    part_mixed = jnp.einsum(
        "rgjt,tgd->rgjd",
        weights.astype(jnp.bfloat16),
        projected_value_rows.reshape(row_count, kv_heads, head_dim),
        preferred_element_type=jnp.float32,
    )
    return (part_peak, part_total, part_mixed)


def on_device(
    layout, tp_count, tokens, new_token_states, w_query, key_matrix, value_matrix, w_out, lengths, block_map
):
    local_rows = tokens.shape[0]
    block_rows = local_rows // 2
    request_count = new_token_states.shape[0]
    head_dim = HEAD_SIZE
    query_width = w_query.shape[1]
    kv_width = key_matrix.shape[1]
    kv_heads = kv_width // head_dim
    query_group_count = query_width // kv_width
    score_scale = 1.0 / math.sqrt(head_dim)
    device = lax.axis_index("ctx")
    request_ends = jnp.cumsum(lengths)
    inputs = jnp.concatenate([tokens, new_token_states], axis=0)
    z_count, p_count = layout
    model_width = inputs.shape[1]
    qkv_width = query_width + 2 * kv_width
    if (qkv_width + w_out.shape[0]) % 384 == 0 and 2 * w_out.shape[0] == qkv_width:
        qkv_rows, out_rows = gather_ctx(
            jnp.concatenate([w_query, key_matrix, value_matrix, w_out.T], axis=1),
            layout,
            0,
            parts=True,
        )
        row_block = model_width // (z_count * p_count)
        permuted = inputs.reshape(-1, z_count, p_count, row_block).transpose(0, 2, 1, 3)
        projected_all = jnp.dot(
            permuted.reshape(-1, model_width),
            qkv_rows.reshape(model_width, qkv_width),
            preferred_element_type=jnp.float32,
        ).astype(jnp.bfloat16)
        out_weight_t = out_rows.reshape(model_width, w_out.shape[0])
    else:
        joined = gather_ctx(
            jnp.concatenate([w_query, key_matrix, value_matrix, w_out.T], axis=1), layout, 0
        )
        projected_all = jnp.dot(
            inputs, joined[:, :qkv_width], preferred_element_type=jnp.float32
        ).astype(jnp.bfloat16)
        out_weight_t = joined[:, qkv_width:]
    query_all = projected_all[:, :query_width]
    key_all = projected_all[:, query_width : query_width + kv_width]
    value_all = projected_all[:, query_width + kv_width :]
    local_query = query_all[:local_rows]
    local_keys = key_all[:local_rows]
    local_values = value_all[:local_rows]
    dec_query = query_all[local_rows:]
    decode_key_rows = key_all[local_rows:]
    decode_value_rows = value_all[local_rows:]
    token_pos = initial_positions(block_map, device * local_rows, local_rows, block_rows)
    token_request = request_index(token_pos, request_ends)
    query_heads = local_query.reshape(local_rows, kv_heads, query_group_count, head_dim)

    def attend(running, shard_pieces, first_row):
        peak_run, total_run, mixed_run = running
        key_piece, value_piece = shard_pieces
        row_count = key_piece.shape[0]
        key_pos = lax.dynamic_slice_in_dim(cache_pos, first_row, row_count, 0)
        key_request = lax.dynamic_slice_in_dim(cache_request, first_row, row_count, 0)
        allowed = (key_request[None, :] == token_request[:, None]) & (
            key_pos[None, :] <= token_pos[:, None]
        )
        scores = (
            jnp.einsum(
                "tgjd,kgd->gjtk",
                query_heads,
                key_piece.reshape(row_count, kv_heads, head_dim),
                preferred_element_type=jnp.float32,
            )
            * score_scale
        )
        scores = jnp.where(allowed, scores, floor_value)
        peak_new = jnp.maximum(peak_run, jnp.max(scores, axis=3))
        weights = jnp.where(allowed, jnp.exp(scores - peak_new[..., None]), 0.0)
        rescale = jnp.exp(peak_run - peak_new)
        total_new = total_run * rescale + jnp.sum(weights, axis=3)
        mixed_new = mixed_run * rescale[..., None] + jnp.einsum(
            "gjtk,kgd->gjtd",
            weights.astype(jnp.bfloat16),
            value_piece.reshape(row_count, kv_heads, head_dim),
            preferred_element_type=jnp.float32,
        )
        return (peak_new, total_new, mixed_new)

    start_state = (
        jnp.full((kv_heads, query_group_count, local_rows), floor_value, jnp.float32),
        jnp.zeros((kv_heads, query_group_count, local_rows), jnp.float32),
        jnp.zeros((kv_heads, query_group_count, local_rows, head_dim), jnp.float32),
    )
    dec_heads = dec_query.reshape(request_count, kv_heads, query_group_count, head_dim)
    request_ids = jnp.arange(request_count, dtype=jnp.int32)
    cache_both = gather_ctx(
        jnp.concatenate([local_keys, local_values], axis=1), layout, 1
    )
    cache_keys = cache_both[:, :kv_width]
    cache_values = cache_both[:, kv_width:]
    total_rows = cache_keys.shape[0]
    step_rows = total_rows
    cache_pos = (
        block_map[:, None] * block_rows + jnp.arange(block_rows, dtype=jnp.int32)[None, :]
    ).reshape(total_rows)
    cache_request = request_index(cache_pos, request_ends)

    def key_step(running, step_index):
        first_row = step_index * step_rows
        pieces = (
            lax.dynamic_slice_in_dim(cache_keys, first_row, step_rows, 0),
            lax.dynamic_slice_in_dim(cache_values, first_row, step_rows, 0),
        )
        return (attend(running, pieces, first_row), None)

    final_state, unused = lax.scan(
        key_step, start_state, jnp.arange(total_rows // step_rows, dtype=jnp.int32)
    )
    peak_run, total_run, mixed_run = final_state
    owned = (cache_request[None, :] == request_ids[:, None])[:, None, None, :]
    cache_peak, cache_total, cache_mixed = softmax_parts(
        dec_heads, cache_keys, cache_values, owned, kv_heads, head_dim, score_scale
    )
    attended = (
        (mixed_run / total_run[..., None]).transpose(2, 0, 1, 3).reshape(local_rows, query_width)
    )
    attended = attended.astype(jnp.bfloat16)
    own_keys = decode_key_rows.reshape(request_count, kv_heads, 1, head_dim).astype(jnp.float32)
    own_values = decode_value_rows.reshape(request_count, kv_heads, 1, head_dim).astype(jnp.float32)
    self_scores = jnp.sum(dec_heads.astype(jnp.float32) * own_keys, axis=3) * score_scale
    peak_all = jnp.maximum(cache_peak, self_scores)
    rescale = jnp.exp(cache_peak - peak_all)
    self_weights = jnp.exp(self_scores - peak_all)
    dec_total = cache_total * rescale + self_weights
    dec_mixed = (
        cache_mixed * rescale[..., None] + round_weights(self_weights)[..., None] * own_values
    )
    dec_attn = (
        (dec_mixed / dec_total[..., None]).reshape(request_count, query_width).astype(jnp.bfloat16)
    )
    attended_all = jnp.concatenate([attended, dec_attn], axis=0)
    projected = lax.dot_general(
        attended_all,
        out_weight_t,
        (((1,), (1,)), ((), ())),
        preferred_element_type=jnp.float32,
    )
    summed_rows = scatter_sum_tp(projected.astype(jnp.bfloat16), tp_count, 2)
    summed_rows = summed_rows.astype(jnp.bfloat16)
    return (summed_rows[:local_rows], summed_rows[local_rows:])


def solution(mesh):
    return jax.shard_map(
        functools.partial(on_device, ctx_layout(mesh), mesh.shape["tp"]),
        mesh=mesh,
        in_specs=(
            P("ctx", None),
            P(),
            P("ctx", "tp"),
            P("ctx", "tp"),
            P("ctx", "tp"),
            P("tp", "ctx"),
            P(),
            P(),
        ),
        out_specs=(P("ctx", "tp"), P(None, "tp")),
        check_vma=False,
    )
```

```python
import functools
import math

import jax
import jax.numpy as jnp
from jax import lax
from jax.experimental import pallas as pl
from jax.experimental.pallas import tpu as pltpu
from jax.sharding import PartitionSpec as P

HEAD_SIZE = 128


floor_value = -1e30


def _gather_kernel(
    z_count,
    p_count,
    first_ref,
    second_ref,
    first_out,
    second_out,
    first_z,
    first_p,
    second_p,
    second_z,
    local_sems,
):
    me = lax.axis_index("ctx")
    z_me = me // p_count
    p_me = lax.rem(me, p_count)
    mesh_ids = pl.DeviceIdType.MESH
    barrier = pltpu.get_barrier_semaphore()

    def z_peer(step):
        return lax.rem(z_me + step, z_count)

    def p_peer(step):
        return lax.rem(p_me + step, p_count)

    def z_target(peer):
        return peer * p_count + p_me

    def p_target(peer):
        return z_me * p_count + peer

    def greet(peer_of, target_of):
        def body(step, carry):
            pl.semaphore_signal(
                barrier, 1, device_id={"ctx": target_of(peer_of(step))}, device_id_type=mesh_ids
            )
            return carry

        return body

    lax.fori_loop(1, z_count, greet(z_peer, z_target), 0)
    lax.fori_loop(1, p_count, greet(p_peer, p_target), 0)
    pl.semaphore_wait(barrier, z_count + p_count - 2)

    def remote(src, dst, send_sem, recv_sem, target):
        return pltpu.make_async_remote_copy(
            src_ref=src,
            dst_ref=dst,
            send_sem=send_sem,
            recv_sem=recv_sem,
            device_id={"ctx": target},
            device_id_type=mesh_ids,
        )

    def first_one(peer, slot):
        return remote(
            first_ref, first_out.at[slot, p_me], first_z[0].at[peer], first_z[1].at[slot],
            z_target(peer),
        )

    def second_one(peer, slot):
        return remote(
            second_ref, second_out.at[z_me, slot], second_p[0].at[peer], second_p[1].at[slot],
            p_target(peer),
        )

    def first_two(peer, row, slot):
        return remote(
            first_out.at[slot, row], first_out.at[slot, row], first_p[0].at[peer],
            first_p[1].at[row], p_target(peer),
        )

    def second_two(peer, row, slot):
        return remote(
            second_out.at[row, slot], second_out.at[row, slot], second_z[0].at[peer],
            second_z[1].at[row], z_target(peer),
        )

    def first_rows(peer, row):
        return remote(
            first_out.at[:, row], first_out.at[:, row], first_p[0].at[peer], first_p[1].at[row],
            p_target(peer),
        )

    def second_rows(peer, row):
        return remote(
            second_out.at[row], second_out.at[row], second_z[0].at[peer], second_z[1].at[row],
            z_target(peer),
        )

    first_own = pltpu.make_async_copy(first_ref, first_out.at[z_me, p_me], local_sems.at[0])
    second_own = pltpu.make_async_copy(second_ref, second_out.at[z_me, p_me], local_sems.at[1])
    first_own.start()
    second_own.start()

    def start_one(step, carry):
        @pl.when(step < z_count)
        def _():
            first_one(z_peer(step), z_me).start()

        @pl.when(step < p_count)
        def _():
            second_one(p_peer(step), p_me).start()

        return carry

    rounds = max(z_count, p_count)
    lax.fori_loop(1, rounds, start_one, 0)

    def forward_first(slot):
        def body(step, carry):
            first_two(p_peer(step), p_me, slot).start()
            return carry

        lax.fori_loop(1, p_count, body, 0)

    def forward_second(slot):
        def body(step, carry):
            second_two(z_peer(step), z_me, slot).start()
            return carry

        lax.fori_loop(1, z_count, body, 0)

    first_own.wait()
    forward_first(z_me)
    second_own.wait()
    forward_second(p_me)

    def relay(step, carry):
        @pl.when(step < z_count)
        def _():
            slot = z_peer(step)
            first_one(slot, slot).wait_recv()
            forward_first(slot)

        @pl.when(step < p_count)
        def _():
            slot = p_peer(step)
            second_one(slot, slot).wait_recv()
            forward_second(slot)

        return carry

    lax.fori_loop(1, rounds, relay, 0)

    def drain(step, carry):
        @pl.when(step < z_count)
        def _():
            peer = z_peer(step)
            first_one(peer, z_me).wait_send()
            second_rows(peer, z_me).wait_send()
            second_rows(peer, peer).wait_recv()

        @pl.when(step < p_count)
        def _():
            peer = p_peer(step)
            second_one(peer, p_me).wait_send()
            first_rows(peer, p_me).wait_send()
            first_rows(peer, peer).wait_recv()

        return carry

    lax.fori_loop(1, rounds, drain, 0)


def gather_ctx(piece, layout, kernel_id, parts=False):
    z_count, p_count = layout
    rows, cols = piece.shape
    lane = 128
    by_columns = cols % (3 * lane) == 0
    if by_columns:
        head = 2 * cols // 3
        shapes = ((rows, head), (rows, cols - head))
        pieces = (piece[:, :head], piece[:, head:])
    else:
        tile = 16
        head = min(rows - tile, max(tile, round(rows * 2 / (3 * tile)) * tile))
        shapes = ((head, cols), (rows - head, cols))
        pieces = (piece[:head], piece[head:])
    dma_pairs = [
        pltpu.SemaphoreType.DMA((z_count,)),
        pltpu.SemaphoreType.DMA((z_count,)),
        pltpu.SemaphoreType.DMA((p_count,)),
        pltpu.SemaphoreType.DMA((p_count,)),
    ]

    def kernel(first_ref, second_ref, first_out, second_out, *sems):
        _gather_kernel(
            z_count, p_count, first_ref, second_ref, first_out, second_out,
            (sems[0], sems[1]), (sems[2], sems[3]), (sems[4], sems[5]), (sems[6], sems[7]),
            sems[8],
        )

    first, second = pl.pallas_call(
        kernel,
        out_shape=(
            jax.ShapeDtypeStruct((z_count, p_count) + shapes[0], piece.dtype),
            jax.ShapeDtypeStruct((z_count, p_count) + shapes[1], piece.dtype),
        ),
        in_specs=[pl.BlockSpec(memory_space=pl.ANY)] * 2,
        out_specs=(pl.BlockSpec(memory_space=pl.ANY),) * 2,
        scratch_shapes=dma_pairs + [dma_pairs[2], dma_pairs[3], dma_pairs[0], dma_pairs[1]]
        + [pltpu.SemaphoreType.DMA((2,))],
        compiler_params=pltpu.CompilerParams(collective_id=kernel_id, has_side_effects=True),
    )(*pieces)
    if parts:
        return first, second
    joined = jnp.concatenate([first, second], axis=3 if by_columns else 2)
    return joined.reshape(z_count * p_count * rows, cols)


def _scatter_kernel(count, part_ref, out_ref, send_sems, recv_sems, local_sem):
    me = lax.axis_index("tp")
    width = out_ref.shape[2]
    mesh_ids = pl.DeviceIdType.MESH
    barrier = pltpu.get_barrier_semaphore()

    def greet(step, carry):
        peer = lax.rem(me + step, count)
        pl.semaphore_signal(barrier, 1, device_id={"tp": peer}, device_id_type=mesh_ids)
        return carry

    lax.fori_loop(1, count, greet, 0)
    pl.semaphore_wait(barrier, count - 1)

    def columns(index):
        return pl.ds(pl.multiple_of(index * width, width), width)

    own = pltpu.make_async_copy(part_ref.at[:, columns(me)], out_ref.at[me], local_sem)
    own.start()

    def remote(peer, slot):
        return pltpu.make_async_remote_copy(
            src_ref=part_ref.at[:, columns(peer)],
            dst_ref=out_ref.at[slot],
            send_sem=send_sems.at[peer],
            recv_sem=recv_sems.at[slot],
            device_id={"tp": peer},
            device_id_type=mesh_ids,
        )

    def send(step, carry):
        remote(lax.rem(me + step, count), me).start()
        return carry

    def finish(step, carry):
        peer = lax.rem(me + step, count)
        remote(peer, me).wait_send()
        remote(peer, peer).wait_recv()
        return carry

    lax.fori_loop(1, count, send, 0)
    lax.fori_loop(1, count, finish, 0)
    own.wait()


def scatter_sum_tp(part, count, kernel_id):
    rows, cols = part.shape
    pieces = pl.pallas_call(
        functools.partial(_scatter_kernel, count),
        out_shape=jax.ShapeDtypeStruct((count, rows, cols // count), part.dtype),
        in_specs=[pl.BlockSpec(memory_space=pl.ANY)],
        out_specs=pl.BlockSpec(memory_space=pl.ANY),
        scratch_shapes=[
            pltpu.SemaphoreType.DMA((count,)),
            pltpu.SemaphoreType.DMA((count,)),
            pltpu.SemaphoreType.DMA(()),
        ],
        compiler_params=pltpu.CompilerParams(collective_id=kernel_id, has_side_effects=True),
    )(part)
    return jnp.sum(pieces.astype(jnp.float32), axis=0)


def ctx_layout(mesh):
    count = mesh.shape["ctx"]
    column = mesh.devices.transpose(
        mesh.axis_names.index("ctx"), mesh.axis_names.index("tp")
    )[:, 0]
    try:
        planes = [device.coords[2] for device in column]
    except (AttributeError, IndexError, TypeError):
        return (count, 1)
    p_count = 1
    while p_count < count and planes[p_count] == planes[0]:
        p_count += 1
    if count % p_count:
        return (count, 1)
    for index in range(count):
        if planes[index] != planes[(index // p_count) * p_count]:
            return (count, 1)
    return (count // p_count, p_count)


def initial_positions(block_map, first_row, row_count, block_rows):
    row_ids = first_row + jnp.arange(row_count, dtype=jnp.int32)
    block_ids = row_ids // block_rows
    table_ids = jnp.arange(block_map.shape[0], dtype=jnp.int32)
    mapped = jnp.sum(
        jnp.where(block_ids[:, None] == table_ids[None, :], block_map[None, :], 0), axis=1
    )
    return mapped * block_rows + row_ids % block_rows


def request_index(positions, request_ends):
    return jnp.sum((positions[:, None] >= request_ends[None, :]).astype(jnp.int32), axis=1)


def round_weights(weights):
    rounded = weights.astype(jnp.bfloat16)
    rounded = lax.optimization_barrier(rounded)
    return rounded.astype(jnp.float32)


def softmax_parts(
    dec_heads, projected_key_rows, projected_value_rows, owned, kv_heads, head_dim, score_scale
):
    row_count = projected_key_rows.shape[0]
    scores = (
        jnp.einsum(
            "rgjd,tgd->rgjt",
            dec_heads,
            projected_key_rows.reshape(row_count, kv_heads, head_dim),
            preferred_element_type=jnp.float32,
        )
        * score_scale
    )
    scores = jnp.where(owned, scores, floor_value)
    part_peak = jnp.max(scores, axis=3)
    weights = jnp.where(owned, jnp.exp(scores - part_peak[..., None]), 0.0)
    part_total = jnp.sum(weights, axis=3)
    part_mixed = jnp.einsum(
        "rgjt,tgd->rgjd",
        weights.astype(jnp.bfloat16),
        projected_value_rows.reshape(row_count, kv_heads, head_dim),
        preferred_element_type=jnp.float32,
    )
    return (part_peak, part_total, part_mixed)


def on_device(
    layout, tp_count, tokens, new_token_states, w_query, key_matrix, value_matrix, w_out, lengths, block_map
):
    local_rows = tokens.shape[0]
    block_rows = local_rows // 2
    request_count = new_token_states.shape[0]
    head_dim = HEAD_SIZE
    query_width = w_query.shape[1]
    kv_width = key_matrix.shape[1]
    kv_heads = kv_width // head_dim
    query_group_count = query_width // kv_width
    score_scale = 1.0 / math.sqrt(head_dim)
    device = lax.axis_index("ctx")
    request_ends = jnp.cumsum(lengths)
    inputs = jnp.concatenate([tokens, new_token_states], axis=0)
    z_count, p_count = layout
    model_width = inputs.shape[1]
    qkv_width = query_width + 2 * kv_width
    if (qkv_width + w_out.shape[0]) % 384 == 0 and 2 * w_out.shape[0] == qkv_width:
        qkv_rows, out_rows = gather_ctx(
            jnp.concatenate([w_query, key_matrix, value_matrix, w_out.T], axis=1),
            layout,
            0,
            parts=True,
        )
        projected_all = jnp.dot(
            inputs,
            qkv_rows.reshape(model_width, qkv_width),
            preferred_element_type=jnp.float32,
        ).astype(jnp.bfloat16)
        out_weight_t = out_rows.reshape(model_width, w_out.shape[0])
    else:
        joined = gather_ctx(
            jnp.concatenate([w_query, key_matrix, value_matrix, w_out.T], axis=1), layout, 0
        )
        projected_all = jnp.dot(
            inputs, joined[:, :qkv_width], preferred_element_type=jnp.float32
        ).astype(jnp.bfloat16)
        out_weight_t = joined[:, qkv_width:]
    query_all = projected_all[:, :query_width]
    key_all = projected_all[:, query_width : query_width + kv_width]
    value_all = projected_all[:, query_width + kv_width :]
    local_query = query_all[:local_rows]
    local_keys = key_all[:local_rows]
    local_values = value_all[:local_rows]
    dec_query = query_all[local_rows:]
    decode_key_rows = key_all[local_rows:]
    decode_value_rows = value_all[local_rows:]
    token_pos = initial_positions(block_map, device * local_rows, local_rows, block_rows)
    token_request = request_index(token_pos, request_ends)
    query_heads = local_query.reshape(local_rows, kv_heads, query_group_count, head_dim)

    def attend(running, shard_pieces, first_row):
        peak_run, total_run, mixed_run = running
        key_piece, value_piece = shard_pieces
        row_count = key_piece.shape[0]
        key_pos = lax.dynamic_slice_in_dim(cache_pos, first_row, row_count, 0)
        key_request = lax.dynamic_slice_in_dim(cache_request, first_row, row_count, 0)
        allowed = (key_request[None, :] == token_request[:, None]) & (
            key_pos[None, :] <= token_pos[:, None]
        )
        scores = (
            jnp.einsum(
                "tgjd,kgd->gjtk",
                query_heads,
                key_piece.reshape(row_count, kv_heads, head_dim),
                preferred_element_type=jnp.float32,
            )
            * score_scale
        )
        scores = jnp.where(allowed, scores, floor_value)
        peak_new = jnp.maximum(peak_run, jnp.max(scores, axis=3))
        weights = jnp.where(allowed, jnp.exp(scores - peak_new[..., None]), 0.0)
        rescale = jnp.exp(peak_run - peak_new)
        total_new = total_run * rescale + jnp.sum(weights, axis=3)
        mixed_new = mixed_run * rescale[..., None] + jnp.einsum(
            "gjtk,kgd->gjtd",
            weights.astype(jnp.bfloat16),
            value_piece.reshape(row_count, kv_heads, head_dim),
            preferred_element_type=jnp.float32,
        )
        return (peak_new, total_new, mixed_new)

    start_state = (
        jnp.full((kv_heads, query_group_count, local_rows), floor_value, jnp.float32),
        jnp.zeros((kv_heads, query_group_count, local_rows), jnp.float32),
        jnp.zeros((kv_heads, query_group_count, local_rows, head_dim), jnp.float32),
    )
    dec_heads = dec_query.reshape(request_count, kv_heads, query_group_count, head_dim)
    request_ids = jnp.arange(request_count, dtype=jnp.int32)
    cache_both = gather_ctx(
        jnp.concatenate([local_keys, local_values], axis=1), layout, 1
    )
    cache_keys = cache_both[:, :kv_width]
    cache_values = cache_both[:, kv_width:]
    total_rows = cache_keys.shape[0]
    step_rows = total_rows
    cache_pos = (
        block_map[:, None] * block_rows + jnp.arange(block_rows, dtype=jnp.int32)[None, :]
    ).reshape(total_rows)
    cache_request = request_index(cache_pos, request_ends)

    def key_step(running, step_index):
        first_row = step_index * step_rows
        pieces = (
            lax.dynamic_slice_in_dim(cache_keys, first_row, step_rows, 0),
            lax.dynamic_slice_in_dim(cache_values, first_row, step_rows, 0),
        )
        return (attend(running, pieces, first_row), None)

    final_state, unused = lax.scan(
        key_step, start_state, jnp.arange(total_rows // step_rows, dtype=jnp.int32)
    )
    peak_run, total_run, mixed_run = final_state
    owned = (cache_request[None, :] == request_ids[:, None])[:, None, None, :]
    cache_peak, cache_total, cache_mixed = softmax_parts(
        dec_heads, cache_keys, cache_values, owned, kv_heads, head_dim, score_scale
    )
    attended = (
        (mixed_run / total_run[..., None]).transpose(2, 0, 1, 3).reshape(local_rows, query_width)
    )
    attended = attended.astype(jnp.bfloat16)
    own_keys = decode_key_rows.reshape(request_count, kv_heads, 1, head_dim).astype(jnp.float32)
    own_values = decode_value_rows.reshape(request_count, kv_heads, 1, head_dim).astype(jnp.float32)
    self_scores = jnp.sum(dec_heads.astype(jnp.float32) * own_keys, axis=3) * score_scale
    peak_all = jnp.maximum(cache_peak, self_scores)
    rescale = jnp.exp(cache_peak - peak_all)
    self_weights = jnp.exp(self_scores - peak_all)
    dec_total = cache_total * rescale + self_weights
    dec_mixed = (
        cache_mixed * rescale[..., None] + round_weights(self_weights)[..., None] * own_values
    )
    dec_attn = (
        (dec_mixed / dec_total[..., None]).reshape(request_count, query_width).astype(jnp.bfloat16)
    )
    attended_all = jnp.concatenate([attended, dec_attn], axis=0)
    projected = lax.dot_general(
        attended_all,
        out_weight_t,
        (((1,), (1,)), ((), ())),
        preferred_element_type=jnp.float32,
    )
    summed_rows = scatter_sum_tp(projected.astype(jnp.bfloat16), tp_count, 2)
    summed_rows = summed_rows.astype(jnp.bfloat16)
    return (summed_rows[:local_rows], summed_rows[local_rows:])


def solution(mesh):
    return jax.shard_map(
        functools.partial(on_device, ctx_layout(mesh), mesh.shape["tp"]),
        mesh=mesh,
        in_specs=(
            P("ctx", None),
            P(),
            P("ctx", "tp"),
            P("ctx", "tp"),
            P("ctx", "tp"),
            P("tp", "ctx"),
            P(),
            P(),
        ),
        out_specs=(P("ctx", "tp"), P(None, "tp")),
        check_vma=False,
    )
```

```python
import functools
import math

import jax
import jax.numpy as jnp
import numpy as np
from jax import lax
from jax.experimental import pallas as pl
from jax.experimental.pallas import tpu as pltpu
from jax.sharding import PartitionSpec as P

HEAD_SIZE = 128


floor_value = -1e30


def _gather_kernel(
    z_count,
    p_count,
    first_ref,
    second_ref,
    first_out,
    second_out,
    first_z,
    first_p,
    second_p,
    second_z,
    local_sems,
):
    me = lax.axis_index("ctx")
    z_me = me // p_count
    p_me = lax.rem(me, p_count)
    mesh_ids = pl.DeviceIdType.MESH
    barrier = pltpu.get_barrier_semaphore()

    def z_peer(step):
        return lax.rem(z_me + step, z_count)

    def p_peer(step):
        return lax.rem(p_me + step, p_count)

    def z_target(peer):
        return peer * p_count + p_me

    def p_target(peer):
        return z_me * p_count + peer

    def greet(peer_of, target_of):
        def body(step, carry):
            pl.semaphore_signal(
                barrier, 1, device_id={"ctx": target_of(peer_of(step))}, device_id_type=mesh_ids
            )
            return carry

        return body

    lax.fori_loop(1, z_count, greet(z_peer, z_target), 0)
    lax.fori_loop(1, p_count, greet(p_peer, p_target), 0)
    pl.semaphore_wait(barrier, z_count + p_count - 2)

    def remote(src, dst, send_sem, recv_sem, target):
        return pltpu.make_async_remote_copy(
            src_ref=src,
            dst_ref=dst,
            send_sem=send_sem,
            recv_sem=recv_sem,
            device_id={"ctx": target},
            device_id_type=mesh_ids,
        )

    def first_one(peer, slot):
        return remote(
            first_ref, first_out.at[slot, p_me], first_z[0].at[peer], first_z[1].at[slot],
            z_target(peer),
        )

    def second_one(peer, slot):
        return remote(
            second_ref, second_out.at[z_me, slot], second_p[0].at[peer], second_p[1].at[slot],
            p_target(peer),
        )

    def first_two(peer, row, slot):
        return remote(
            first_out.at[slot, row], first_out.at[slot, row], first_p[0].at[peer],
            first_p[1].at[row], p_target(peer),
        )

    def second_two(peer, row, slot):
        return remote(
            second_out.at[row, slot], second_out.at[row, slot], second_z[0].at[peer],
            second_z[1].at[row], z_target(peer),
        )

    def first_rows(peer, row):
        return remote(
            first_out.at[:, row], first_out.at[:, row], first_p[0].at[peer], first_p[1].at[row],
            p_target(peer),
        )

    def second_rows(peer, row):
        return remote(
            second_out.at[row], second_out.at[row], second_z[0].at[peer], second_z[1].at[row],
            z_target(peer),
        )

    first_own = pltpu.make_async_copy(first_ref, first_out.at[z_me, p_me], local_sems.at[0])
    second_own = pltpu.make_async_copy(second_ref, second_out.at[z_me, p_me], local_sems.at[1])
    first_own.start()
    second_own.start()

    def start_one(step, carry):
        @pl.when(step < z_count)
        def _():
            first_one(z_peer(step), z_me).start()

        @pl.when(step < p_count)
        def _():
            second_one(p_peer(step), p_me).start()

        return carry

    rounds = max(z_count, p_count)
    lax.fori_loop(1, rounds, start_one, 0)

    def forward_first(slot):
        def body(step, carry):
            first_two(p_peer(step), p_me, slot).start()
            return carry

        lax.fori_loop(1, p_count, body, 0)

    def forward_second(slot):
        def body(step, carry):
            second_two(z_peer(step), z_me, slot).start()
            return carry

        lax.fori_loop(1, z_count, body, 0)

    first_own.wait()
    forward_first(z_me)
    second_own.wait()
    forward_second(p_me)

    def relay(step, carry):
        @pl.when(step < z_count)
        def _():
            slot = z_peer(step)
            first_one(slot, slot).wait_recv()
            forward_first(slot)

        @pl.when(step < p_count)
        def _():
            slot = p_peer(step)
            second_one(slot, slot).wait_recv()
            forward_second(slot)

        return carry

    lax.fori_loop(1, rounds, relay, 0)

    def drain(step, carry):
        @pl.when(step < z_count)
        def _():
            peer = z_peer(step)
            first_one(peer, z_me).wait_send()
            second_rows(peer, z_me).wait_send()
            second_rows(peer, peer).wait_recv()

        @pl.when(step < p_count)
        def _():
            peer = p_peer(step)
            second_one(peer, p_me).wait_send()
            first_rows(peer, p_me).wait_send()
            first_rows(peer, peer).wait_recv()

        return carry

    lax.fori_loop(1, rounds, drain, 0)


def gather_ctx(piece, layout, kernel_id, parts=False):
    z_count, p_count = layout
    rows, cols = piece.shape
    lane = 128
    by_columns = cols % (3 * lane) == 0
    if by_columns:
        head = 2 * cols // 3
        shapes = ((rows, head), (rows, cols - head))
        pieces = (piece[:, :head], piece[:, head:])
    else:
        tile = 16
        head = min(rows - tile, max(tile, round(rows * 2 / (3 * tile)) * tile))
        shapes = ((head, cols), (rows - head, cols))
        pieces = (piece[:head], piece[head:])
    dma_pairs = [
        pltpu.SemaphoreType.DMA((z_count,)),
        pltpu.SemaphoreType.DMA((z_count,)),
        pltpu.SemaphoreType.DMA((p_count,)),
        pltpu.SemaphoreType.DMA((p_count,)),
    ]

    def kernel(first_ref, second_ref, first_out, second_out, *sems):
        _gather_kernel(
            z_count, p_count, first_ref, second_ref, first_out, second_out,
            (sems[0], sems[1]), (sems[2], sems[3]), (sems[4], sems[5]), (sems[6], sems[7]),
            sems[8],
        )

    first, second = pl.pallas_call(
        kernel,
        out_shape=(
            jax.ShapeDtypeStruct((z_count, p_count) + shapes[0], piece.dtype),
            jax.ShapeDtypeStruct((z_count, p_count) + shapes[1], piece.dtype),
        ),
        in_specs=[pl.BlockSpec(memory_space=pl.ANY)] * 2,
        out_specs=(pl.BlockSpec(memory_space=pl.ANY),) * 2,
        scratch_shapes=dma_pairs + [dma_pairs[2], dma_pairs[3], dma_pairs[0], dma_pairs[1]]
        + [pltpu.SemaphoreType.DMA((2,))],
        compiler_params=pltpu.CompilerParams(collective_id=kernel_id, has_side_effects=True),
    )(*pieces)
    if parts:
        return first, second
    joined = jnp.concatenate([first, second], axis=3 if by_columns else 2)
    return joined.reshape(z_count * p_count * rows, cols)


def _scatter_kernel(count, part_ref, out_ref, send_sems, recv_sems, local_sem):
    me = lax.axis_index("tp")
    width = out_ref.shape[2]
    mesh_ids = pl.DeviceIdType.MESH
    barrier = pltpu.get_barrier_semaphore()

    def greet(step, carry):
        peer = lax.rem(me + step, count)
        pl.semaphore_signal(barrier, 1, device_id={"tp": peer}, device_id_type=mesh_ids)
        return carry

    lax.fori_loop(1, count, greet, 0)
    pl.semaphore_wait(barrier, count - 1)

    def columns(index):
        return pl.ds(pl.multiple_of(index * width, width), width)

    own = pltpu.make_async_copy(part_ref.at[:, columns(me)], out_ref.at[me], local_sem)
    own.start()

    def remote(peer, slot):
        return pltpu.make_async_remote_copy(
            src_ref=part_ref.at[:, columns(peer)],
            dst_ref=out_ref.at[slot],
            send_sem=send_sems.at[peer],
            recv_sem=recv_sems.at[slot],
            device_id={"tp": peer},
            device_id_type=mesh_ids,
        )

    def send(step, carry):
        remote(lax.rem(me + step, count), me).start()
        return carry

    def finish(step, carry):
        peer = lax.rem(me + step, count)
        remote(peer, me).wait_send()
        remote(peer, peer).wait_recv()
        return carry

    lax.fori_loop(1, count, send, 0)
    lax.fori_loop(1, count, finish, 0)
    own.wait()


def scatter_sum_tp(part, count, kernel_id):
    rows, cols = part.shape
    pieces = pl.pallas_call(
        functools.partial(_scatter_kernel, count),
        out_shape=jax.ShapeDtypeStruct((count, rows, cols // count), part.dtype),
        in_specs=[pl.BlockSpec(memory_space=pl.ANY)],
        out_specs=pl.BlockSpec(memory_space=pl.ANY),
        scratch_shapes=[
            pltpu.SemaphoreType.DMA((count,)),
            pltpu.SemaphoreType.DMA((count,)),
            pltpu.SemaphoreType.DMA(()),
        ],
        compiler_params=pltpu.CompilerParams(collective_id=kernel_id, has_side_effects=True),
    )(part)
    return jnp.sum(pieces.astype(jnp.float32), axis=0)


def ctx_layout(mesh):
    count = mesh.shape["ctx"]
    column = mesh.devices.transpose(
        mesh.axis_names.index("ctx"), mesh.axis_names.index("tp")
    )[:, 0]
    try:
        planes = [device.coords[2] for device in column]
    except (AttributeError, IndexError, TypeError):
        return (count, 1)
    p_count = 1
    while p_count < count and planes[p_count] == planes[0]:
        p_count += 1
    if count % p_count:
        return (count, 1)
    for index in range(count):
        if planes[index] != planes[(index // p_count) * p_count]:
            return (count, 1)
    return (count // p_count, p_count)


def initial_positions(block_map, first_row, row_count, block_rows):
    row_ids = first_row + jnp.arange(row_count, dtype=jnp.int32)
    block_ids = row_ids // block_rows
    table_ids = jnp.arange(block_map.shape[0], dtype=jnp.int32)
    mapped = jnp.sum(
        jnp.where(block_ids[:, None] == table_ids[None, :], block_map[None, :], 0), axis=1
    )
    return mapped * block_rows + row_ids % block_rows


def request_index(positions, request_ends):
    return jnp.sum((positions[:, None] >= request_ends[None, :]).astype(jnp.int32), axis=1)


def round_weights(weights):
    rounded = weights.astype(jnp.bfloat16)
    rounded = lax.optimization_barrier(rounded)
    return rounded.astype(jnp.float32)


def softmax_parts(
    dec_heads, projected_key_rows, projected_value_rows, owned, kv_heads, head_dim, score_scale
):
    row_count = projected_key_rows.shape[0]
    scores = (
        jnp.einsum(
            "rgjd,tgd->rgjt",
            dec_heads,
            projected_key_rows.reshape(row_count, kv_heads, head_dim),
            preferred_element_type=jnp.float32,
        )
        * score_scale
    )
    scores = jnp.where(owned, scores, floor_value)
    part_peak = jnp.max(scores, axis=3)
    weights = jnp.where(owned, jnp.exp(scores - part_peak[..., None]), 0.0)
    part_total = jnp.sum(weights, axis=3)
    part_mixed = jnp.einsum(
        "rgjt,tgd->rgjd",
        weights.astype(jnp.bfloat16),
        projected_value_rows.reshape(row_count, kv_heads, head_dim),
        preferred_element_type=jnp.float32,
    )
    return (part_peak, part_total, part_mixed)


def on_device(
    layout, tp_count, tokens, new_token_states, w_query, key_matrix, value_matrix, w_out, lengths, block_map
):
    local_rows = tokens.shape[0]
    block_rows = local_rows // 2
    request_count = new_token_states.shape[0]
    head_dim = HEAD_SIZE
    query_width = w_query.shape[1]
    kv_width = key_matrix.shape[1]
    kv_heads = kv_width // head_dim
    query_group_count = query_width // kv_width
    score_scale = 1.0 / math.sqrt(head_dim)
    device = lax.axis_index("ctx")
    request_ends = jnp.cumsum(lengths)
    inputs = jnp.concatenate([tokens, new_token_states], axis=0)
    z_count, p_count = layout
    model_width = inputs.shape[1]
    qkv_width = query_width + 2 * kv_width
    if (qkv_width + w_out.shape[0]) % 384 == 0 and 2 * w_out.shape[0] == qkv_width:
        qkv_rows, out_rows = gather_ctx(
            jnp.concatenate([w_query, key_matrix, value_matrix, w_out.T], axis=1),
            layout,
            0,
            parts=True,
        )
        projected_all = jnp.dot(
            inputs,
            qkv_rows.reshape(model_width, qkv_width),
            preferred_element_type=jnp.float32,
        ).astype(jnp.bfloat16)
        out_weight_t = out_rows.reshape(model_width, w_out.shape[0])
    else:
        joined = gather_ctx(
            jnp.concatenate([w_query, key_matrix, value_matrix, w_out.T], axis=1), layout, 0
        )
        projected_all = jnp.dot(
            inputs, joined[:, :qkv_width], preferred_element_type=jnp.float32
        ).astype(jnp.bfloat16)
        out_weight_t = joined[:, qkv_width:]
    query_all = projected_all[:, :query_width]
    key_all = projected_all[:, query_width : query_width + kv_width]
    value_all = projected_all[:, query_width + kv_width :]
    local_query = query_all[:local_rows]
    local_keys = key_all[:local_rows]
    local_values = value_all[:local_rows]
    dec_query = query_all[local_rows:]
    decode_key_rows = key_all[local_rows:]
    decode_value_rows = value_all[local_rows:]
    token_pos = initial_positions(block_map, device * local_rows, local_rows, block_rows)
    token_request = request_index(token_pos, request_ends)
    query_heads = local_query.reshape(local_rows, kv_heads, query_group_count, head_dim)

    def attend(running, shard_pieces, key_pos, key_request):
        peak_run, total_run, mixed_run = running
        key_piece, value_piece = shard_pieces
        row_count = key_piece.shape[0]
        allowed = (key_request[None, :] == token_request[:, None]) & (
            key_pos[None, :] <= token_pos[:, None]
        )
        scores = (
            jnp.einsum(
                "tgjd,kgd->gjtk",
                query_heads,
                key_piece.reshape(row_count, kv_heads, head_dim),
                preferred_element_type=jnp.float32,
            )
            * score_scale
        )
        scores = jnp.where(allowed, scores, floor_value)
        peak_new = jnp.maximum(peak_run, jnp.max(scores, axis=3))
        weights = jnp.where(allowed, jnp.exp(scores - peak_new[..., None]), 0.0)
        rescale = jnp.exp(peak_run - peak_new)
        total_new = total_run * rescale + jnp.sum(weights, axis=3)
        mixed_new = mixed_run * rescale[..., None] + jnp.einsum(
            "gjtk,kgd->gjtd",
            weights.astype(jnp.bfloat16),
            value_piece.reshape(row_count, kv_heads, head_dim),
            preferred_element_type=jnp.float32,
        )
        return (peak_new, total_new, mixed_new)

    start_state = (
        jnp.full((kv_heads, query_group_count, local_rows), floor_value, jnp.float32),
        jnp.zeros((kv_heads, query_group_count, local_rows), jnp.float32),
        jnp.zeros((kv_heads, query_group_count, local_rows, head_dim), jnp.float32),
    )
    dec_heads = dec_query.reshape(request_count, kv_heads, query_group_count, head_dim)
    request_ids = jnp.arange(request_count, dtype=jnp.int32)
    kv_sets = gather_ctx(
        jnp.concatenate([local_keys, local_values], axis=1), layout, 1, parts=True
    )
    block_count = z_count * p_count
    offsets = (0, kv_sets[0].shape[2])
    key_sets = []
    for part, offset in zip(kv_sets, offsets):
        part_rows = part.shape[2]
        flat = part.reshape(block_count * part_rows, 2 * kv_width)
        row_ids = (
            np.arange(block_count, dtype=np.int32)[:, None] * local_rows
            + offset
            + np.arange(part_rows, dtype=np.int32)[None, :]
        ).reshape(-1)
        part_pos = jnp.take(block_map, row_ids // block_rows) * block_rows + row_ids % block_rows
        key_sets.append(
            (flat[:, :kv_width], flat[:, kv_width:], part_pos, request_index(part_pos, request_ends))
        )
    final_state = start_state
    for set_keys, set_values, set_pos, set_request in key_sets:
        final_state = attend(final_state, (set_keys, set_values), set_pos, set_request)
    peak_run, total_run, mixed_run = final_state
    dec_parts = []
    for set_keys, set_values, set_pos, set_request in key_sets:
        owned = (set_request[None, :] == request_ids[:, None])[:, None, None, :]
        dec_parts.append(
            softmax_parts(dec_heads, set_keys, set_values, owned, kv_heads, head_dim, score_scale)
        )
    cache_peak = jnp.maximum(dec_parts[0][0], dec_parts[1][0])
    cache_total = 0.0
    cache_mixed = 0.0
    for part_peak, part_total, part_mixed in dec_parts:
        part_scale = jnp.exp(part_peak - cache_peak)
        cache_total = cache_total + part_total * part_scale
        cache_mixed = cache_mixed + part_mixed * part_scale[..., None]
    attended = (
        (mixed_run / total_run[..., None]).transpose(2, 0, 1, 3).reshape(local_rows, query_width)
    )
    attended = attended.astype(jnp.bfloat16)
    own_keys = decode_key_rows.reshape(request_count, kv_heads, 1, head_dim).astype(jnp.float32)
    own_values = decode_value_rows.reshape(request_count, kv_heads, 1, head_dim).astype(jnp.float32)
    self_scores = jnp.sum(dec_heads.astype(jnp.float32) * own_keys, axis=3) * score_scale
    peak_all = jnp.maximum(cache_peak, self_scores)
    rescale = jnp.exp(cache_peak - peak_all)
    self_weights = jnp.exp(self_scores - peak_all)
    dec_total = cache_total * rescale + self_weights
    dec_mixed = (
        cache_mixed * rescale[..., None] + round_weights(self_weights)[..., None] * own_values
    )
    dec_attn = (
        (dec_mixed / dec_total[..., None]).reshape(request_count, query_width).astype(jnp.bfloat16)
    )
    attended_all = jnp.concatenate([attended, dec_attn], axis=0)
    projected = lax.dot_general(
        attended_all,
        out_weight_t,
        (((1,), (1,)), ((), ())),
        preferred_element_type=jnp.float32,
    )
    summed_rows = scatter_sum_tp(projected.astype(jnp.bfloat16), tp_count, 2)
    summed_rows = summed_rows.astype(jnp.bfloat16)
    return (summed_rows[:local_rows], summed_rows[local_rows:])


def solution(mesh):
    return jax.shard_map(
        functools.partial(on_device, ctx_layout(mesh), mesh.shape["tp"]),
        mesh=mesh,
        in_specs=(
            P("ctx", None),
            P(),
            P("ctx", "tp"),
            P("ctx", "tp"),
            P("ctx", "tp"),
            P("tp", "ctx"),
            P(),
            P(),
        ),
        out_specs=(P("ctx", "tp"), P(None, "tp")),
        check_vma=False,
    )
```

```python
import functools
import math

import jax
import jax.numpy as jnp
from jax import lax
from jax.experimental import pallas as pl
from jax.experimental.pallas import tpu as pltpu
from jax.sharding import PartitionSpec as P

HEAD_SIZE = 128


floor_value = -1e30


def _gather_kernel(
    z_count,
    p_count,
    first_ref,
    second_ref,
    first_out,
    second_out,
    first_z,
    first_p,
    second_p,
    second_z,
    local_sems,
):
    me = lax.axis_index("ctx")
    z_me = me // p_count
    p_me = lax.rem(me, p_count)
    mesh_ids = pl.DeviceIdType.MESH
    barrier = pltpu.get_barrier_semaphore()

    def z_peer(step):
        return lax.rem(z_me + step, z_count)

    def p_peer(step):
        return lax.rem(p_me + step, p_count)

    def z_target(peer):
        return peer * p_count + p_me

    def p_target(peer):
        return z_me * p_count + peer

    def greet(peer_of, target_of):
        def body(step, carry):
            pl.semaphore_signal(
                barrier, 1, device_id={"ctx": target_of(peer_of(step))}, device_id_type=mesh_ids
            )
            return carry

        return body

    lax.fori_loop(1, z_count, greet(z_peer, z_target), 0)
    lax.fori_loop(1, p_count, greet(p_peer, p_target), 0)
    pl.semaphore_wait(barrier, z_count + p_count - 2)

    def remote(src, dst, send_sem, recv_sem, target):
        return pltpu.make_async_remote_copy(
            src_ref=src,
            dst_ref=dst,
            send_sem=send_sem,
            recv_sem=recv_sem,
            device_id={"ctx": target},
            device_id_type=mesh_ids,
        )

    def first_one(peer, slot):
        return remote(
            first_ref, first_out.at[slot, p_me], first_z[0].at[peer], first_z[1].at[slot],
            z_target(peer),
        )

    def second_one(peer, slot):
        return remote(
            second_ref, second_out.at[z_me, slot], second_p[0].at[peer], second_p[1].at[slot],
            p_target(peer),
        )

    def first_two(peer, row, slot):
        return remote(
            first_out.at[slot, row], first_out.at[slot, row], first_p[0].at[peer],
            first_p[1].at[row], p_target(peer),
        )

    def second_two(peer, row, slot):
        return remote(
            second_out.at[row, slot], second_out.at[row, slot], second_z[0].at[peer],
            second_z[1].at[row], z_target(peer),
        )

    def first_rows(peer, row):
        return remote(
            first_out.at[:, row], first_out.at[:, row], first_p[0].at[peer], first_p[1].at[row],
            p_target(peer),
        )

    def second_rows(peer, row):
        return remote(
            second_out.at[row], second_out.at[row], second_z[0].at[peer], second_z[1].at[row],
            z_target(peer),
        )

    first_own = pltpu.make_async_copy(first_ref, first_out.at[z_me, p_me], local_sems.at[0])
    second_own = pltpu.make_async_copy(second_ref, second_out.at[z_me, p_me], local_sems.at[1])
    first_own.start()
    second_own.start()

    def start_one(step, carry):
        @pl.when(step < z_count)
        def _():
            first_one(z_peer(step), z_me).start()

        @pl.when(step < p_count)
        def _():
            second_one(p_peer(step), p_me).start()

        return carry

    rounds = max(z_count, p_count)
    lax.fori_loop(1, rounds, start_one, 0)

    def forward_first(slot):
        def body(step, carry):
            first_two(p_peer(step), p_me, slot).start()
            return carry

        lax.fori_loop(1, p_count, body, 0)

    def forward_second(slot):
        def body(step, carry):
            second_two(z_peer(step), z_me, slot).start()
            return carry

        lax.fori_loop(1, z_count, body, 0)

    first_own.wait()
    forward_first(z_me)
    second_own.wait()
    forward_second(p_me)

    def relay(step, carry):
        @pl.when(step < z_count)
        def _():
            slot = z_peer(step)
            first_one(slot, slot).wait_recv()
            forward_first(slot)

        @pl.when(step < p_count)
        def _():
            slot = p_peer(step)
            second_one(slot, slot).wait_recv()
            forward_second(slot)

        return carry

    lax.fori_loop(1, rounds, relay, 0)

    def drain(step, carry):
        @pl.when(step < z_count)
        def _():
            peer = z_peer(step)
            first_one(peer, z_me).wait_send()
            second_rows(peer, z_me).wait_send()
            second_rows(peer, peer).wait_recv()

        @pl.when(step < p_count)
        def _():
            peer = p_peer(step)
            second_one(peer, p_me).wait_send()
            first_rows(peer, p_me).wait_send()
            first_rows(peer, peer).wait_recv()

        return carry

    lax.fori_loop(1, rounds, drain, 0)


def gather_ctx(piece, layout, kernel_id, parts=False):
    z_count, p_count = layout
    rows, cols = piece.shape
    lane = 128
    by_columns = cols % (3 * lane) == 0
    if by_columns:
        head = 2 * cols // 3
        shapes = ((rows, head), (rows, cols - head))
        pieces = (piece[:, :head], piece[:, head:])
    else:
        tile = 16
        head = min(rows - tile, max(tile, round(rows * 2 / (3 * tile)) * tile))
        shapes = ((head, cols), (rows - head, cols))
        pieces = (piece[:head], piece[head:])
    dma_pairs = [
        pltpu.SemaphoreType.DMA((z_count,)),
        pltpu.SemaphoreType.DMA((z_count,)),
        pltpu.SemaphoreType.DMA((p_count,)),
        pltpu.SemaphoreType.DMA((p_count,)),
    ]

    def kernel(first_ref, second_ref, first_out, second_out, *sems):
        _gather_kernel(
            z_count, p_count, first_ref, second_ref, first_out, second_out,
            (sems[0], sems[1]), (sems[2], sems[3]), (sems[4], sems[5]), (sems[6], sems[7]),
            sems[8],
        )

    if not by_columns and not parts:
        split_rows = shapes[0][0]

        def owned_kernel(piece_ref, out_ref, *sems):
            kernel(
                piece_ref.at[pl.ds(0, split_rows)],
                piece_ref.at[pl.ds(split_rows, rows - split_rows)],
                out_ref.at[:, :, pl.ds(0, split_rows)],
                out_ref.at[:, :, pl.ds(split_rows, rows - split_rows)],
                *sems,
            )

        whole = pl.pallas_call(
            owned_kernel,
            out_shape=jax.ShapeDtypeStruct((z_count, p_count, rows, cols), piece.dtype),
            in_specs=[pl.BlockSpec(memory_space=pl.ANY)],
            out_specs=pl.BlockSpec(memory_space=pl.ANY),
            scratch_shapes=dma_pairs + [dma_pairs[2], dma_pairs[3], dma_pairs[0], dma_pairs[1]]
            + [pltpu.SemaphoreType.DMA((2,))],
            compiler_params=pltpu.CompilerParams(collective_id=kernel_id, has_side_effects=True),
        )(piece)
        return whole.reshape(z_count * p_count * rows, cols)
    first, second = pl.pallas_call(
        kernel,
        out_shape=(
            jax.ShapeDtypeStruct((z_count, p_count) + shapes[0], piece.dtype),
            jax.ShapeDtypeStruct((z_count, p_count) + shapes[1], piece.dtype),
        ),
        in_specs=[pl.BlockSpec(memory_space=pl.ANY)] * 2,
        out_specs=(pl.BlockSpec(memory_space=pl.ANY),) * 2,
        scratch_shapes=dma_pairs + [dma_pairs[2], dma_pairs[3], dma_pairs[0], dma_pairs[1]]
        + [pltpu.SemaphoreType.DMA((2,))],
        compiler_params=pltpu.CompilerParams(collective_id=kernel_id, has_side_effects=True),
    )(*pieces)
    if parts:
        return first, second
    joined = jnp.concatenate([first, second], axis=3 if by_columns else 2)
    return joined.reshape(z_count * p_count * rows, cols)


def _scatter_kernel(count, part_ref, out_ref, send_sems, recv_sems, local_sem):
    me = lax.axis_index("tp")
    width = out_ref.shape[2]
    mesh_ids = pl.DeviceIdType.MESH
    barrier = pltpu.get_barrier_semaphore()

    def greet(step, carry):
        peer = lax.rem(me + step, count)
        pl.semaphore_signal(barrier, 1, device_id={"tp": peer}, device_id_type=mesh_ids)
        return carry

    lax.fori_loop(1, count, greet, 0)
    pl.semaphore_wait(barrier, count - 1)

    def columns(index):
        return pl.ds(pl.multiple_of(index * width, width), width)

    own = pltpu.make_async_copy(part_ref.at[:, columns(me)], out_ref.at[me], local_sem)
    own.start()

    def remote(peer, slot):
        return pltpu.make_async_remote_copy(
            src_ref=part_ref.at[:, columns(peer)],
            dst_ref=out_ref.at[slot],
            send_sem=send_sems.at[peer],
            recv_sem=recv_sems.at[slot],
            device_id={"tp": peer},
            device_id_type=mesh_ids,
        )

    def send(step, carry):
        remote(lax.rem(me + step, count), me).start()
        return carry

    def finish(step, carry):
        peer = lax.rem(me + step, count)
        remote(peer, me).wait_send()
        remote(peer, peer).wait_recv()
        return carry

    lax.fori_loop(1, count, send, 0)
    lax.fori_loop(1, count, finish, 0)
    own.wait()


def scatter_sum_tp(part, count, kernel_id):
    rows, cols = part.shape
    pieces = pl.pallas_call(
        functools.partial(_scatter_kernel, count),
        out_shape=jax.ShapeDtypeStruct((count, rows, cols // count), part.dtype),
        in_specs=[pl.BlockSpec(memory_space=pl.ANY)],
        out_specs=pl.BlockSpec(memory_space=pl.ANY),
        scratch_shapes=[
            pltpu.SemaphoreType.DMA((count,)),
            pltpu.SemaphoreType.DMA((count,)),
            pltpu.SemaphoreType.DMA(()),
        ],
        compiler_params=pltpu.CompilerParams(collective_id=kernel_id, has_side_effects=True),
    )(part)
    return jnp.sum(pieces.astype(jnp.float32), axis=0)


def ctx_layout(mesh):
    count = mesh.shape["ctx"]
    column = mesh.devices.transpose(
        mesh.axis_names.index("ctx"), mesh.axis_names.index("tp")
    )[:, 0]
    try:
        planes = [device.coords[2] for device in column]
    except (AttributeError, IndexError, TypeError):
        return (count, 1)
    p_count = 1
    while p_count < count and planes[p_count] == planes[0]:
        p_count += 1
    if count % p_count:
        return (count, 1)
    for index in range(count):
        if planes[index] != planes[(index // p_count) * p_count]:
            return (count, 1)
    return (count // p_count, p_count)


def initial_positions(block_map, first_row, row_count, block_rows):
    row_ids = first_row + jnp.arange(row_count, dtype=jnp.int32)
    block_ids = row_ids // block_rows
    table_ids = jnp.arange(block_map.shape[0], dtype=jnp.int32)
    mapped = jnp.sum(
        jnp.where(block_ids[:, None] == table_ids[None, :], block_map[None, :], 0), axis=1
    )
    return mapped * block_rows + row_ids % block_rows


def request_index(positions, request_ends):
    return jnp.sum((positions[:, None] >= request_ends[None, :]).astype(jnp.int32), axis=1)


def round_weights(weights):
    rounded = weights.astype(jnp.bfloat16)
    rounded = lax.optimization_barrier(rounded)
    return rounded.astype(jnp.float32)


def softmax_parts(
    dec_heads, projected_key_rows, projected_value_rows, owned, kv_heads, head_dim, score_scale
):
    row_count = projected_key_rows.shape[0]
    scores = (
        jnp.einsum(
            "rgjd,tgd->rgjt",
            dec_heads,
            projected_key_rows.reshape(row_count, kv_heads, head_dim),
            preferred_element_type=jnp.float32,
        )
        * score_scale
    )
    scores = jnp.where(owned, scores, floor_value)
    part_peak = jnp.max(scores, axis=3)
    weights = jnp.where(owned, jnp.exp(scores - part_peak[..., None]), 0.0)
    part_total = jnp.sum(weights, axis=3)
    part_mixed = jnp.einsum(
        "rgjt,tgd->rgjd",
        weights.astype(jnp.bfloat16),
        projected_value_rows.reshape(row_count, kv_heads, head_dim),
        preferred_element_type=jnp.float32,
    )
    return (part_peak, part_total, part_mixed)


def on_device(
    layout, tp_count, tokens, new_token_states, w_query, key_matrix, value_matrix, w_out, lengths, block_map
):
    local_rows = tokens.shape[0]
    block_rows = local_rows // 2
    request_count = new_token_states.shape[0]
    head_dim = HEAD_SIZE
    query_width = w_query.shape[1]
    kv_width = key_matrix.shape[1]
    kv_heads = kv_width // head_dim
    query_group_count = query_width // kv_width
    score_scale = 1.0 / math.sqrt(head_dim)
    device = lax.axis_index("ctx")
    request_ends = jnp.cumsum(lengths)
    inputs = jnp.concatenate([tokens, new_token_states], axis=0)
    z_count, p_count = layout
    model_width = inputs.shape[1]
    qkv_width = query_width + 2 * kv_width
    if (qkv_width + w_out.shape[0]) % 384 == 0 and 2 * w_out.shape[0] == qkv_width:
        qkv_rows, out_rows = gather_ctx(
            jnp.concatenate([w_query, key_matrix, value_matrix, w_out.T], axis=1),
            layout,
            0,
            parts=True,
        )
        projected_all = jnp.dot(
            inputs,
            qkv_rows.reshape(model_width, qkv_width),
            preferred_element_type=jnp.float32,
        ).astype(jnp.bfloat16)
        out_weight_t = out_rows.reshape(model_width, w_out.shape[0])
    else:
        joined = gather_ctx(
            jnp.concatenate([w_query, key_matrix, value_matrix, w_out.T], axis=1), layout, 0
        )
        projected_all = jnp.dot(
            inputs, joined[:, :qkv_width], preferred_element_type=jnp.float32
        ).astype(jnp.bfloat16)
        out_weight_t = joined[:, qkv_width:]
    query_all = projected_all[:, :query_width]
    key_all = projected_all[:, query_width : query_width + kv_width]
    value_all = projected_all[:, query_width + kv_width :]
    local_query = query_all[:local_rows]
    local_keys = key_all[:local_rows]
    local_values = value_all[:local_rows]
    dec_query = query_all[local_rows:]
    decode_key_rows = key_all[local_rows:]
    decode_value_rows = value_all[local_rows:]
    token_pos = initial_positions(block_map, device * local_rows, local_rows, block_rows)
    token_request = request_index(token_pos, request_ends)
    query_heads = local_query.reshape(local_rows, kv_heads, query_group_count, head_dim)

    def attend(running, shard_pieces, first_row):
        peak_run, total_run, mixed_run = running
        key_piece, value_piece = shard_pieces
        row_count = key_piece.shape[0]
        key_pos = lax.dynamic_slice_in_dim(cache_pos, first_row, row_count, 0)
        key_request = lax.dynamic_slice_in_dim(cache_request, first_row, row_count, 0)
        allowed = (key_request[None, :] == token_request[:, None]) & (
            key_pos[None, :] <= token_pos[:, None]
        )
        scores = (
            jnp.einsum(
                "tgjd,kgd->gjtk",
                query_heads,
                key_piece.reshape(row_count, kv_heads, head_dim),
                preferred_element_type=jnp.float32,
            )
            * score_scale
        )
        scores = jnp.where(allowed, scores, floor_value)
        peak_new = jnp.maximum(peak_run, jnp.max(scores, axis=3))
        weights = jnp.where(allowed, jnp.exp(scores - peak_new[..., None]), 0.0)
        rescale = jnp.exp(peak_run - peak_new)
        total_new = total_run * rescale + jnp.sum(weights, axis=3)
        mixed_new = mixed_run * rescale[..., None] + jnp.einsum(
            "gjtk,kgd->gjtd",
            weights.astype(jnp.bfloat16),
            value_piece.reshape(row_count, kv_heads, head_dim),
            preferred_element_type=jnp.float32,
        )
        return (peak_new, total_new, mixed_new)

    start_state = (
        jnp.full((kv_heads, query_group_count, local_rows), floor_value, jnp.float32),
        jnp.zeros((kv_heads, query_group_count, local_rows), jnp.float32),
        jnp.zeros((kv_heads, query_group_count, local_rows, head_dim), jnp.float32),
    )
    dec_heads = dec_query.reshape(request_count, kv_heads, query_group_count, head_dim)
    request_ids = jnp.arange(request_count, dtype=jnp.int32)
    cache_both = gather_ctx(
        jnp.concatenate([local_keys, local_values], axis=1), layout, 1
    )
    cache_keys = cache_both[:, :kv_width]
    cache_values = cache_both[:, kv_width:]
    total_rows = cache_keys.shape[0]
    step_rows = total_rows
    cache_pos = (
        block_map[:, None] * block_rows + jnp.arange(block_rows, dtype=jnp.int32)[None, :]
    ).reshape(total_rows)
    cache_request = request_index(cache_pos, request_ends)

    def key_step(running, step_index):
        first_row = step_index * step_rows
        pieces = (
            lax.dynamic_slice_in_dim(cache_keys, first_row, step_rows, 0),
            lax.dynamic_slice_in_dim(cache_values, first_row, step_rows, 0),
        )
        return (attend(running, pieces, first_row), None)

    final_state, unused = lax.scan(
        key_step, start_state, jnp.arange(total_rows // step_rows, dtype=jnp.int32)
    )
    peak_run, total_run, mixed_run = final_state
    owned = (cache_request[None, :] == request_ids[:, None])[:, None, None, :]
    cache_peak, cache_total, cache_mixed = softmax_parts(
        dec_heads, cache_keys, cache_values, owned, kv_heads, head_dim, score_scale
    )
    attended = (
        (mixed_run / total_run[..., None]).transpose(2, 0, 1, 3).reshape(local_rows, query_width)
    )
    attended = attended.astype(jnp.bfloat16)
    own_keys = decode_key_rows.reshape(request_count, kv_heads, 1, head_dim).astype(jnp.float32)
    own_values = decode_value_rows.reshape(request_count, kv_heads, 1, head_dim).astype(jnp.float32)
    self_scores = jnp.sum(dec_heads.astype(jnp.float32) * own_keys, axis=3) * score_scale
    peak_all = jnp.maximum(cache_peak, self_scores)
    rescale = jnp.exp(cache_peak - peak_all)
    self_weights = jnp.exp(self_scores - peak_all)
    dec_total = cache_total * rescale + self_weights
    dec_mixed = (
        cache_mixed * rescale[..., None] + round_weights(self_weights)[..., None] * own_values
    )
    dec_attn = (
        (dec_mixed / dec_total[..., None]).reshape(request_count, query_width).astype(jnp.bfloat16)
    )
    attended_all = jnp.concatenate([attended, dec_attn], axis=0)
    projected = lax.dot_general(
        attended_all,
        out_weight_t,
        (((1,), (1,)), ((), ())),
        preferred_element_type=jnp.float32,
    )
    summed_rows = scatter_sum_tp(projected.astype(jnp.bfloat16), tp_count, 2)
    summed_rows = summed_rows.astype(jnp.bfloat16)
    return (summed_rows[:local_rows], summed_rows[local_rows:])


def solution(mesh):
    return jax.shard_map(
        functools.partial(on_device, ctx_layout(mesh), mesh.shape["tp"]),
        mesh=mesh,
        in_specs=(
            P("ctx", None),
            P(),
            P("ctx", "tp"),
            P("ctx", "tp"),
            P("ctx", "tp"),
            P("tp", "ctx"),
            P(),
            P(),
        ),
        out_specs=(P("ctx", "tp"), P(None, "tp")),
        check_vma=False,
    )
```

```python
import functools
import math

import jax
import jax.numpy as jnp
from jax import lax
from jax.experimental import pallas as pl
from jax.experimental.pallas import tpu as pltpu
from jax.sharding import PartitionSpec as P

HEAD_SIZE = 128


floor_value = -1e30


def _gather_kernel(
    z_count,
    p_count,
    first_ref,
    second_ref,
    first_out,
    second_out,
    first_z,
    first_p,
    second_p,
    second_z,
    local_sems,
):
    me = lax.axis_index("ctx")
    z_me = me // p_count
    p_me = lax.rem(me, p_count)
    mesh_ids = pl.DeviceIdType.MESH
    barrier = pltpu.get_barrier_semaphore()

    def z_peer(step):
        return lax.rem(z_me + step, z_count)

    def p_peer(step):
        return lax.rem(p_me + step, p_count)

    def z_target(peer):
        return peer * p_count + p_me

    def p_target(peer):
        return z_me * p_count + peer

    def greet(peer_of, target_of):
        def body(step, carry):
            pl.semaphore_signal(
                barrier, 1, device_id={"ctx": target_of(peer_of(step))}, device_id_type=mesh_ids
            )
            return carry

        return body

    lax.fori_loop(1, z_count, greet(z_peer, z_target), 0)
    lax.fori_loop(1, p_count, greet(p_peer, p_target), 0)
    pl.semaphore_wait(barrier, z_count + p_count - 2)

    def remote(src, dst, send_sem, recv_sem, target):
        return pltpu.make_async_remote_copy(
            src_ref=src,
            dst_ref=dst,
            send_sem=send_sem,
            recv_sem=recv_sem,
            device_id={"ctx": target},
            device_id_type=mesh_ids,
        )

    def first_one(peer, slot):
        return remote(
            first_ref, first_out.at[slot, p_me], first_z[0].at[peer], first_z[1].at[slot],
            z_target(peer),
        )

    def second_one(peer, slot):
        return remote(
            second_ref, second_out.at[z_me, slot], second_p[0].at[peer], second_p[1].at[slot],
            p_target(peer),
        )

    def first_two(peer, row, slot):
        return remote(
            first_out.at[slot, row], first_out.at[slot, row], first_p[0].at[peer],
            first_p[1].at[row], p_target(peer),
        )

    def second_two(peer, row, slot):
        return remote(
            second_out.at[row, slot], second_out.at[row, slot], second_z[0].at[peer],
            second_z[1].at[row], z_target(peer),
        )

    def first_rows(peer, row):
        return remote(
            first_out.at[:, row], first_out.at[:, row], first_p[0].at[peer], first_p[1].at[row],
            p_target(peer),
        )

    def second_rows(peer, row):
        return remote(
            second_out.at[row], second_out.at[row], second_z[0].at[peer], second_z[1].at[row],
            z_target(peer),
        )

    first_own = pltpu.make_async_copy(first_ref, first_out.at[z_me, p_me], local_sems.at[0])
    second_own = pltpu.make_async_copy(second_ref, second_out.at[z_me, p_me], local_sems.at[1])
    first_own.start()
    second_own.start()

    def start_one(step, carry):
        @pl.when(step < z_count)
        def _():
            first_one(z_peer(step), z_me).start()

        @pl.when(step < p_count)
        def _():
            second_one(p_peer(step), p_me).start()

        return carry

    rounds = max(z_count, p_count)
    lax.fori_loop(1, rounds, start_one, 0)

    def forward_first(slot):
        def body(step, carry):
            first_two(p_peer(step), p_me, slot).start()
            return carry

        lax.fori_loop(1, p_count, body, 0)

    def forward_second(slot):
        def body(step, carry):
            second_two(z_peer(step), z_me, slot).start()
            return carry

        lax.fori_loop(1, z_count, body, 0)

    first_own.wait()
    forward_first(z_me)
    second_own.wait()
    forward_second(p_me)

    def relay(step, carry):
        @pl.when(step < z_count)
        def _():
            slot = z_peer(step)
            first_one(slot, slot).wait_recv()
            forward_first(slot)

        @pl.when(step < p_count)
        def _():
            slot = p_peer(step)
            second_one(slot, slot).wait_recv()
            forward_second(slot)

        return carry

    lax.fori_loop(1, rounds, relay, 0)

    def drain(step, carry):
        @pl.when(step < z_count)
        def _():
            peer = z_peer(step)
            first_one(peer, z_me).wait_send()
            second_rows(peer, z_me).wait_send()
            second_rows(peer, peer).wait_recv()

        @pl.when(step < p_count)
        def _():
            peer = p_peer(step)
            second_one(peer, p_me).wait_send()
            first_rows(peer, p_me).wait_send()
            first_rows(peer, peer).wait_recv()

        return carry

    lax.fori_loop(1, rounds, drain, 0)


def gather_ctx(piece, layout, kernel_id, parts=False):
    z_count, p_count = layout
    rows, cols = piece.shape
    lane = 128
    by_columns = cols % (3 * lane) == 0
    if by_columns:
        head = 2 * cols // 3
        shapes = ((rows, head), (rows, cols - head))
        pieces = (piece[:, :head], piece[:, head:])
    else:
        tile = 16
        head = min(rows - tile, max(tile, round(rows * 2 / (3 * tile)) * tile))
        shapes = ((head, cols), (rows - head, cols))
        pieces = (piece[:head], piece[head:])
    dma_pairs = [
        pltpu.SemaphoreType.DMA((z_count,)),
        pltpu.SemaphoreType.DMA((z_count,)),
        pltpu.SemaphoreType.DMA((p_count,)),
        pltpu.SemaphoreType.DMA((p_count,)),
    ]

    def kernel(first_ref, second_ref, first_out, second_out, *sems):
        _gather_kernel(
            z_count, p_count, first_ref, second_ref, first_out, second_out,
            (sems[0], sems[1]), (sems[2], sems[3]), (sems[4], sems[5]), (sems[6], sems[7]),
            sems[8],
        )

    if not by_columns and not parts:
        split_rows = shapes[0][0]

        def owned_kernel(piece_ref, out_ref, *sems):
            kernel(
                piece_ref.at[pl.ds(0, split_rows)],
                piece_ref.at[pl.ds(split_rows, rows - split_rows)],
                out_ref.at[:, :, pl.ds(0, split_rows)],
                out_ref.at[:, :, pl.ds(split_rows, rows - split_rows)],
                *sems,
            )

        whole = pl.pallas_call(
            owned_kernel,
            out_shape=jax.ShapeDtypeStruct((z_count, p_count, rows, cols), piece.dtype),
            in_specs=[pl.BlockSpec(memory_space=pl.ANY)],
            out_specs=pl.BlockSpec(memory_space=pl.ANY),
            scratch_shapes=dma_pairs + [dma_pairs[2], dma_pairs[3], dma_pairs[0], dma_pairs[1]]
            + [pltpu.SemaphoreType.DMA((2,))],
            compiler_params=pltpu.CompilerParams(collective_id=kernel_id, has_side_effects=True),
        )(piece)
        return whole.reshape(z_count * p_count * rows, cols)
    first, second = pl.pallas_call(
        kernel,
        out_shape=(
            jax.ShapeDtypeStruct((z_count, p_count) + shapes[0], piece.dtype),
            jax.ShapeDtypeStruct((z_count, p_count) + shapes[1], piece.dtype),
        ),
        in_specs=[pl.BlockSpec(memory_space=pl.ANY)] * 2,
        out_specs=(pl.BlockSpec(memory_space=pl.ANY),) * 2,
        scratch_shapes=dma_pairs + [dma_pairs[2], dma_pairs[3], dma_pairs[0], dma_pairs[1]]
        + [pltpu.SemaphoreType.DMA((2,))],
        compiler_params=pltpu.CompilerParams(collective_id=kernel_id, has_side_effects=True),
    )(*pieces)
    if parts:
        return first, second
    joined = jnp.concatenate([first, second], axis=3 if by_columns else 2)
    return joined.reshape(z_count * p_count * rows, cols)


def _scatter_kernel(count, part_ref, out_ref, send_sems, recv_sems, local_sem):
    me = lax.axis_index("tp")
    width = out_ref.shape[2]
    mesh_ids = pl.DeviceIdType.MESH
    barrier = pltpu.get_barrier_semaphore()

    def greet(step, carry):
        peer = lax.rem(me + step, count)
        pl.semaphore_signal(barrier, 1, device_id={"tp": peer}, device_id_type=mesh_ids)
        return carry

    lax.fori_loop(1, count, greet, 0)
    pl.semaphore_wait(barrier, count - 1)

    def columns(index):
        return pl.ds(pl.multiple_of(index * width, width), width)

    own = pltpu.make_async_copy(part_ref.at[:, columns(me)], out_ref.at[me], local_sem)
    own.start()

    def remote(peer, slot):
        return pltpu.make_async_remote_copy(
            src_ref=part_ref.at[:, columns(peer)],
            dst_ref=out_ref.at[slot],
            send_sem=send_sems.at[peer],
            recv_sem=recv_sems.at[slot],
            device_id={"tp": peer},
            device_id_type=mesh_ids,
        )

    def send(step, carry):
        remote(lax.rem(me + step, count), me).start()
        return carry

    def finish(step, carry):
        peer = lax.rem(me + step, count)
        remote(peer, me).wait_send()
        remote(peer, peer).wait_recv()
        return carry

    lax.fori_loop(1, count, send, 0)
    lax.fori_loop(1, count, finish, 0)
    own.wait()


def scatter_sum_tp(part, count, kernel_id):
    rows, cols = part.shape
    pieces = pl.pallas_call(
        functools.partial(_scatter_kernel, count),
        out_shape=jax.ShapeDtypeStruct((count, rows, cols // count), part.dtype),
        in_specs=[pl.BlockSpec(memory_space=pl.ANY)],
        out_specs=pl.BlockSpec(memory_space=pl.ANY),
        scratch_shapes=[
            pltpu.SemaphoreType.DMA((count,)),
            pltpu.SemaphoreType.DMA((count,)),
            pltpu.SemaphoreType.DMA(()),
        ],
        compiler_params=pltpu.CompilerParams(collective_id=kernel_id, has_side_effects=True),
    )(part)
    return jnp.sum(pieces.astype(jnp.float32), axis=0)


def ctx_layout(mesh):
    count = mesh.shape["ctx"]
    column = mesh.devices.transpose(
        mesh.axis_names.index("ctx"), mesh.axis_names.index("tp")
    )[:, 0]
    try:
        planes = [device.coords[2] for device in column]
    except (AttributeError, IndexError, TypeError):
        return (count, 1)
    p_count = 1
    while p_count < count and planes[p_count] == planes[0]:
        p_count += 1
    if count % p_count:
        return (count, 1)
    for index in range(count):
        if planes[index] != planes[(index // p_count) * p_count]:
            return (count, 1)
    return (count // p_count, p_count)


def initial_positions(block_map, first_row, row_count, block_rows):
    row_ids = first_row + jnp.arange(row_count, dtype=jnp.int32)
    block_ids = row_ids // block_rows
    table_ids = jnp.arange(block_map.shape[0], dtype=jnp.int32)
    mapped = jnp.sum(
        jnp.where(block_ids[:, None] == table_ids[None, :], block_map[None, :], 0), axis=1
    )
    return mapped * block_rows + row_ids % block_rows


def request_index(positions, request_ends):
    return jnp.sum((positions[:, None] >= request_ends[None, :]).astype(jnp.int32), axis=1)


def round_weights(weights):
    rounded = weights.astype(jnp.bfloat16)
    rounded = lax.optimization_barrier(rounded)
    return rounded.astype(jnp.float32)


def softmax_parts(
    dec_heads, projected_key_rows, projected_value_rows, owned, kv_heads, head_dim, score_scale
):
    row_count = projected_key_rows.shape[0]
    scores = (
        jnp.einsum(
            "rgjd,tgd->rgjt",
            dec_heads,
            projected_key_rows.reshape(row_count, kv_heads, head_dim),
            preferred_element_type=jnp.float32,
        )
        * score_scale
    )
    scores = jnp.where(owned, scores, floor_value)
    part_peak = jnp.max(scores, axis=3)
    weights = jnp.where(owned, jnp.exp(scores - part_peak[..., None]), 0.0)
    part_total = jnp.sum(weights, axis=3)
    part_mixed = jnp.einsum(
        "rgjt,tgd->rgjd",
        weights.astype(jnp.bfloat16),
        projected_value_rows.reshape(row_count, kv_heads, head_dim),
        preferred_element_type=jnp.float32,
    )
    return (part_peak, part_total, part_mixed)


def on_device(
    layout, tp_count, tokens, new_token_states, w_query, key_matrix, value_matrix, w_out, lengths, block_map
):
    local_rows = tokens.shape[0]
    block_rows = local_rows // 2
    request_count = new_token_states.shape[0]
    head_dim = HEAD_SIZE
    query_width = w_query.shape[1]
    kv_width = key_matrix.shape[1]
    kv_heads = kv_width // head_dim
    query_group_count = query_width // kv_width
    score_scale = 1.0 / math.sqrt(head_dim)
    device = lax.axis_index("ctx")
    request_ends = jnp.cumsum(lengths)
    inputs = jnp.concatenate([tokens, new_token_states], axis=0)
    z_count, p_count = layout
    model_width = inputs.shape[1]
    qkv_width = query_width + 2 * kv_width
    if (qkv_width + w_out.shape[0]) % 384 == 0 and 2 * w_out.shape[0] == qkv_width:
        qkv_rows, out_rows = gather_ctx(
            jnp.concatenate([w_query, key_matrix, value_matrix, w_out.T], axis=1),
            layout,
            0,
            parts=True,
        )
        projected_all = jnp.dot(
            inputs,
            qkv_rows.reshape(model_width, qkv_width),
            preferred_element_type=jnp.float32,
        ).astype(jnp.bfloat16)
        out_weight_t = out_rows.reshape(model_width, w_out.shape[0])
    else:
        joined = gather_ctx(
            jnp.concatenate([w_query, key_matrix, value_matrix, w_out.T], axis=1), layout, 0
        )
        projected_all = jnp.dot(
            inputs, joined[:, :qkv_width], preferred_element_type=jnp.float32
        ).astype(jnp.bfloat16)
        out_weight_t = joined[:, qkv_width:]
    query_all = projected_all[:, :query_width]
    key_all = projected_all[:, query_width : query_width + kv_width]
    value_all = projected_all[:, query_width + kv_width :]
    local_query = query_all[:local_rows]
    local_keys = key_all[:local_rows]
    local_values = value_all[:local_rows]
    dec_query = query_all[local_rows:]
    decode_key_rows = key_all[local_rows:]
    decode_value_rows = value_all[local_rows:]
    token_pos = initial_positions(block_map, device * local_rows, local_rows, block_rows)
    token_request = request_index(token_pos, request_ends)
    query_heads = local_query.reshape(local_rows, kv_heads, query_group_count, head_dim)

    def attend(running, shard_pieces, first_row):
        peak_run, total_run, mixed_run = running
        key_piece, value_piece = shard_pieces
        row_count = key_piece.shape[0]
        key_pos = lax.dynamic_slice_in_dim(cache_pos, first_row, row_count, 0)
        key_request = lax.dynamic_slice_in_dim(cache_request, first_row, row_count, 0)
        allowed = (key_request[None, :] == token_request[:, None]) & (
            key_pos[None, :] <= token_pos[:, None]
        )
        scores = (
            jnp.einsum(
                "tgjd,kgd->gjtk",
                query_heads,
                key_piece.reshape(row_count, kv_heads, head_dim),
                preferred_element_type=jnp.float32,
            )
            * score_scale
        )
        scores = jnp.where(allowed, scores, floor_value)
        peak_new = jnp.maximum(peak_run, jnp.max(scores, axis=3))
        weights = jnp.exp(scores - peak_new[..., None])
        rescale = jnp.exp(peak_run - peak_new)
        total_new = total_run * rescale + jnp.sum(weights, axis=3)
        mixed_new = mixed_run * rescale[..., None] + jnp.einsum(
            "gjtk,kgd->gjtd",
            weights.astype(jnp.bfloat16),
            value_piece.reshape(row_count, kv_heads, head_dim),
            preferred_element_type=jnp.float32,
        )
        return (peak_new, total_new, mixed_new)

    start_state = (
        jnp.full((kv_heads, query_group_count, local_rows), floor_value, jnp.float32),
        jnp.zeros((kv_heads, query_group_count, local_rows), jnp.float32),
        jnp.zeros((kv_heads, query_group_count, local_rows, head_dim), jnp.float32),
    )
    dec_heads = dec_query.reshape(request_count, kv_heads, query_group_count, head_dim)
    request_ids = jnp.arange(request_count, dtype=jnp.int32)
    cache_both = gather_ctx(
        jnp.concatenate([local_keys, local_values], axis=1), layout, 1
    )
    cache_keys = cache_both[:, :kv_width]
    cache_values = cache_both[:, kv_width:]
    total_rows = cache_keys.shape[0]
    step_rows = total_rows
    cache_pos = (
        block_map[:, None] * block_rows + jnp.arange(block_rows, dtype=jnp.int32)[None, :]
    ).reshape(total_rows)
    cache_request = request_index(cache_pos, request_ends)

    def key_step(running, step_index):
        first_row = step_index * step_rows
        pieces = (
            lax.dynamic_slice_in_dim(cache_keys, first_row, step_rows, 0),
            lax.dynamic_slice_in_dim(cache_values, first_row, step_rows, 0),
        )
        return (attend(running, pieces, first_row), None)

    final_state, unused = lax.scan(
        key_step, start_state, jnp.arange(total_rows // step_rows, dtype=jnp.int32)
    )
    peak_run, total_run, mixed_run = final_state
    owned = (cache_request[None, :] == request_ids[:, None])[:, None, None, :]
    cache_peak, cache_total, cache_mixed = softmax_parts(
        dec_heads, cache_keys, cache_values, owned, kv_heads, head_dim, score_scale
    )
    attended = (
        (mixed_run / total_run[..., None]).transpose(2, 0, 1, 3).reshape(local_rows, query_width)
    )
    attended = attended.astype(jnp.bfloat16)
    own_keys = decode_key_rows.reshape(request_count, kv_heads, 1, head_dim).astype(jnp.float32)
    own_values = decode_value_rows.reshape(request_count, kv_heads, 1, head_dim).astype(jnp.float32)
    self_scores = jnp.sum(dec_heads.astype(jnp.float32) * own_keys, axis=3) * score_scale
    peak_all = jnp.maximum(cache_peak, self_scores)
    rescale = jnp.exp(cache_peak - peak_all)
    self_weights = jnp.exp(self_scores - peak_all)
    dec_total = cache_total * rescale + self_weights
    dec_mixed = (
        cache_mixed * rescale[..., None] + round_weights(self_weights)[..., None] * own_values
    )
    dec_attn = (
        (dec_mixed / dec_total[..., None]).reshape(request_count, query_width).astype(jnp.bfloat16)
    )
    attended_all = jnp.concatenate([attended, dec_attn], axis=0)
    projected = lax.dot_general(
        attended_all,
        out_weight_t,
        (((1,), (1,)), ((), ())),
        preferred_element_type=jnp.float32,
    )
    summed_rows = scatter_sum_tp(projected.astype(jnp.bfloat16), tp_count, 2)
    summed_rows = summed_rows.astype(jnp.bfloat16)
    return (summed_rows[:local_rows], summed_rows[local_rows:])


def solution(mesh):
    return jax.shard_map(
        functools.partial(on_device, ctx_layout(mesh), mesh.shape["tp"]),
        mesh=mesh,
        in_specs=(
            P("ctx", None),
            P(),
            P("ctx", "tp"),
            P("ctx", "tp"),
            P("ctx", "tp"),
            P("tp", "ctx"),
            P(),
            P(),
        ),
        out_specs=(P("ctx", "tp"), P(None, "tp")),
        check_vma=False,
    )
```

```python
import functools
import math

import jax
import jax.numpy as jnp
from jax import lax
from jax.experimental import pallas as pl
from jax.experimental.pallas import tpu as pltpu
from jax.sharding import PartitionSpec as P

HEAD_SIZE = 128


floor_value = -1e30


def _gather_kernel(
    z_count,
    p_count,
    first_ref,
    second_ref,
    first_out,
    second_out,
    first_z,
    first_p,
    second_p,
    second_z,
    local_sems,
):
    me = lax.axis_index("ctx")
    z_me = me // p_count
    p_me = lax.rem(me, p_count)
    mesh_ids = pl.DeviceIdType.MESH
    barrier = pltpu.get_barrier_semaphore()

    def z_peer(step):
        return lax.rem(z_me + step, z_count)

    def p_peer(step):
        return lax.rem(p_me + step, p_count)

    def z_target(peer):
        return peer * p_count + p_me

    def p_target(peer):
        return z_me * p_count + peer

    def greet(peer_of, target_of):
        def body(step, carry):
            pl.semaphore_signal(
                barrier, 1, device_id={"ctx": target_of(peer_of(step))}, device_id_type=mesh_ids
            )
            return carry

        return body

    lax.fori_loop(1, z_count, greet(z_peer, z_target), 0)
    lax.fori_loop(1, p_count, greet(p_peer, p_target), 0)
    pl.semaphore_wait(barrier, z_count + p_count - 2)

    def remote(src, dst, send_sem, recv_sem, target):
        return pltpu.make_async_remote_copy(
            src_ref=src,
            dst_ref=dst,
            send_sem=send_sem,
            recv_sem=recv_sem,
            device_id={"ctx": target},
            device_id_type=mesh_ids,
        )

    def first_one(peer, slot):
        return remote(
            first_ref, first_out.at[slot, p_me], first_z[0].at[peer], first_z[1].at[slot],
            z_target(peer),
        )

    def second_one(peer, slot):
        return remote(
            second_ref, second_out.at[z_me, slot], second_p[0].at[peer], second_p[1].at[slot],
            p_target(peer),
        )

    def first_two(peer, row, slot):
        return remote(
            first_out.at[slot, row], first_out.at[slot, row], first_p[0].at[peer],
            first_p[1].at[row], p_target(peer),
        )

    def second_two(peer, row, slot):
        return remote(
            second_out.at[row, slot], second_out.at[row, slot], second_z[0].at[peer],
            second_z[1].at[row], z_target(peer),
        )

    def first_rows(peer, row):
        return remote(
            first_out.at[:, row], first_out.at[:, row], first_p[0].at[peer], first_p[1].at[row],
            p_target(peer),
        )

    def second_rows(peer, row):
        return remote(
            second_out.at[row], second_out.at[row], second_z[0].at[peer], second_z[1].at[row],
            z_target(peer),
        )

    first_own = pltpu.make_async_copy(first_ref, first_out.at[z_me, p_me], local_sems.at[0])
    second_own = pltpu.make_async_copy(second_ref, second_out.at[z_me, p_me], local_sems.at[1])
    first_own.start()
    second_own.start()

    def start_one(step, carry):
        @pl.when(step < z_count)
        def _():
            first_one(z_peer(step), z_me).start()

        @pl.when(step < p_count)
        def _():
            second_one(p_peer(step), p_me).start()

        return carry

    rounds = max(z_count, p_count)
    lax.fori_loop(1, rounds, start_one, 0)

    def forward_first(slot):
        def body(step, carry):
            first_two(p_peer(step), p_me, slot).start()
            return carry

        lax.fori_loop(1, p_count, body, 0)

    def forward_second(slot):
        def body(step, carry):
            second_two(z_peer(step), z_me, slot).start()
            return carry

        lax.fori_loop(1, z_count, body, 0)

    first_own.wait()
    forward_first(z_me)
    second_own.wait()
    forward_second(p_me)

    def relay(step, carry):
        @pl.when(step < z_count)
        def _():
            slot = z_peer(step)
            first_one(slot, slot).wait_recv()
            forward_first(slot)

        @pl.when(step < p_count)
        def _():
            slot = p_peer(step)
            second_one(slot, slot).wait_recv()
            forward_second(slot)

        return carry

    lax.fori_loop(1, rounds, relay, 0)

    def drain(step, carry):
        @pl.when(step < z_count)
        def _():
            peer = z_peer(step)
            first_one(peer, z_me).wait_send()
            second_rows(peer, z_me).wait_send()
            second_rows(peer, peer).wait_recv()

        @pl.when(step < p_count)
        def _():
            peer = p_peer(step)
            second_one(peer, p_me).wait_send()
            first_rows(peer, p_me).wait_send()
            first_rows(peer, peer).wait_recv()

        return carry

    lax.fori_loop(1, rounds, drain, 0)


def gather_ctx(piece, layout, kernel_id, parts=False):
    z_count, p_count = layout
    rows, cols = piece.shape
    lane = 128
    by_columns = cols % (3 * lane) == 0
    if by_columns:
        head = 2 * cols // 3
        shapes = ((rows, head), (rows, cols - head))
        pieces = (piece[:, :head], piece[:, head:])
    else:
        tile = 16
        head = min(rows - tile, max(tile, round(rows * 2 / (3 * tile)) * tile))
        shapes = ((head, cols), (rows - head, cols))
        pieces = (piece[:head], piece[head:])
    dma_pairs = [
        pltpu.SemaphoreType.DMA((z_count,)),
        pltpu.SemaphoreType.DMA((z_count,)),
        pltpu.SemaphoreType.DMA((p_count,)),
        pltpu.SemaphoreType.DMA((p_count,)),
    ]

    def kernel(first_ref, second_ref, first_out, second_out, *sems):
        _gather_kernel(
            z_count, p_count, first_ref, second_ref, first_out, second_out,
            (sems[0], sems[1]), (sems[2], sems[3]), (sems[4], sems[5]), (sems[6], sems[7]),
            sems[8],
        )

    if not by_columns and not parts:
        split_rows = shapes[0][0]

        def owned_kernel(piece_ref, out_ref, *sems):
            kernel(
                piece_ref.at[pl.ds(0, split_rows)],
                piece_ref.at[pl.ds(split_rows, rows - split_rows)],
                out_ref.at[:, :, pl.ds(0, split_rows)],
                out_ref.at[:, :, pl.ds(split_rows, rows - split_rows)],
                *sems,
            )

        whole = pl.pallas_call(
            owned_kernel,
            out_shape=jax.ShapeDtypeStruct((z_count, p_count, rows, cols), piece.dtype),
            in_specs=[pl.BlockSpec(memory_space=pl.ANY)],
            out_specs=pl.BlockSpec(memory_space=pl.ANY),
            scratch_shapes=dma_pairs + [dma_pairs[2], dma_pairs[3], dma_pairs[0], dma_pairs[1]]
            + [pltpu.SemaphoreType.DMA((2,))],
            compiler_params=pltpu.CompilerParams(collective_id=kernel_id, has_side_effects=True),
        )(piece)
        return whole.reshape(z_count * p_count * rows, cols)
    first, second = pl.pallas_call(
        kernel,
        out_shape=(
            jax.ShapeDtypeStruct((z_count, p_count) + shapes[0], piece.dtype),
            jax.ShapeDtypeStruct((z_count, p_count) + shapes[1], piece.dtype),
        ),
        in_specs=[pl.BlockSpec(memory_space=pl.ANY)] * 2,
        out_specs=(pl.BlockSpec(memory_space=pl.ANY),) * 2,
        scratch_shapes=dma_pairs + [dma_pairs[2], dma_pairs[3], dma_pairs[0], dma_pairs[1]]
        + [pltpu.SemaphoreType.DMA((2,))],
        compiler_params=pltpu.CompilerParams(collective_id=kernel_id, has_side_effects=True),
    )(*pieces)
    if parts:
        return first, second
    joined = jnp.concatenate([first, second], axis=3 if by_columns else 2)
    return joined.reshape(z_count * p_count * rows, cols)


def _scatter_kernel(count, part_ref, out_ref, send_sems, recv_sems, local_sem):
    me = lax.axis_index("tp")
    width = out_ref.shape[2]
    mesh_ids = pl.DeviceIdType.MESH
    barrier = pltpu.get_barrier_semaphore()

    def greet(step, carry):
        peer = lax.rem(me + step, count)
        pl.semaphore_signal(barrier, 1, device_id={"tp": peer}, device_id_type=mesh_ids)
        return carry

    lax.fori_loop(1, count, greet, 0)
    pl.semaphore_wait(barrier, count - 1)

    def columns(index):
        return pl.ds(pl.multiple_of(index * width, width), width)

    own = pltpu.make_async_copy(part_ref.at[:, columns(me)], out_ref.at[me], local_sem)
    own.start()

    def remote(peer, slot):
        return pltpu.make_async_remote_copy(
            src_ref=part_ref.at[:, columns(peer)],
            dst_ref=out_ref.at[slot],
            send_sem=send_sems.at[peer],
            recv_sem=recv_sems.at[slot],
            device_id={"tp": peer},
            device_id_type=mesh_ids,
        )

    def send(step, carry):
        remote(lax.rem(me + step, count), me).start()
        return carry

    def finish(step, carry):
        peer = lax.rem(me + step, count)
        remote(peer, me).wait_send()
        remote(peer, peer).wait_recv()
        return carry

    lax.fori_loop(1, count, send, 0)
    lax.fori_loop(1, count, finish, 0)
    own.wait()


def scatter_sum_tp(part, count, kernel_id, split=None):
    rows, cols = part.shape
    pieces = pl.pallas_call(
        functools.partial(_scatter_kernel, count),
        out_shape=jax.ShapeDtypeStruct((count, rows, cols // count), part.dtype),
        in_specs=[pl.BlockSpec(memory_space=pl.ANY)],
        out_specs=pl.BlockSpec(memory_space=pl.ANY),
        scratch_shapes=[
            pltpu.SemaphoreType.DMA((count,)),
            pltpu.SemaphoreType.DMA((count,)),
            pltpu.SemaphoreType.DMA(()),
        ],
        compiler_params=pltpu.CompilerParams(collective_id=kernel_id, has_side_effects=True),
    )(part)
    if split is not None:
        return (
            jnp.sum(pieces[:, :split].astype(jnp.float32), axis=0).astype(part.dtype),
            jnp.sum(pieces[:, split:].astype(jnp.float32), axis=0).astype(part.dtype),
        )
    return jnp.sum(pieces.astype(jnp.float32), axis=0)


def ctx_layout(mesh):
    count = mesh.shape["ctx"]
    column = mesh.devices.transpose(
        mesh.axis_names.index("ctx"), mesh.axis_names.index("tp")
    )[:, 0]
    try:
        planes = [device.coords[2] for device in column]
    except (AttributeError, IndexError, TypeError):
        return (count, 1)
    p_count = 1
    while p_count < count and planes[p_count] == planes[0]:
        p_count += 1
    if count % p_count:
        return (count, 1)
    for index in range(count):
        if planes[index] != planes[(index // p_count) * p_count]:
            return (count, 1)
    return (count // p_count, p_count)


def initial_positions(block_map, first_row, row_count, block_rows):
    row_ids = first_row + jnp.arange(row_count, dtype=jnp.int32)
    block_ids = row_ids // block_rows
    table_ids = jnp.arange(block_map.shape[0], dtype=jnp.int32)
    mapped = jnp.sum(
        jnp.where(block_ids[:, None] == table_ids[None, :], block_map[None, :], 0), axis=1
    )
    return mapped * block_rows + row_ids % block_rows


def request_index(positions, request_ends):
    return jnp.sum((positions[:, None] >= request_ends[None, :]).astype(jnp.int32), axis=1)


def round_weights(weights):
    rounded = weights.astype(jnp.bfloat16)
    rounded = lax.optimization_barrier(rounded)
    return rounded.astype(jnp.float32)


def softmax_parts(
    dec_heads, projected_key_rows, projected_value_rows, owned, kv_heads, head_dim, score_scale
):
    row_count = projected_key_rows.shape[0]
    scores = (
        jnp.einsum(
            "rgjd,tgd->rgjt",
            dec_heads,
            projected_key_rows.reshape(row_count, kv_heads, head_dim),
            preferred_element_type=jnp.float32,
        )
        * score_scale
    )
    scores = jnp.where(owned, scores, floor_value)
    part_peak = jnp.max(scores, axis=3)
    weights = jnp.where(owned, jnp.exp(scores - part_peak[..., None]), 0.0)
    part_total = jnp.sum(weights, axis=3)
    part_mixed = jnp.einsum(
        "rgjt,tgd->rgjd",
        weights.astype(jnp.bfloat16),
        projected_value_rows.reshape(row_count, kv_heads, head_dim),
        preferred_element_type=jnp.float32,
    )
    return (part_peak, part_total, part_mixed)


def on_device(
    layout, tp_count, tokens, new_token_states, w_query, key_matrix, value_matrix, w_out, lengths, block_map
):
    local_rows = tokens.shape[0]
    block_rows = local_rows // 2
    request_count = new_token_states.shape[0]
    head_dim = HEAD_SIZE
    query_width = w_query.shape[1]
    kv_width = key_matrix.shape[1]
    kv_heads = kv_width // head_dim
    query_group_count = query_width // kv_width
    score_scale = 1.0 / math.sqrt(head_dim)
    device = lax.axis_index("ctx")
    request_ends = jnp.cumsum(lengths)
    inputs = jnp.concatenate([tokens, new_token_states], axis=0)
    z_count, p_count = layout
    model_width = inputs.shape[1]
    qkv_width = query_width + 2 * kv_width
    if (qkv_width + w_out.shape[0]) % 384 == 0 and 2 * w_out.shape[0] == qkv_width:
        qkv_rows, out_rows = gather_ctx(
            jnp.concatenate([w_query, key_matrix, value_matrix, w_out.T], axis=1),
            layout,
            0,
            parts=True,
        )
        projected_all = jnp.dot(
            inputs,
            qkv_rows.reshape(model_width, qkv_width),
            preferred_element_type=jnp.float32,
        ).astype(jnp.bfloat16)
        out_weight_t = out_rows.reshape(model_width, w_out.shape[0])
    else:
        joined = gather_ctx(
            jnp.concatenate([w_query, key_matrix, value_matrix, w_out.T], axis=1), layout, 0
        )
        projected_all = jnp.dot(
            inputs, joined[:, :qkv_width], preferred_element_type=jnp.float32
        ).astype(jnp.bfloat16)
        out_weight_t = joined[:, qkv_width:]
    query_all = projected_all[:, :query_width]
    key_all = projected_all[:, query_width : query_width + kv_width]
    value_all = projected_all[:, query_width + kv_width :]
    local_query = query_all[:local_rows]
    local_keys = key_all[:local_rows]
    local_values = value_all[:local_rows]
    dec_query = query_all[local_rows:]
    decode_key_rows = key_all[local_rows:]
    decode_value_rows = value_all[local_rows:]
    token_pos = initial_positions(block_map, device * local_rows, local_rows, block_rows)
    token_request = request_index(token_pos, request_ends)
    query_heads = local_query.reshape(local_rows, kv_heads, query_group_count, head_dim)

    def attend(running, shard_pieces, first_row):
        peak_run, total_run, mixed_run = running
        key_piece, value_piece = shard_pieces
        row_count = key_piece.shape[0]
        key_pos = lax.dynamic_slice_in_dim(cache_pos, first_row, row_count, 0)
        key_request = lax.dynamic_slice_in_dim(cache_request, first_row, row_count, 0)
        allowed = (key_request[None, :] == token_request[:, None]) & (
            key_pos[None, :] <= token_pos[:, None]
        )
        scores = (
            jnp.einsum(
                "tgjd,kgd->gjtk",
                query_heads,
                key_piece.reshape(row_count, kv_heads, head_dim),
                preferred_element_type=jnp.float32,
            )
            * score_scale
        )
        scores = jnp.where(allowed, scores, floor_value)
        peak_new = jnp.maximum(peak_run, jnp.max(scores, axis=3))
        weights = jnp.exp(scores - peak_new[..., None])
        rescale = jnp.exp(peak_run - peak_new)
        total_new = total_run * rescale + jnp.sum(weights, axis=3)
        mixed_new = mixed_run * rescale[..., None] + jnp.einsum(
            "gjtk,kgd->gjtd",
            weights.astype(jnp.bfloat16),
            value_piece.reshape(row_count, kv_heads, head_dim),
            preferred_element_type=jnp.float32,
        )
        return (peak_new, total_new, mixed_new)

    start_state = (
        jnp.full((kv_heads, query_group_count, local_rows), floor_value, jnp.float32),
        jnp.zeros((kv_heads, query_group_count, local_rows), jnp.float32),
        jnp.zeros((kv_heads, query_group_count, local_rows, head_dim), jnp.float32),
    )
    dec_heads = dec_query.reshape(request_count, kv_heads, query_group_count, head_dim)
    request_ids = jnp.arange(request_count, dtype=jnp.int32)
    cache_both = gather_ctx(
        jnp.concatenate([local_keys, local_values], axis=1), layout, 1
    )
    cache_keys = cache_both[:, :kv_width]
    cache_values = cache_both[:, kv_width:]
    total_rows = cache_keys.shape[0]
    step_rows = total_rows
    cache_pos = (
        block_map[:, None] * block_rows + jnp.arange(block_rows, dtype=jnp.int32)[None, :]
    ).reshape(total_rows)
    cache_request = request_index(cache_pos, request_ends)

    def key_step(running, step_index):
        first_row = step_index * step_rows
        pieces = (
            lax.dynamic_slice_in_dim(cache_keys, first_row, step_rows, 0),
            lax.dynamic_slice_in_dim(cache_values, first_row, step_rows, 0),
        )
        return (attend(running, pieces, first_row), None)

    final_state, unused = lax.scan(
        key_step, start_state, jnp.arange(total_rows // step_rows, dtype=jnp.int32)
    )
    peak_run, total_run, mixed_run = final_state
    owned = (cache_request[None, :] == request_ids[:, None])[:, None, None, :]
    cache_peak, cache_total, cache_mixed = softmax_parts(
        dec_heads, cache_keys, cache_values, owned, kv_heads, head_dim, score_scale
    )
    attended = (
        (mixed_run / total_run[..., None]).transpose(2, 0, 1, 3).reshape(local_rows, query_width)
    )
    attended = attended.astype(jnp.bfloat16)
    own_keys = decode_key_rows.reshape(request_count, kv_heads, 1, head_dim).astype(jnp.float32)
    own_values = decode_value_rows.reshape(request_count, kv_heads, 1, head_dim).astype(jnp.float32)
    self_scores = jnp.sum(dec_heads.astype(jnp.float32) * own_keys, axis=3) * score_scale
    peak_all = jnp.maximum(cache_peak, self_scores)
    rescale = jnp.exp(cache_peak - peak_all)
    self_weights = jnp.exp(self_scores - peak_all)
    dec_total = cache_total * rescale + self_weights
    dec_mixed = (
        cache_mixed * rescale[..., None] + round_weights(self_weights)[..., None] * own_values
    )
    dec_attn = (
        (dec_mixed / dec_total[..., None]).reshape(request_count, query_width).astype(jnp.bfloat16)
    )
    attended_all = jnp.concatenate([attended, dec_attn], axis=0)
    projected = lax.dot_general(
        attended_all,
        out_weight_t,
        (((1,), (1,)), ((), ())),
        preferred_element_type=jnp.float32,
    )
    return scatter_sum_tp(projected.astype(jnp.bfloat16), tp_count, 2, split=local_rows)


def solution(mesh):
    return jax.shard_map(
        functools.partial(on_device, ctx_layout(mesh), mesh.shape["tp"]),
        mesh=mesh,
        in_specs=(
            P("ctx", None),
            P(),
            P("ctx", "tp"),
            P("ctx", "tp"),
            P("ctx", "tp"),
            P("tp", "ctx"),
            P(),
            P(),
        ),
        out_specs=(P("ctx", "tp"), P(None, "tp")),
        check_vma=False,
    )
```

```python
import functools
import math

import jax
import jax.numpy as jnp
from jax import lax
from jax.experimental import pallas as pl
from jax.experimental.pallas import tpu as pltpu
from jax.sharding import PartitionSpec as P

HEAD_SIZE = 128


floor_value = -1e30


def _gather_kernel(
    z_count,
    p_count,
    first_ref,
    second_ref,
    first_out,
    second_out,
    first_z,
    first_p,
    second_p,
    second_z,
    local_sems,
):
    me = lax.axis_index("ctx")
    z_me = me // p_count
    p_me = lax.rem(me, p_count)
    mesh_ids = pl.DeviceIdType.MESH
    barrier = pltpu.get_barrier_semaphore()

    def z_peer(step):
        return lax.rem(z_me + step, z_count)

    def p_peer(step):
        return lax.rem(p_me + step, p_count)

    def z_target(peer):
        return peer * p_count + p_me

    def p_target(peer):
        return z_me * p_count + peer

    def greet(peer_of, target_of):
        def body(step, carry):
            pl.semaphore_signal(
                barrier, 1, device_id={"ctx": target_of(peer_of(step))}, device_id_type=mesh_ids
            )
            return carry

        return body

    lax.fori_loop(1, z_count, greet(z_peer, z_target), 0)
    lax.fori_loop(1, p_count, greet(p_peer, p_target), 0)
    pl.semaphore_wait(barrier, z_count + p_count - 2)

    def remote(src, dst, send_sem, recv_sem, target):
        return pltpu.make_async_remote_copy(
            src_ref=src,
            dst_ref=dst,
            send_sem=send_sem,
            recv_sem=recv_sem,
            device_id={"ctx": target},
            device_id_type=mesh_ids,
        )

    def first_one(peer, slot):
        return remote(
            first_ref, first_out.at[slot, p_me], first_z[0].at[peer], first_z[1].at[slot],
            z_target(peer),
        )

    def second_one(peer, slot):
        return remote(
            second_ref, second_out.at[z_me, slot], second_p[0].at[peer], second_p[1].at[slot],
            p_target(peer),
        )

    def first_two(peer, row, slot):
        return remote(
            first_out.at[slot, row], first_out.at[slot, row], first_p[0].at[peer],
            first_p[1].at[row], p_target(peer),
        )

    def second_two(peer, row, slot):
        return remote(
            second_out.at[row, slot], second_out.at[row, slot], second_z[0].at[peer],
            second_z[1].at[row], z_target(peer),
        )

    def first_rows(peer, row):
        return remote(
            first_out.at[:, row], first_out.at[:, row], first_p[0].at[peer], first_p[1].at[row],
            p_target(peer),
        )

    def second_rows(peer, row):
        return remote(
            second_out.at[row], second_out.at[row], second_z[0].at[peer], second_z[1].at[row],
            z_target(peer),
        )

    first_own = pltpu.make_async_copy(first_ref, first_out.at[z_me, p_me], local_sems.at[0])
    second_own = pltpu.make_async_copy(second_ref, second_out.at[z_me, p_me], local_sems.at[1])
    first_own.start()
    second_own.start()

    def start_one(step, carry):
        @pl.when(step < z_count)
        def _():
            first_one(z_peer(step), z_me).start()

        @pl.when(step < p_count)
        def _():
            second_one(p_peer(step), p_me).start()

        return carry

    rounds = max(z_count, p_count)
    lax.fori_loop(1, rounds, start_one, 0)

    def forward_first(slot):
        def body(step, carry):
            first_two(p_peer(step), p_me, slot).start()
            return carry

        lax.fori_loop(1, p_count, body, 0)

    def forward_second(slot):
        def body(step, carry):
            second_two(z_peer(step), z_me, slot).start()
            return carry

        lax.fori_loop(1, z_count, body, 0)

    first_own.wait()
    forward_first(z_me)
    second_own.wait()
    forward_second(p_me)

    def relay(step, carry):
        @pl.when(step < z_count)
        def _():
            slot = z_peer(step)
            first_one(slot, slot).wait_recv()
            forward_first(slot)

        @pl.when(step < p_count)
        def _():
            slot = p_peer(step)
            second_one(slot, slot).wait_recv()
            forward_second(slot)

        return carry

    lax.fori_loop(1, rounds, relay, 0)

    def drain(step, carry):
        @pl.when(step < z_count)
        def _():
            peer = z_peer(step)
            first_one(peer, z_me).wait_send()
            second_rows(peer, z_me).wait_send()
            second_rows(peer, peer).wait_recv()

        @pl.when(step < p_count)
        def _():
            peer = p_peer(step)
            second_one(peer, p_me).wait_send()
            first_rows(peer, p_me).wait_send()
            first_rows(peer, peer).wait_recv()

        return carry

    lax.fori_loop(1, rounds, drain, 0)


def gather_ctx(piece, layout, kernel_id, parts=False):
    z_count, p_count = layout
    rows, cols = piece.shape
    lane = 128
    by_columns = cols % (3 * lane) == 0
    if by_columns:
        head = 2 * cols // 3
        shapes = ((rows, head), (rows, cols - head))
        pieces = (piece[:, :head], piece[:, head:])
    else:
        tile = 16
        head = min(rows - tile, max(tile, round(rows * 2 / (3 * tile)) * tile))
        shapes = ((head, cols), (rows - head, cols))
        pieces = (piece[:head], piece[head:])
    dma_pairs = [
        pltpu.SemaphoreType.DMA((z_count,)),
        pltpu.SemaphoreType.DMA((z_count,)),
        pltpu.SemaphoreType.DMA((p_count,)),
        pltpu.SemaphoreType.DMA((p_count,)),
    ]

    def kernel(first_ref, second_ref, first_out, second_out, *sems):
        _gather_kernel(
            z_count, p_count, first_ref, second_ref, first_out, second_out,
            (sems[0], sems[1]), (sems[2], sems[3]), (sems[4], sems[5]), (sems[6], sems[7]),
            sems[8],
        )

    if not by_columns and not parts:
        split_rows = shapes[0][0]

        def owned_kernel(piece_ref, out_ref, *sems):
            kernel(
                piece_ref.at[pl.ds(0, split_rows)],
                piece_ref.at[pl.ds(split_rows, rows - split_rows)],
                out_ref.at[:, :, pl.ds(0, split_rows)],
                out_ref.at[:, :, pl.ds(split_rows, rows - split_rows)],
                *sems,
            )

        whole = pl.pallas_call(
            owned_kernel,
            out_shape=jax.ShapeDtypeStruct((z_count, p_count, rows, cols), piece.dtype),
            in_specs=[pl.BlockSpec(memory_space=pl.ANY)],
            out_specs=pl.BlockSpec(memory_space=pl.ANY),
            scratch_shapes=dma_pairs + [dma_pairs[2], dma_pairs[3], dma_pairs[0], dma_pairs[1]]
            + [pltpu.SemaphoreType.DMA((2,))],
            compiler_params=pltpu.CompilerParams(collective_id=kernel_id, has_side_effects=True),
        )(piece)
        return whole.reshape(z_count * p_count * rows, cols)
    first, second = pl.pallas_call(
        kernel,
        out_shape=(
            jax.ShapeDtypeStruct((z_count, p_count) + shapes[0], piece.dtype),
            jax.ShapeDtypeStruct((z_count, p_count) + shapes[1], piece.dtype),
        ),
        in_specs=[pl.BlockSpec(memory_space=pl.ANY)] * 2,
        out_specs=(pl.BlockSpec(memory_space=pl.ANY),) * 2,
        scratch_shapes=dma_pairs + [dma_pairs[2], dma_pairs[3], dma_pairs[0], dma_pairs[1]]
        + [pltpu.SemaphoreType.DMA((2,))],
        compiler_params=pltpu.CompilerParams(collective_id=kernel_id, has_side_effects=True),
    )(*pieces)
    if parts:
        return first, second
    joined = jnp.concatenate([first, second], axis=3 if by_columns else 2)
    return joined.reshape(z_count * p_count * rows, cols)


def _scatter_kernel(count, part_ref, out_ref, send_sems, recv_sems, local_sem):
    me = lax.axis_index("tp")
    width = out_ref.shape[2]
    mesh_ids = pl.DeviceIdType.MESH
    barrier = pltpu.get_barrier_semaphore()

    def greet(step, carry):
        peer = lax.rem(me + step, count)
        pl.semaphore_signal(barrier, 1, device_id={"tp": peer}, device_id_type=mesh_ids)
        return carry

    lax.fori_loop(1, count, greet, 0)
    pl.semaphore_wait(barrier, count - 1)

    def columns(index):
        return pl.ds(pl.multiple_of(index * width, width), width)

    own = pltpu.make_async_copy(part_ref.at[:, columns(me)], out_ref.at[me], local_sem)
    own.start()

    def remote(peer, slot):
        return pltpu.make_async_remote_copy(
            src_ref=part_ref.at[:, columns(peer)],
            dst_ref=out_ref.at[slot],
            send_sem=send_sems.at[peer],
            recv_sem=recv_sems.at[slot],
            device_id={"tp": peer},
            device_id_type=mesh_ids,
        )

    def send(step, carry):
        remote(lax.rem(me + step, count), me).start()
        return carry

    def finish(step, carry):
        peer = lax.rem(me + step, count)
        remote(peer, me).wait_send()
        remote(peer, peer).wait_recv()
        return carry

    if count % 2 == 0 and count >= 4:
        outer = count // 2
        order = sorted(range(outer), key=lambda hop: -min(hop, outer - hop))
        for hop in order:
            for core in range(2):
                peer = lax.rem(me // 2 + hop, outer) * 2 + core

                @pl.when(peer != me)
                def _():
                    remote(peer, me).start()
    else:
        lax.fori_loop(1, count, send, 0)
    lax.fori_loop(1, count, finish, 0)
    own.wait()


def scatter_sum_tp(part, count, kernel_id):
    rows, cols = part.shape
    pieces = pl.pallas_call(
        functools.partial(_scatter_kernel, count),
        out_shape=jax.ShapeDtypeStruct((count, rows, cols // count), part.dtype),
        in_specs=[pl.BlockSpec(memory_space=pl.ANY)],
        out_specs=pl.BlockSpec(memory_space=pl.ANY),
        scratch_shapes=[
            pltpu.SemaphoreType.DMA((count,)),
            pltpu.SemaphoreType.DMA((count,)),
            pltpu.SemaphoreType.DMA(()),
        ],
        compiler_params=pltpu.CompilerParams(collective_id=kernel_id, has_side_effects=True),
    )(part)
    return jnp.sum(pieces.astype(jnp.float32), axis=0)


def ctx_layout(mesh):
    count = mesh.shape["ctx"]
    column = mesh.devices.transpose(
        mesh.axis_names.index("ctx"), mesh.axis_names.index("tp")
    )[:, 0]
    try:
        planes = [device.coords[2] for device in column]
    except (AttributeError, IndexError, TypeError):
        return (count, 1)
    p_count = 1
    while p_count < count and planes[p_count] == planes[0]:
        p_count += 1
    if count % p_count:
        return (count, 1)
    for index in range(count):
        if planes[index] != planes[(index // p_count) * p_count]:
            return (count, 1)
    return (count // p_count, p_count)


def initial_positions(block_map, first_row, row_count, block_rows):
    row_ids = first_row + jnp.arange(row_count, dtype=jnp.int32)
    block_ids = row_ids // block_rows
    table_ids = jnp.arange(block_map.shape[0], dtype=jnp.int32)
    mapped = jnp.sum(
        jnp.where(block_ids[:, None] == table_ids[None, :], block_map[None, :], 0), axis=1
    )
    return mapped * block_rows + row_ids % block_rows


def request_index(positions, request_ends):
    return jnp.sum((positions[:, None] >= request_ends[None, :]).astype(jnp.int32), axis=1)


def round_weights(weights):
    rounded = weights.astype(jnp.bfloat16)
    rounded = lax.optimization_barrier(rounded)
    return rounded.astype(jnp.float32)


def softmax_parts(
    dec_heads, projected_key_rows, projected_value_rows, owned, kv_heads, head_dim, score_scale
):
    row_count = projected_key_rows.shape[0]
    scores = (
        jnp.einsum(
            "rgjd,tgd->rgjt",
            dec_heads,
            projected_key_rows.reshape(row_count, kv_heads, head_dim),
            preferred_element_type=jnp.float32,
        )
        * score_scale
    )
    scores = jnp.where(owned, scores, floor_value)
    part_peak = jnp.max(scores, axis=3)
    weights = jnp.where(owned, jnp.exp(scores - part_peak[..., None]), 0.0)
    part_total = jnp.sum(weights, axis=3)
    part_mixed = jnp.einsum(
        "rgjt,tgd->rgjd",
        weights.astype(jnp.bfloat16),
        projected_value_rows.reshape(row_count, kv_heads, head_dim),
        preferred_element_type=jnp.float32,
    )
    return (part_peak, part_total, part_mixed)


def on_device(
    layout, tp_count, tokens, new_token_states, w_query, key_matrix, value_matrix, w_out, lengths, block_map
):
    local_rows = tokens.shape[0]
    block_rows = local_rows // 2
    request_count = new_token_states.shape[0]
    head_dim = HEAD_SIZE
    query_width = w_query.shape[1]
    kv_width = key_matrix.shape[1]
    kv_heads = kv_width // head_dim
    query_group_count = query_width // kv_width
    score_scale = 1.0 / math.sqrt(head_dim)
    device = lax.axis_index("ctx")
    request_ends = jnp.cumsum(lengths)
    inputs = jnp.concatenate([tokens, new_token_states], axis=0)
    z_count, p_count = layout
    model_width = inputs.shape[1]
    qkv_width = query_width + 2 * kv_width
    if (qkv_width + w_out.shape[0]) % 384 == 0 and 2 * w_out.shape[0] == qkv_width:
        qkv_rows, out_rows = gather_ctx(
            jnp.concatenate([w_query, key_matrix, value_matrix, w_out.T], axis=1),
            layout,
            0,
            parts=True,
        )
        projected_all = jnp.dot(
            inputs,
            qkv_rows.reshape(model_width, qkv_width),
            preferred_element_type=jnp.float32,
        ).astype(jnp.bfloat16)
        out_weight_t = out_rows.reshape(model_width, w_out.shape[0])
    else:
        joined = gather_ctx(
            jnp.concatenate([w_query, key_matrix, value_matrix, w_out.T], axis=1), layout, 0
        )
        projected_all = jnp.dot(
            inputs, joined[:, :qkv_width], preferred_element_type=jnp.float32
        ).astype(jnp.bfloat16)
        out_weight_t = joined[:, qkv_width:]
    query_all = projected_all[:, :query_width]
    key_all = projected_all[:, query_width : query_width + kv_width]
    value_all = projected_all[:, query_width + kv_width :]
    local_query = query_all[:local_rows]
    local_keys = key_all[:local_rows]
    local_values = value_all[:local_rows]
    dec_query = query_all[local_rows:]
    decode_key_rows = key_all[local_rows:]
    decode_value_rows = value_all[local_rows:]
    token_pos = initial_positions(block_map, device * local_rows, local_rows, block_rows)
    token_request = request_index(token_pos, request_ends)
    query_heads = local_query.reshape(local_rows, kv_heads, query_group_count, head_dim)

    def attend(running, shard_pieces, first_row):
        peak_run, total_run, mixed_run = running
        key_piece, value_piece = shard_pieces
        row_count = key_piece.shape[0]
        key_pos = lax.dynamic_slice_in_dim(cache_pos, first_row, row_count, 0)
        key_request = lax.dynamic_slice_in_dim(cache_request, first_row, row_count, 0)
        allowed = (key_request[None, :] == token_request[:, None]) & (
            key_pos[None, :] <= token_pos[:, None]
        )
        scores = (
            jnp.einsum(
                "tgjd,kgd->gjtk",
                query_heads,
                key_piece.reshape(row_count, kv_heads, head_dim),
                preferred_element_type=jnp.float32,
            )
            * score_scale
        )
        scores = jnp.where(allowed, scores, floor_value)
        peak_new = jnp.maximum(peak_run, jnp.max(scores, axis=3))
        weights = jnp.where(allowed, jnp.exp(scores - peak_new[..., None]), 0.0)
        rescale = jnp.exp(peak_run - peak_new)
        total_new = total_run * rescale + jnp.sum(weights, axis=3)
        mixed_new = mixed_run * rescale[..., None] + jnp.einsum(
            "gjtk,kgd->gjtd",
            weights.astype(jnp.bfloat16),
            value_piece.reshape(row_count, kv_heads, head_dim),
            preferred_element_type=jnp.float32,
        )
        return (peak_new, total_new, mixed_new)

    start_state = (
        jnp.full((kv_heads, query_group_count, local_rows), floor_value, jnp.float32),
        jnp.zeros((kv_heads, query_group_count, local_rows), jnp.float32),
        jnp.zeros((kv_heads, query_group_count, local_rows, head_dim), jnp.float32),
    )
    dec_heads = dec_query.reshape(request_count, kv_heads, query_group_count, head_dim)
    request_ids = jnp.arange(request_count, dtype=jnp.int32)
    cache_both = gather_ctx(
        jnp.concatenate([local_keys, local_values], axis=1), layout, 1
    )
    cache_keys = cache_both[:, :kv_width]
    cache_values = cache_both[:, kv_width:]
    total_rows = cache_keys.shape[0]
    step_rows = total_rows
    cache_pos = (
        block_map[:, None] * block_rows + jnp.arange(block_rows, dtype=jnp.int32)[None, :]
    ).reshape(total_rows)
    cache_request = request_index(cache_pos, request_ends)

    def key_step(running, step_index):
        first_row = step_index * step_rows
        pieces = (
            lax.dynamic_slice_in_dim(cache_keys, first_row, step_rows, 0),
            lax.dynamic_slice_in_dim(cache_values, first_row, step_rows, 0),
        )
        return (attend(running, pieces, first_row), None)

    final_state, unused = lax.scan(
        key_step, start_state, jnp.arange(total_rows // step_rows, dtype=jnp.int32)
    )
    peak_run, total_run, mixed_run = final_state
    owned = (cache_request[None, :] == request_ids[:, None])[:, None, None, :]
    cache_peak, cache_total, cache_mixed = softmax_parts(
        dec_heads, cache_keys, cache_values, owned, kv_heads, head_dim, score_scale
    )
    attended = (
        (mixed_run / total_run[..., None]).transpose(2, 0, 1, 3).reshape(local_rows, query_width)
    )
    attended = attended.astype(jnp.bfloat16)
    own_keys = decode_key_rows.reshape(request_count, kv_heads, 1, head_dim).astype(jnp.float32)
    own_values = decode_value_rows.reshape(request_count, kv_heads, 1, head_dim).astype(jnp.float32)
    self_scores = jnp.sum(dec_heads.astype(jnp.float32) * own_keys, axis=3) * score_scale
    peak_all = jnp.maximum(cache_peak, self_scores)
    rescale = jnp.exp(cache_peak - peak_all)
    self_weights = jnp.exp(self_scores - peak_all)
    dec_total = cache_total * rescale + self_weights
    dec_mixed = (
        cache_mixed * rescale[..., None] + round_weights(self_weights)[..., None] * own_values
    )
    dec_attn = (
        (dec_mixed / dec_total[..., None]).reshape(request_count, query_width).astype(jnp.bfloat16)
    )
    attended_all = jnp.concatenate([attended, dec_attn], axis=0)
    projected = lax.dot_general(
        attended_all,
        out_weight_t,
        (((1,), (1,)), ((), ())),
        preferred_element_type=jnp.float32,
    )
    summed_rows = scatter_sum_tp(projected.astype(jnp.bfloat16), tp_count, 2)
    summed_rows = summed_rows.astype(jnp.bfloat16)
    return (summed_rows[:local_rows], summed_rows[local_rows:])


def solution(mesh):
    return jax.shard_map(
        functools.partial(on_device, ctx_layout(mesh), mesh.shape["tp"]),
        mesh=mesh,
        in_specs=(
            P("ctx", None),
            P(),
            P("ctx", "tp"),
            P("ctx", "tp"),
            P("ctx", "tp"),
            P("tp", "ctx"),
            P(),
            P(),
        ),
        out_specs=(P("ctx", "tp"), P(None, "tp")),
        check_vma=False,
    )
```

```python
import functools
import math

import jax
import jax.numpy as jnp
from jax import lax
from jax.experimental import pallas as pl
from jax.experimental.pallas import tpu as pltpu
from jax.sharding import PartitionSpec as P

HEAD_SIZE = 128


floor_value = -1e30


def _gather_kernel(
    z_count,
    p_count,
    first_ref,
    second_ref,
    first_out,
    second_out,
    first_z,
    first_p,
    second_p,
    second_z,
    local_sems,
):
    me = lax.axis_index("ctx")
    z_me = me // p_count
    p_me = lax.rem(me, p_count)
    mesh_ids = pl.DeviceIdType.MESH
    barrier = pltpu.get_barrier_semaphore()

    def z_peer(step):
        return lax.rem(z_me + step, z_count)

    def p_peer(step):
        return lax.rem(p_me + step, p_count)

    def z_target(peer):
        return peer * p_count + p_me

    def p_target(peer):
        return z_me * p_count + peer

    def greet(peer_of, target_of):
        def body(step, carry):
            pl.semaphore_signal(
                barrier, 1, device_id={"ctx": target_of(peer_of(step))}, device_id_type=mesh_ids
            )
            return carry

        return body

    lax.fori_loop(1, z_count, greet(z_peer, z_target), 0)
    lax.fori_loop(1, p_count, greet(p_peer, p_target), 0)
    pl.semaphore_wait(barrier, z_count + p_count - 2)

    def remote(src, dst, send_sem, recv_sem, target):
        return pltpu.make_async_remote_copy(
            src_ref=src,
            dst_ref=dst,
            send_sem=send_sem,
            recv_sem=recv_sem,
            device_id={"ctx": target},
            device_id_type=mesh_ids,
        )

    def first_one(peer, slot):
        return remote(
            first_ref, first_out.at[slot, p_me], first_z[0].at[peer], first_z[1].at[slot],
            z_target(peer),
        )

    def second_one(peer, slot):
        return remote(
            second_ref, second_out.at[z_me, slot], second_p[0].at[peer], second_p[1].at[slot],
            p_target(peer),
        )

    def first_two(peer, row, slot):
        return remote(
            first_out.at[slot, row], first_out.at[slot, row], first_p[0].at[peer],
            first_p[1].at[row], p_target(peer),
        )

    def second_two(peer, row, slot):
        return remote(
            second_out.at[row, slot], second_out.at[row, slot], second_z[0].at[peer],
            second_z[1].at[row], z_target(peer),
        )

    def first_rows(peer, row):
        return remote(
            first_out.at[:, row], first_out.at[:, row], first_p[0].at[peer], first_p[1].at[row],
            p_target(peer),
        )

    def second_rows(peer, row):
        return remote(
            second_out.at[row], second_out.at[row], second_z[0].at[peer], second_z[1].at[row],
            z_target(peer),
        )

    first_own = pltpu.make_async_copy(first_ref, first_out.at[z_me, p_me], local_sems.at[0])
    second_own = pltpu.make_async_copy(second_ref, second_out.at[z_me, p_me], local_sems.at[1])
    first_own.start()
    second_own.start()

    def start_one(step, carry):
        @pl.when(step < z_count)
        def _():
            first_one(z_peer(step), z_me).start()

        @pl.when(step < p_count)
        def _():
            second_one(p_peer(step), p_me).start()

        return carry

    rounds = max(z_count, p_count)
    for hop in sorted(range(1, z_count), key=lambda hop: -min(hop, z_count - hop)):
        first_one(z_peer(hop), z_me).start()

    def start_second(step, carry):
        second_one(p_peer(step), p_me).start()
        return carry

    lax.fori_loop(1, p_count, start_second, 0)

    def forward_first(slot):
        def body(step, carry):
            first_two(p_peer(step), p_me, slot).start()
            return carry

        lax.fori_loop(1, p_count, body, 0)

    def forward_second(slot):
        def body(step, carry):
            second_two(z_peer(step), z_me, slot).start()
            return carry

        lax.fori_loop(1, z_count, body, 0)

    first_own.wait()
    forward_first(z_me)
    second_own.wait()
    forward_second(p_me)

    def relay(step, carry):
        @pl.when(step < z_count)
        def _():
            slot = z_peer(step)
            first_one(slot, slot).wait_recv()
            forward_first(slot)

        @pl.when(step < p_count)
        def _():
            slot = p_peer(step)
            second_one(slot, slot).wait_recv()
            forward_second(slot)

        return carry

    lax.fori_loop(1, rounds, relay, 0)

    def drain(step, carry):
        @pl.when(step < z_count)
        def _():
            peer = z_peer(step)
            first_one(peer, z_me).wait_send()
            second_rows(peer, z_me).wait_send()
            second_rows(peer, peer).wait_recv()

        @pl.when(step < p_count)
        def _():
            peer = p_peer(step)
            second_one(peer, p_me).wait_send()
            first_rows(peer, p_me).wait_send()
            first_rows(peer, peer).wait_recv()

        return carry

    lax.fori_loop(1, rounds, drain, 0)


def gather_ctx(piece, layout, kernel_id, parts=False):
    z_count, p_count = layout
    rows, cols = piece.shape
    lane = 128
    by_columns = cols % (3 * lane) == 0
    if by_columns:
        head = 2 * cols // 3
        shapes = ((rows, head), (rows, cols - head))
        pieces = (piece[:, :head], piece[:, head:])
    else:
        tile = 16
        head = min(rows - tile, max(tile, round(rows * 2 / (3 * tile)) * tile))
        shapes = ((head, cols), (rows - head, cols))
        pieces = (piece[:head], piece[head:])
    dma_pairs = [
        pltpu.SemaphoreType.DMA((z_count,)),
        pltpu.SemaphoreType.DMA((z_count,)),
        pltpu.SemaphoreType.DMA((p_count,)),
        pltpu.SemaphoreType.DMA((p_count,)),
    ]

    def kernel(first_ref, second_ref, first_out, second_out, *sems):
        _gather_kernel(
            z_count, p_count, first_ref, second_ref, first_out, second_out,
            (sems[0], sems[1]), (sems[2], sems[3]), (sems[4], sems[5]), (sems[6], sems[7]),
            sems[8],
        )

    if not by_columns and not parts:
        split_rows = shapes[0][0]

        def owned_kernel(piece_ref, out_ref, *sems):
            kernel(
                piece_ref.at[pl.ds(0, split_rows)],
                piece_ref.at[pl.ds(split_rows, rows - split_rows)],
                out_ref.at[:, :, pl.ds(0, split_rows)],
                out_ref.at[:, :, pl.ds(split_rows, rows - split_rows)],
                *sems,
            )

        whole = pl.pallas_call(
            owned_kernel,
            out_shape=jax.ShapeDtypeStruct((z_count, p_count, rows, cols), piece.dtype),
            in_specs=[pl.BlockSpec(memory_space=pl.ANY)],
            out_specs=pl.BlockSpec(memory_space=pl.ANY),
            scratch_shapes=dma_pairs + [dma_pairs[2], dma_pairs[3], dma_pairs[0], dma_pairs[1]]
            + [pltpu.SemaphoreType.DMA((2,))],
            compiler_params=pltpu.CompilerParams(collective_id=kernel_id, has_side_effects=True),
        )(piece)
        return whole.reshape(z_count * p_count * rows, cols)
    first, second = pl.pallas_call(
        kernel,
        out_shape=(
            jax.ShapeDtypeStruct((z_count, p_count) + shapes[0], piece.dtype),
            jax.ShapeDtypeStruct((z_count, p_count) + shapes[1], piece.dtype),
        ),
        in_specs=[pl.BlockSpec(memory_space=pl.ANY)] * 2,
        out_specs=(pl.BlockSpec(memory_space=pl.ANY),) * 2,
        scratch_shapes=dma_pairs + [dma_pairs[2], dma_pairs[3], dma_pairs[0], dma_pairs[1]]
        + [pltpu.SemaphoreType.DMA((2,))],
        compiler_params=pltpu.CompilerParams(collective_id=kernel_id, has_side_effects=True),
    )(*pieces)
    if parts:
        return first, second
    joined = jnp.concatenate([first, second], axis=3 if by_columns else 2)
    return joined.reshape(z_count * p_count * rows, cols)


def _scatter_kernel(count, part_ref, out_ref, send_sems, recv_sems, local_sem):
    me = lax.axis_index("tp")
    width = out_ref.shape[2]
    mesh_ids = pl.DeviceIdType.MESH
    barrier = pltpu.get_barrier_semaphore()

    def greet(step, carry):
        peer = lax.rem(me + step, count)
        pl.semaphore_signal(barrier, 1, device_id={"tp": peer}, device_id_type=mesh_ids)
        return carry

    lax.fori_loop(1, count, greet, 0)
    pl.semaphore_wait(barrier, count - 1)

    def columns(index):
        return pl.ds(pl.multiple_of(index * width, width), width)

    own = pltpu.make_async_copy(part_ref.at[:, columns(me)], out_ref.at[me], local_sem)
    own.start()

    def remote(peer, slot):
        return pltpu.make_async_remote_copy(
            src_ref=part_ref.at[:, columns(peer)],
            dst_ref=out_ref.at[slot],
            send_sem=send_sems.at[peer],
            recv_sem=recv_sems.at[slot],
            device_id={"tp": peer},
            device_id_type=mesh_ids,
        )

    def send(step, carry):
        remote(lax.rem(me + step, count), me).start()
        return carry

    def finish(step, carry):
        peer = lax.rem(me + step, count)
        remote(peer, me).wait_send()
        remote(peer, peer).wait_recv()
        return carry

    if count % 2 == 0 and count >= 4:
        outer = count // 2
        order = sorted(range(outer), key=lambda hop: -min(hop, outer - hop))
        for hop in order:
            for core in range(2):
                peer = lax.rem(me // 2 + hop, outer) * 2 + core

                @pl.when(peer != me)
                def _():
                    remote(peer, me).start()
    else:
        lax.fori_loop(1, count, send, 0)
    lax.fori_loop(1, count, finish, 0)
    own.wait()


def scatter_sum_tp(part, count, kernel_id):
    rows, cols = part.shape
    pieces = pl.pallas_call(
        functools.partial(_scatter_kernel, count),
        out_shape=jax.ShapeDtypeStruct((count, rows, cols // count), part.dtype),
        in_specs=[pl.BlockSpec(memory_space=pl.ANY)],
        out_specs=pl.BlockSpec(memory_space=pl.ANY),
        scratch_shapes=[
            pltpu.SemaphoreType.DMA((count,)),
            pltpu.SemaphoreType.DMA((count,)),
            pltpu.SemaphoreType.DMA(()),
        ],
        compiler_params=pltpu.CompilerParams(collective_id=kernel_id, has_side_effects=True),
    )(part)
    return jnp.sum(pieces.astype(jnp.float32), axis=0)


def ctx_layout(mesh):
    count = mesh.shape["ctx"]
    column = mesh.devices.transpose(
        mesh.axis_names.index("ctx"), mesh.axis_names.index("tp")
    )[:, 0]
    try:
        planes = [device.coords[2] for device in column]
    except (AttributeError, IndexError, TypeError):
        return (count, 1)
    p_count = 1
    while p_count < count and planes[p_count] == planes[0]:
        p_count += 1
    if count % p_count:
        return (count, 1)
    for index in range(count):
        if planes[index] != planes[(index // p_count) * p_count]:
            return (count, 1)
    return (count // p_count, p_count)


def initial_positions(block_map, first_row, row_count, block_rows):
    row_ids = first_row + jnp.arange(row_count, dtype=jnp.int32)
    block_ids = row_ids // block_rows
    table_ids = jnp.arange(block_map.shape[0], dtype=jnp.int32)
    mapped = jnp.sum(
        jnp.where(block_ids[:, None] == table_ids[None, :], block_map[None, :], 0), axis=1
    )
    return mapped * block_rows + row_ids % block_rows


def request_index(positions, request_ends):
    return jnp.sum((positions[:, None] >= request_ends[None, :]).astype(jnp.int32), axis=1)


def round_weights(weights):
    rounded = weights.astype(jnp.bfloat16)
    rounded = lax.optimization_barrier(rounded)
    return rounded.astype(jnp.float32)


def softmax_parts(
    dec_heads, projected_key_rows, projected_value_rows, owned, kv_heads, head_dim, score_scale
):
    row_count = projected_key_rows.shape[0]
    scores = (
        jnp.einsum(
            "rgjd,tgd->rgjt",
            dec_heads,
            projected_key_rows.reshape(row_count, kv_heads, head_dim),
            preferred_element_type=jnp.float32,
        )
        * score_scale
    )
    scores = jnp.where(owned, scores, floor_value)
    part_peak = jnp.max(scores, axis=3)
    weights = jnp.where(owned, jnp.exp(scores - part_peak[..., None]), 0.0)
    part_total = jnp.sum(weights, axis=3)
    part_mixed = jnp.einsum(
        "rgjt,tgd->rgjd",
        weights.astype(jnp.bfloat16),
        projected_value_rows.reshape(row_count, kv_heads, head_dim),
        preferred_element_type=jnp.float32,
    )
    return (part_peak, part_total, part_mixed)


def on_device(
    layout, tp_count, tokens, new_token_states, w_query, key_matrix, value_matrix, w_out, lengths, block_map
):
    local_rows = tokens.shape[0]
    block_rows = local_rows // 2
    request_count = new_token_states.shape[0]
    head_dim = HEAD_SIZE
    query_width = w_query.shape[1]
    kv_width = key_matrix.shape[1]
    kv_heads = kv_width // head_dim
    query_group_count = query_width // kv_width
    score_scale = 1.0 / math.sqrt(head_dim)
    device = lax.axis_index("ctx")
    request_ends = jnp.cumsum(lengths)
    inputs = jnp.concatenate([tokens, new_token_states], axis=0)
    z_count, p_count = layout
    model_width = inputs.shape[1]
    qkv_width = query_width + 2 * kv_width
    if (qkv_width + w_out.shape[0]) % 384 == 0 and 2 * w_out.shape[0] == qkv_width:
        qkv_rows, out_rows = gather_ctx(
            jnp.concatenate([w_query, key_matrix, value_matrix, w_out.T], axis=1),
            layout,
            0,
            parts=True,
        )
        projected_all = jnp.dot(
            inputs,
            qkv_rows.reshape(model_width, qkv_width),
            preferred_element_type=jnp.float32,
        ).astype(jnp.bfloat16)
        out_weight_t = out_rows.reshape(model_width, w_out.shape[0])
    else:
        joined = gather_ctx(
            jnp.concatenate([w_query, key_matrix, value_matrix, w_out.T], axis=1), layout, 0
        )
        projected_all = jnp.dot(
            inputs, joined[:, :qkv_width], preferred_element_type=jnp.float32
        ).astype(jnp.bfloat16)
        out_weight_t = joined[:, qkv_width:]
    query_all = projected_all[:, :query_width]
    key_all = projected_all[:, query_width : query_width + kv_width]
    value_all = projected_all[:, query_width + kv_width :]
    local_query = query_all[:local_rows]
    local_keys = key_all[:local_rows]
    local_values = value_all[:local_rows]
    dec_query = query_all[local_rows:]
    decode_key_rows = key_all[local_rows:]
    decode_value_rows = value_all[local_rows:]
    token_pos = initial_positions(block_map, device * local_rows, local_rows, block_rows)
    token_request = request_index(token_pos, request_ends)
    query_heads = local_query.reshape(local_rows, kv_heads, query_group_count, head_dim)

    def attend(running, shard_pieces, first_row):
        peak_run, total_run, mixed_run = running
        key_piece, value_piece = shard_pieces
        row_count = key_piece.shape[0]
        key_pos = lax.dynamic_slice_in_dim(cache_pos, first_row, row_count, 0)
        key_request = lax.dynamic_slice_in_dim(cache_request, first_row, row_count, 0)
        allowed = (key_request[None, :] == token_request[:, None]) & (
            key_pos[None, :] <= token_pos[:, None]
        )
        scores = (
            jnp.einsum(
                "tgjd,kgd->gjtk",
                query_heads,
                key_piece.reshape(row_count, kv_heads, head_dim),
                preferred_element_type=jnp.float32,
            )
            * score_scale
        )
        scores = jnp.where(allowed, scores, floor_value)
        peak_new = jnp.maximum(peak_run, jnp.max(scores, axis=3))
        weights = jnp.where(allowed, jnp.exp(scores - peak_new[..., None]), 0.0)
        rescale = jnp.exp(peak_run - peak_new)
        total_new = total_run * rescale + jnp.sum(weights, axis=3)
        mixed_new = mixed_run * rescale[..., None] + jnp.einsum(
            "gjtk,kgd->gjtd",
            weights.astype(jnp.bfloat16),
            value_piece.reshape(row_count, kv_heads, head_dim),
            preferred_element_type=jnp.float32,
        )
        return (peak_new, total_new, mixed_new)

    start_state = (
        jnp.full((kv_heads, query_group_count, local_rows), floor_value, jnp.float32),
        jnp.zeros((kv_heads, query_group_count, local_rows), jnp.float32),
        jnp.zeros((kv_heads, query_group_count, local_rows, head_dim), jnp.float32),
    )
    dec_heads = dec_query.reshape(request_count, kv_heads, query_group_count, head_dim)
    request_ids = jnp.arange(request_count, dtype=jnp.int32)
    cache_both = gather_ctx(
        jnp.concatenate([local_keys, local_values], axis=1), layout, 1
    )
    cache_keys = cache_both[:, :kv_width]
    cache_values = cache_both[:, kv_width:]
    total_rows = cache_keys.shape[0]
    step_rows = total_rows
    cache_pos = (
        block_map[:, None] * block_rows + jnp.arange(block_rows, dtype=jnp.int32)[None, :]
    ).reshape(total_rows)
    cache_request = request_index(cache_pos, request_ends)

    def key_step(running, step_index):
        first_row = step_index * step_rows
        pieces = (
            lax.dynamic_slice_in_dim(cache_keys, first_row, step_rows, 0),
            lax.dynamic_slice_in_dim(cache_values, first_row, step_rows, 0),
        )
        return (attend(running, pieces, first_row), None)

    final_state, unused = lax.scan(
        key_step, start_state, jnp.arange(total_rows // step_rows, dtype=jnp.int32)
    )
    peak_run, total_run, mixed_run = final_state
    owned = (cache_request[None, :] == request_ids[:, None])[:, None, None, :]
    cache_peak, cache_total, cache_mixed = softmax_parts(
        dec_heads, cache_keys, cache_values, owned, kv_heads, head_dim, score_scale
    )
    attended = (
        (mixed_run / total_run[..., None]).transpose(2, 0, 1, 3).reshape(local_rows, query_width)
    )
    attended = attended.astype(jnp.bfloat16)
    own_keys = decode_key_rows.reshape(request_count, kv_heads, 1, head_dim).astype(jnp.float32)
    own_values = decode_value_rows.reshape(request_count, kv_heads, 1, head_dim).astype(jnp.float32)
    self_scores = jnp.sum(dec_heads.astype(jnp.float32) * own_keys, axis=3) * score_scale
    peak_all = jnp.maximum(cache_peak, self_scores)
    rescale = jnp.exp(cache_peak - peak_all)
    self_weights = jnp.exp(self_scores - peak_all)
    dec_total = cache_total * rescale + self_weights
    dec_mixed = (
        cache_mixed * rescale[..., None] + round_weights(self_weights)[..., None] * own_values
    )
    dec_attn = (
        (dec_mixed / dec_total[..., None]).reshape(request_count, query_width).astype(jnp.bfloat16)
    )
    attended_all = jnp.concatenate([attended, dec_attn], axis=0)
    projected = lax.dot_general(
        attended_all,
        out_weight_t,
        (((1,), (1,)), ((), ())),
        preferred_element_type=jnp.float32,
    )
    summed_rows = scatter_sum_tp(projected.astype(jnp.bfloat16), tp_count, 2)
    summed_rows = summed_rows.astype(jnp.bfloat16)
    return (summed_rows[:local_rows], summed_rows[local_rows:])


def solution(mesh):
    return jax.shard_map(
        functools.partial(on_device, ctx_layout(mesh), mesh.shape["tp"]),
        mesh=mesh,
        in_specs=(
            P("ctx", None),
            P(),
            P("ctx", "tp"),
            P("ctx", "tp"),
            P("ctx", "tp"),
            P("tp", "ctx"),
            P(),
            P(),
        ),
        out_specs=(P("ctx", "tp"), P(None, "tp")),
        check_vma=False,
    )
```

```python
import functools
import math

import jax
import jax.numpy as jnp
from jax import lax
from jax.experimental import pallas as pl
from jax.experimental.pallas import tpu as pltpu
from jax.sharding import PartitionSpec as P

HEAD_SIZE = 128


floor_value = -1e30


def _gather_kernel(
    z_count,
    p_count,
    first_ref,
    second_ref,
    first_out,
    second_out,
    first_z,
    first_p,
    second_p,
    second_z,
    local_sems,
):
    me = lax.axis_index("ctx")
    z_me = me // p_count
    p_me = lax.rem(me, p_count)
    mesh_ids = pl.DeviceIdType.MESH
    barrier = pltpu.get_barrier_semaphore()

    def z_peer(step):
        return lax.rem(z_me + step, z_count)

    def p_peer(step):
        return lax.rem(p_me + step, p_count)

    def z_target(peer):
        return peer * p_count + p_me

    def p_target(peer):
        return z_me * p_count + peer

    def greet(peer_of, target_of):
        def body(step, carry):
            pl.semaphore_signal(
                barrier, 1, device_id={"ctx": target_of(peer_of(step))}, device_id_type=mesh_ids
            )
            return carry

        return body

    lax.fori_loop(1, z_count, greet(z_peer, z_target), 0)
    lax.fori_loop(1, p_count, greet(p_peer, p_target), 0)
    pl.semaphore_wait(barrier, z_count + p_count - 2)

    def remote(src, dst, send_sem, recv_sem, target):
        return pltpu.make_async_remote_copy(
            src_ref=src,
            dst_ref=dst,
            send_sem=send_sem,
            recv_sem=recv_sem,
            device_id={"ctx": target},
            device_id_type=mesh_ids,
        )

    def first_one(peer, slot):
        return remote(
            first_ref, first_out.at[slot, p_me], first_z[0].at[peer], first_z[1].at[slot],
            z_target(peer),
        )

    def second_one(peer, slot):
        return remote(
            second_ref, second_out.at[z_me, slot], second_p[0].at[peer], second_p[1].at[slot],
            p_target(peer),
        )

    def first_two(peer, row, slot):
        return remote(
            first_out.at[slot, row], first_out.at[slot, row], first_p[0].at[peer],
            first_p[1].at[row], p_target(peer),
        )

    def second_two(peer, row, slot):
        return remote(
            second_out.at[row, slot], second_out.at[row, slot], second_z[0].at[peer],
            second_z[1].at[row], z_target(peer),
        )

    def first_rows(peer, row):
        return remote(
            first_out.at[:, row], first_out.at[:, row], first_p[0].at[peer], first_p[1].at[row],
            p_target(peer),
        )

    def second_rows(peer, row):
        return remote(
            second_out.at[row], second_out.at[row], second_z[0].at[peer], second_z[1].at[row],
            z_target(peer),
        )

    first_own = pltpu.make_async_copy(first_ref, first_out.at[z_me, p_me], local_sems.at[0])
    second_own = pltpu.make_async_copy(second_ref, second_out.at[z_me, p_me], local_sems.at[1])
    first_own.start()
    second_own.start()

    def start_one(step, carry):
        @pl.when(step < z_count)
        def _():
            first_one(z_peer(step), z_me).start()

        @pl.when(step < p_count)
        def _():
            second_one(p_peer(step), p_me).start()

        return carry

    rounds = max(z_count, p_count)
    lax.fori_loop(1, rounds, start_one, 0)

    def forward_first(slot):
        def body(step, carry):
            first_two(p_peer(step), p_me, slot).start()
            return carry

        lax.fori_loop(1, p_count, body, 0)

    def forward_second(slot):
        def body(step, carry):
            second_two(z_peer(step), z_me, slot).start()
            return carry

        lax.fori_loop(1, z_count, body, 0)

    first_own.wait()
    forward_first(z_me)
    second_own.wait()
    forward_second(p_me)

    def relay(step, carry):
        @pl.when(step < z_count)
        def _():
            slot = z_peer(step)
            first_one(slot, slot).wait_recv()
            forward_first(slot)

        @pl.when(step < p_count)
        def _():
            slot = p_peer(step)
            second_one(slot, slot).wait_recv()
            forward_second(slot)

        return carry

    lax.fori_loop(1, rounds, relay, 0)

    def drain(step, carry):
        @pl.when(step < z_count)
        def _():
            peer = z_peer(step)
            first_one(peer, z_me).wait_send()
            second_rows(peer, z_me).wait_send()
            second_rows(peer, peer).wait_recv()

        @pl.when(step < p_count)
        def _():
            peer = p_peer(step)
            second_one(peer, p_me).wait_send()
            first_rows(peer, p_me).wait_send()
            first_rows(peer, peer).wait_recv()

        return carry

    lax.fori_loop(1, rounds, drain, 0)


def gather_ctx(piece, layout, kernel_id, parts=False):
    z_count, p_count = layout
    rows, cols = piece.shape
    lane = 128
    by_columns = cols % (3 * lane) == 0
    if by_columns:
        head = 2 * cols // 3
        shapes = ((rows, head), (rows, cols - head))
        pieces = (piece[:, :head], piece[:, head:])
    else:
        tile = 16
        head = min(rows - tile, max(tile, round(rows * 2 / (3 * tile)) * tile))
        shapes = ((head, cols), (rows - head, cols))
        pieces = (piece[:head], piece[head:])
    dma_pairs = [
        pltpu.SemaphoreType.DMA((z_count,)),
        pltpu.SemaphoreType.DMA((z_count,)),
        pltpu.SemaphoreType.DMA((p_count,)),
        pltpu.SemaphoreType.DMA((p_count,)),
    ]

    def kernel(first_ref, second_ref, first_out, second_out, *sems):
        _gather_kernel(
            z_count, p_count, first_ref, second_ref, first_out, second_out,
            (sems[0], sems[1]), (sems[2], sems[3]), (sems[4], sems[5]), (sems[6], sems[7]),
            sems[8],
        )

    if not by_columns and not parts:
        split_rows = shapes[0][0]

        def owned_kernel(piece_ref, out_ref, *sems):
            kernel(
                piece_ref.at[pl.ds(0, split_rows)],
                piece_ref.at[pl.ds(split_rows, rows - split_rows)],
                out_ref.at[:, :, pl.ds(0, split_rows)],
                out_ref.at[:, :, pl.ds(split_rows, rows - split_rows)],
                *sems,
            )

        whole = pl.pallas_call(
            owned_kernel,
            out_shape=jax.ShapeDtypeStruct((z_count, p_count, rows, cols), piece.dtype),
            in_specs=[pl.BlockSpec(memory_space=pl.ANY)],
            out_specs=pl.BlockSpec(memory_space=pl.ANY),
            scratch_shapes=dma_pairs + [dma_pairs[2], dma_pairs[3], dma_pairs[0], dma_pairs[1]]
            + [pltpu.SemaphoreType.DMA((2,))],
            compiler_params=pltpu.CompilerParams(collective_id=kernel_id, has_side_effects=True),
        )(piece)
        return whole.reshape(z_count * p_count * rows, cols)
    first, second = pl.pallas_call(
        kernel,
        out_shape=(
            jax.ShapeDtypeStruct((z_count, p_count) + shapes[0], piece.dtype),
            jax.ShapeDtypeStruct((z_count, p_count) + shapes[1], piece.dtype),
        ),
        in_specs=[pl.BlockSpec(memory_space=pl.ANY)] * 2,
        out_specs=(pl.BlockSpec(memory_space=pl.ANY),) * 2,
        scratch_shapes=dma_pairs + [dma_pairs[2], dma_pairs[3], dma_pairs[0], dma_pairs[1]]
        + [pltpu.SemaphoreType.DMA((2,))],
        compiler_params=pltpu.CompilerParams(collective_id=kernel_id, has_side_effects=True),
    )(*pieces)
    if parts:
        return first, second
    joined = jnp.concatenate([first, second], axis=3 if by_columns else 2)
    return joined.reshape(z_count * p_count * rows, cols)


def _scatter_kernel(count, part_ref, out_ref, send_sems, recv_sems, local_sem):
    me = lax.axis_index("tp")
    width = out_ref.shape[2]
    mesh_ids = pl.DeviceIdType.MESH
    barrier = pltpu.get_barrier_semaphore()

    def greet(step, carry):
        peer = lax.rem(me + step, count)
        pl.semaphore_signal(barrier, 1, device_id={"tp": peer}, device_id_type=mesh_ids)
        return carry

    lax.fori_loop(1, count, greet, 0)
    pl.semaphore_wait(barrier, count - 1)

    def columns(index):
        return pl.ds(pl.multiple_of(index * width, width), width)

    own = pltpu.make_async_copy(part_ref.at[:, columns(me)], out_ref.at[me], local_sem)
    own.start()

    def remote(peer, slot):
        return pltpu.make_async_remote_copy(
            src_ref=part_ref.at[:, columns(peer)],
            dst_ref=out_ref.at[slot],
            send_sem=send_sems.at[peer],
            recv_sem=recv_sems.at[slot],
            device_id={"tp": peer},
            device_id_type=mesh_ids,
        )

    def send(step, carry):
        remote(lax.rem(me + step, count), me).start()
        return carry

    def finish(step, carry):
        peer = lax.rem(me + step, count)
        remote(peer, me).wait_send()
        remote(peer, peer).wait_recv()
        return carry

    if count % 2 == 0 and count >= 4:
        outer = count // 2
        order = sorted(range(outer), key=lambda hop: -min(hop, outer - hop))
        for hop in order:
            for core in range(2):
                peer = lax.rem(me // 2 + hop, outer) * 2 + core

                @pl.when(peer != me)
                def _():
                    remote(peer, me).start()
    else:
        lax.fori_loop(1, count, send, 0)
    lax.fori_loop(1, count, finish, 0)
    own.wait()


def scatter_sum_tp(part, count, kernel_id, split=None):
    rows, cols = part.shape
    pieces = pl.pallas_call(
        functools.partial(_scatter_kernel, count),
        out_shape=jax.ShapeDtypeStruct((count, rows, cols // count), part.dtype),
        in_specs=[pl.BlockSpec(memory_space=pl.ANY)],
        out_specs=pl.BlockSpec(memory_space=pl.ANY),
        scratch_shapes=[
            pltpu.SemaphoreType.DMA((count,)),
            pltpu.SemaphoreType.DMA((count,)),
            pltpu.SemaphoreType.DMA(()),
        ],
        compiler_params=pltpu.CompilerParams(collective_id=kernel_id, has_side_effects=True),
    )(part)
    if split is not None:
        return (
            jnp.sum(pieces[:, :split].astype(jnp.float32), axis=0).astype(part.dtype),
            jnp.sum(pieces[:, split:].astype(jnp.float32), axis=0).astype(part.dtype),
        )
    return jnp.sum(pieces.astype(jnp.float32), axis=0)


def ctx_layout(mesh):
    count = mesh.shape["ctx"]
    column = mesh.devices.transpose(
        mesh.axis_names.index("ctx"), mesh.axis_names.index("tp")
    )[:, 0]
    try:
        planes = [device.coords[2] for device in column]
    except (AttributeError, IndexError, TypeError):
        return (count, 1)
    p_count = 1
    while p_count < count and planes[p_count] == planes[0]:
        p_count += 1
    if count % p_count:
        return (count, 1)
    for index in range(count):
        if planes[index] != planes[(index // p_count) * p_count]:
            return (count, 1)
    return (count // p_count, p_count)


def initial_positions(block_map, first_row, row_count, block_rows):
    row_ids = first_row + jnp.arange(row_count, dtype=jnp.int32)
    block_ids = row_ids // block_rows
    table_ids = jnp.arange(block_map.shape[0], dtype=jnp.int32)
    mapped = jnp.sum(
        jnp.where(block_ids[:, None] == table_ids[None, :], block_map[None, :], 0), axis=1
    )
    return mapped * block_rows + row_ids % block_rows


def request_index(positions, request_ends):
    return jnp.sum((positions[:, None] >= request_ends[None, :]).astype(jnp.int32), axis=1)


def round_weights(weights):
    rounded = weights.astype(jnp.bfloat16)
    rounded = lax.optimization_barrier(rounded)
    return rounded.astype(jnp.float32)


def softmax_parts(
    dec_heads, projected_key_rows, projected_value_rows, owned, kv_heads, head_dim, score_scale
):
    row_count = projected_key_rows.shape[0]
    scores = (
        jnp.einsum(
            "rgjd,tgd->rgjt",
            dec_heads,
            projected_key_rows.reshape(row_count, kv_heads, head_dim),
            preferred_element_type=jnp.float32,
        )
        * score_scale
    )
    scores = jnp.where(owned, scores, floor_value)
    part_peak = jnp.max(scores, axis=3)
    weights = jnp.where(owned, jnp.exp(scores - part_peak[..., None]), 0.0)
    part_total = jnp.sum(weights, axis=3)
    part_mixed = jnp.einsum(
        "rgjt,tgd->rgjd",
        weights.astype(jnp.bfloat16),
        projected_value_rows.reshape(row_count, kv_heads, head_dim),
        preferred_element_type=jnp.float32,
    )
    return (part_peak, part_total, part_mixed)


def on_device(
    layout, tp_count, tokens, new_token_states, w_query, key_matrix, value_matrix, w_out, lengths, block_map
):
    local_rows = tokens.shape[0]
    block_rows = local_rows // 2
    request_count = new_token_states.shape[0]
    head_dim = HEAD_SIZE
    query_width = w_query.shape[1]
    kv_width = key_matrix.shape[1]
    kv_heads = kv_width // head_dim
    query_group_count = query_width // kv_width
    score_scale = 1.0 / math.sqrt(head_dim)
    device = lax.axis_index("ctx")
    request_ends = jnp.cumsum(lengths)
    inputs = jnp.concatenate([tokens, new_token_states], axis=0)
    z_count, p_count = layout
    model_width = inputs.shape[1]
    qkv_width = query_width + 2 * kv_width
    if (qkv_width + w_out.shape[0]) % 384 == 0 and 2 * w_out.shape[0] == qkv_width:
        qkv_rows, out_rows = gather_ctx(
            jnp.concatenate([w_query, key_matrix, value_matrix, w_out.T], axis=1),
            layout,
            0,
            parts=True,
        )
        projected_all = jnp.dot(
            inputs,
            qkv_rows.reshape(model_width, qkv_width),
            preferred_element_type=jnp.float32,
        ).astype(jnp.bfloat16)
        out_weight_t = out_rows.reshape(model_width, w_out.shape[0])
    else:
        joined = gather_ctx(
            jnp.concatenate([w_query, key_matrix, value_matrix, w_out.T], axis=1), layout, 0
        )
        projected_all = jnp.dot(
            inputs, joined[:, :qkv_width], preferred_element_type=jnp.float32
        ).astype(jnp.bfloat16)
        out_weight_t = joined[:, qkv_width:]
    query_all = projected_all[:, :query_width]
    key_all = projected_all[:, query_width : query_width + kv_width]
    value_all = projected_all[:, query_width + kv_width :]
    local_query = query_all[:local_rows]
    local_keys = key_all[:local_rows]
    local_values = value_all[:local_rows]
    dec_query = query_all[local_rows:]
    decode_key_rows = key_all[local_rows:]
    decode_value_rows = value_all[local_rows:]
    token_pos = initial_positions(block_map, device * local_rows, local_rows, block_rows)
    token_request = request_index(token_pos, request_ends)
    query_heads = local_query.reshape(local_rows, kv_heads, query_group_count, head_dim)

    def attend(running, shard_pieces, first_row):
        peak_run, total_run, mixed_run = running
        key_piece, value_piece = shard_pieces
        row_count = key_piece.shape[0]
        key_pos = lax.dynamic_slice_in_dim(cache_pos, first_row, row_count, 0)
        key_request = lax.dynamic_slice_in_dim(cache_request, first_row, row_count, 0)
        allowed = (key_request[None, :] == token_request[:, None]) & (
            key_pos[None, :] <= token_pos[:, None]
        )
        scores = (
            jnp.einsum(
                "tgjd,kgd->gjtk",
                query_heads,
                key_piece.reshape(row_count, kv_heads, head_dim),
                preferred_element_type=jnp.float32,
            )
            * score_scale
        )
        scores = jnp.where(allowed, scores, floor_value)
        peak_new = jnp.maximum(peak_run, jnp.max(scores, axis=3))
        weights = jnp.exp(scores - peak_new[..., None])
        rescale = jnp.exp(peak_run - peak_new)
        total_new = total_run * rescale + jnp.sum(weights, axis=3)
        mixed_new = mixed_run * rescale[..., None] + jnp.einsum(
            "gjtk,kgd->gjtd",
            weights.astype(jnp.bfloat16),
            value_piece.reshape(row_count, kv_heads, head_dim),
            preferred_element_type=jnp.float32,
        )
        return (peak_new, total_new, mixed_new)

    start_state = (
        jnp.full((kv_heads, query_group_count, local_rows), floor_value, jnp.float32),
        jnp.zeros((kv_heads, query_group_count, local_rows), jnp.float32),
        jnp.zeros((kv_heads, query_group_count, local_rows, head_dim), jnp.float32),
    )
    dec_heads = dec_query.reshape(request_count, kv_heads, query_group_count, head_dim)
    request_ids = jnp.arange(request_count, dtype=jnp.int32)
    cache_both = gather_ctx(
        jnp.concatenate([local_keys, local_values], axis=1), layout, 1
    )
    cache_keys = cache_both[:, :kv_width]
    cache_values = cache_both[:, kv_width:]
    total_rows = cache_keys.shape[0]
    step_rows = total_rows
    cache_pos = (
        block_map[:, None] * block_rows + jnp.arange(block_rows, dtype=jnp.int32)[None, :]
    ).reshape(total_rows)
    cache_request = request_index(cache_pos, request_ends)

    def key_step(running, step_index):
        first_row = step_index * step_rows
        pieces = (
            lax.dynamic_slice_in_dim(cache_keys, first_row, step_rows, 0),
            lax.dynamic_slice_in_dim(cache_values, first_row, step_rows, 0),
        )
        return (attend(running, pieces, first_row), None)

    final_state, unused = lax.scan(
        key_step, start_state, jnp.arange(total_rows // step_rows, dtype=jnp.int32)
    )
    peak_run, total_run, mixed_run = final_state
    owned = (cache_request[None, :] == request_ids[:, None])[:, None, None, :]
    cache_peak, cache_total, cache_mixed = softmax_parts(
        dec_heads, cache_keys, cache_values, owned, kv_heads, head_dim, score_scale
    )
    attended = (
        (mixed_run / total_run[..., None]).transpose(2, 0, 1, 3).reshape(local_rows, query_width)
    )
    attended = attended.astype(jnp.bfloat16)
    own_keys = decode_key_rows.reshape(request_count, kv_heads, 1, head_dim).astype(jnp.float32)
    own_values = decode_value_rows.reshape(request_count, kv_heads, 1, head_dim).astype(jnp.float32)
    self_scores = jnp.sum(dec_heads.astype(jnp.float32) * own_keys, axis=3) * score_scale
    peak_all = jnp.maximum(cache_peak, self_scores)
    rescale = jnp.exp(cache_peak - peak_all)
    self_weights = jnp.exp(self_scores - peak_all)
    dec_total = cache_total * rescale + self_weights
    dec_mixed = (
        cache_mixed * rescale[..., None] + round_weights(self_weights)[..., None] * own_values
    )
    dec_attn = (
        (dec_mixed / dec_total[..., None]).reshape(request_count, query_width).astype(jnp.bfloat16)
    )
    attended_all = jnp.concatenate([attended, dec_attn], axis=0)
    projected = lax.dot_general(
        attended_all,
        out_weight_t,
        (((1,), (1,)), ((), ())),
        preferred_element_type=jnp.float32,
    )
    return scatter_sum_tp(projected.astype(jnp.bfloat16), tp_count, 2, split=local_rows)


def solution(mesh):
    return jax.shard_map(
        functools.partial(on_device, ctx_layout(mesh), mesh.shape["tp"]),
        mesh=mesh,
        in_specs=(
            P("ctx", None),
            P(),
            P("ctx", "tp"),
            P("ctx", "tp"),
            P("ctx", "tp"),
            P("tp", "ctx"),
            P(),
            P(),
        ),
        out_specs=(P("ctx", "tp"), P(None, "tp")),
        check_vma=False,
    )
```

```python
import functools
import math

import jax
import jax.numpy as jnp
from jax import lax
from jax.experimental import pallas as pl
from jax.experimental.pallas import tpu as pltpu
from jax.sharding import PartitionSpec as P

HEAD_SIZE = 128


floor_value = -1e30


def _gather_kernel(
    z_count,
    p_count,
    first_ref,
    second_ref,
    first_out,
    second_out,
    first_z,
    first_p,
    second_p,
    second_z,
    local_sems,
):
    me = lax.axis_index("ctx")
    z_me = me // p_count
    p_me = lax.rem(me, p_count)
    mesh_ids = pl.DeviceIdType.MESH
    barrier = pltpu.get_barrier_semaphore()

    def z_peer(step):
        return lax.rem(z_me + step, z_count)

    def p_peer(step):
        return lax.rem(p_me + step, p_count)

    def z_target(peer):
        return peer * p_count + p_me

    def p_target(peer):
        return z_me * p_count + peer

    def greet(peer_of, target_of):
        def body(step, carry):
            pl.semaphore_signal(
                barrier, 1, device_id={"ctx": target_of(peer_of(step))}, device_id_type=mesh_ids
            )
            return carry

        return body

    lax.fori_loop(1, z_count, greet(z_peer, z_target), 0)
    lax.fori_loop(1, p_count, greet(p_peer, p_target), 0)
    pl.semaphore_wait(barrier, z_count + p_count - 2)

    def remote(src, dst, send_sem, recv_sem, target):
        return pltpu.make_async_remote_copy(
            src_ref=src,
            dst_ref=dst,
            send_sem=send_sem,
            recv_sem=recv_sem,
            device_id={"ctx": target},
            device_id_type=mesh_ids,
        )

    def first_one(peer, slot):
        return remote(
            first_ref, first_out.at[slot, p_me], first_z[0].at[peer], first_z[1].at[slot],
            z_target(peer),
        )

    def second_one(peer, slot):
        return remote(
            second_ref, second_out.at[z_me, slot], second_p[0].at[peer], second_p[1].at[slot],
            p_target(peer),
        )

    def first_two(peer, row, slot):
        return remote(
            first_out.at[slot, row], first_out.at[slot, row], first_p[0].at[peer],
            first_p[1].at[row], p_target(peer),
        )

    def second_two(peer, row, slot):
        return remote(
            second_out.at[row, slot], second_out.at[row, slot], second_z[0].at[peer],
            second_z[1].at[row], z_target(peer),
        )

    def first_rows(peer, row):
        return remote(
            first_out.at[:, row], first_out.at[:, row], first_p[0].at[peer], first_p[1].at[row],
            p_target(peer),
        )

    def second_rows(peer, row):
        return remote(
            second_out.at[row], second_out.at[row], second_z[0].at[peer], second_z[1].at[row],
            z_target(peer),
        )

    first_own = pltpu.make_async_copy(first_ref, first_out.at[z_me, p_me], local_sems.at[0])
    second_own = pltpu.make_async_copy(second_ref, second_out.at[z_me, p_me], local_sems.at[1])
    first_own.start()
    second_own.start()

    def start_one(step, carry):
        @pl.when(step < z_count)
        def _():
            first_one(z_peer(step), z_me).start()

        @pl.when(step < p_count)
        def _():
            second_one(p_peer(step), p_me).start()

        return carry

    rounds = max(z_count, p_count)
    lax.fori_loop(1, rounds, start_one, 0)

    def forward_first(slot):
        def body(step, carry):
            first_two(p_peer(step), p_me, slot).start()
            return carry

        lax.fori_loop(1, p_count, body, 0)

    def forward_second(slot):
        def body(step, carry):
            second_two(z_peer(step), z_me, slot).start()
            return carry

        lax.fori_loop(1, z_count, body, 0)

    first_own.wait()
    forward_first(z_me)
    second_own.wait()
    forward_second(p_me)

    def relay(step, carry):
        @pl.when(step < z_count)
        def _():
            slot = z_peer(step)
            first_one(slot, slot).wait_recv()
            forward_first(slot)

        @pl.when(step < p_count)
        def _():
            slot = p_peer(step)
            second_one(slot, slot).wait_recv()
            forward_second(slot)

        return carry

    lax.fori_loop(1, rounds, relay, 0)

    def drain(step, carry):
        @pl.when(step < z_count)
        def _():
            peer = z_peer(step)
            first_one(peer, z_me).wait_send()
            second_rows(peer, z_me).wait_send()
            second_rows(peer, peer).wait_recv()

        @pl.when(step < p_count)
        def _():
            peer = p_peer(step)
            second_one(peer, p_me).wait_send()
            first_rows(peer, p_me).wait_send()
            first_rows(peer, peer).wait_recv()

        return carry

    lax.fori_loop(1, rounds, drain, 0)


def gather_ctx(piece, layout, kernel_id, parts=False):
    z_count, p_count = layout
    rows, cols = piece.shape
    lane = 128
    by_columns = cols % (3 * lane) == 0
    if by_columns:
        head = 2 * cols // 3
        shapes = ((rows, head), (rows, cols - head))
        pieces = (piece[:, :head], piece[:, head:])
    else:
        tile = 16
        head = min(rows - tile, max(tile, round(rows * 2 / (3 * tile)) * tile))
        shapes = ((head, cols), (rows - head, cols))
        pieces = (piece[:head], piece[head:])
    dma_pairs = [
        pltpu.SemaphoreType.DMA((z_count,)),
        pltpu.SemaphoreType.DMA((z_count,)),
        pltpu.SemaphoreType.DMA((p_count,)),
        pltpu.SemaphoreType.DMA((p_count,)),
    ]

    def kernel(first_ref, second_ref, first_out, second_out, *sems):
        _gather_kernel(
            z_count, p_count, first_ref, second_ref, first_out, second_out,
            (sems[0], sems[1]), (sems[2], sems[3]), (sems[4], sems[5]), (sems[6], sems[7]),
            sems[8],
        )

    if not by_columns and not parts:
        split_rows = shapes[0][0]

        def owned_kernel(piece_ref, out_ref, *sems):
            kernel(
                piece_ref.at[pl.ds(0, split_rows)],
                piece_ref.at[pl.ds(split_rows, rows - split_rows)],
                out_ref.at[:, :, pl.ds(0, split_rows)],
                out_ref.at[:, :, pl.ds(split_rows, rows - split_rows)],
                *sems,
            )

        whole = pl.pallas_call(
            owned_kernel,
            out_shape=jax.ShapeDtypeStruct((z_count, p_count, rows, cols), piece.dtype),
            in_specs=[pl.BlockSpec(memory_space=pl.ANY)],
            out_specs=pl.BlockSpec(memory_space=pl.ANY),
            scratch_shapes=dma_pairs + [dma_pairs[2], dma_pairs[3], dma_pairs[0], dma_pairs[1]]
            + [pltpu.SemaphoreType.DMA((2,))],
            compiler_params=pltpu.CompilerParams(collective_id=kernel_id, has_side_effects=True),
        )(piece)
        return whole.reshape(z_count * p_count * rows, cols)
    first, second = pl.pallas_call(
        kernel,
        out_shape=(
            jax.ShapeDtypeStruct((z_count, p_count) + shapes[0], piece.dtype),
            jax.ShapeDtypeStruct((z_count, p_count) + shapes[1], piece.dtype),
        ),
        in_specs=[pl.BlockSpec(memory_space=pl.ANY)] * 2,
        out_specs=(pl.BlockSpec(memory_space=pl.ANY),) * 2,
        scratch_shapes=dma_pairs + [dma_pairs[2], dma_pairs[3], dma_pairs[0], dma_pairs[1]]
        + [pltpu.SemaphoreType.DMA((2,))],
        compiler_params=pltpu.CompilerParams(collective_id=kernel_id, has_side_effects=True),
    )(*pieces)
    if parts:
        return first, second
    joined = jnp.concatenate([first, second], axis=3 if by_columns else 2)
    return joined.reshape(z_count * p_count * rows, cols)


def _scatter_kernel(count, part_ref, out_ref, send_sems, recv_sems, local_sem):
    me = lax.axis_index("tp")
    width = out_ref.shape[2]
    mesh_ids = pl.DeviceIdType.MESH
    barrier = pltpu.get_barrier_semaphore()

    def greet(step, carry):
        peer = lax.rem(me + step, count)
        pl.semaphore_signal(barrier, 1, device_id={"tp": peer}, device_id_type=mesh_ids)
        return carry

    lax.fori_loop(1, count, greet, 0)
    pl.semaphore_wait(barrier, count - 1)

    def columns(index):
        return pl.ds(pl.multiple_of(index * width, width), width)

    own = pltpu.make_async_copy(part_ref.at[:, columns(me)], out_ref.at[me], local_sem)
    own.start()

    def remote(peer, slot):
        return pltpu.make_async_remote_copy(
            src_ref=part_ref.at[:, columns(peer)],
            dst_ref=out_ref.at[slot],
            send_sem=send_sems.at[peer],
            recv_sem=recv_sems.at[slot],
            device_id={"tp": peer},
            device_id_type=mesh_ids,
        )

    def send(step, carry):
        remote(lax.rem(me + step, count), me).start()
        return carry

    def finish(step, carry):
        peer = lax.rem(me + step, count)
        remote(peer, me).wait_send()
        remote(peer, peer).wait_recv()
        return carry

    if count % 2 == 0 and count >= 4:
        outer = count // 2
        order = sorted(range(outer), key=lambda hop: -min(hop, outer - hop))
        for hop in order:
            for core in range(2):
                peer = lax.rem(me // 2 + hop, outer) * 2 + core

                @pl.when(peer != me)
                def _():
                    remote(peer, me).start()
    else:
        lax.fori_loop(1, count, send, 0)
    lax.fori_loop(1, count, finish, 0)
    own.wait()


def scatter_sum_tp(part, count, kernel_id, split=None):
    rows, cols = part.shape
    pieces = pl.pallas_call(
        functools.partial(_scatter_kernel, count),
        out_shape=jax.ShapeDtypeStruct((count, rows, cols // count), part.dtype),
        in_specs=[pl.BlockSpec(memory_space=pl.ANY)],
        out_specs=pl.BlockSpec(memory_space=pl.ANY),
        scratch_shapes=[
            pltpu.SemaphoreType.DMA((count,)),
            pltpu.SemaphoreType.DMA((count,)),
            pltpu.SemaphoreType.DMA(()),
        ],
        compiler_params=pltpu.CompilerParams(collective_id=kernel_id, has_side_effects=True),
    )(part)
    if split is not None:
        return (
            jnp.sum(pieces[:, :split].astype(jnp.float32), axis=0).astype(part.dtype),
            jnp.sum(pieces[:, split:].astype(jnp.float32), axis=0).astype(part.dtype),
        )
    return jnp.sum(pieces.astype(jnp.float32), axis=0)


def ctx_layout(mesh):
    count = mesh.shape["ctx"]
    column = mesh.devices.transpose(
        mesh.axis_names.index("ctx"), mesh.axis_names.index("tp")
    )[:, 0]
    try:
        planes = [device.coords[2] for device in column]
    except (AttributeError, IndexError, TypeError):
        return (count, 1)
    p_count = 1
    while p_count < count and planes[p_count] == planes[0]:
        p_count += 1
    if count % p_count:
        return (count, 1)
    for index in range(count):
        if planes[index] != planes[(index // p_count) * p_count]:
            return (count, 1)
    return (count // p_count, p_count)


def initial_positions(block_map, first_row, row_count, block_rows):
    row_ids = first_row + jnp.arange(row_count, dtype=jnp.int32)
    block_ids = row_ids // block_rows
    table_ids = jnp.arange(block_map.shape[0], dtype=jnp.int32)
    mapped = jnp.sum(
        jnp.where(block_ids[:, None] == table_ids[None, :], block_map[None, :], 0), axis=1
    )
    return mapped * block_rows + row_ids % block_rows


def request_index(positions, request_ends):
    return jnp.sum((positions[:, None] >= request_ends[None, :]).astype(jnp.int32), axis=1)


def round_weights(weights):
    rounded = weights.astype(jnp.bfloat16)
    rounded = lax.optimization_barrier(rounded)
    return rounded.astype(jnp.float32)


def softmax_parts(
    dec_heads, projected_key_rows, projected_value_rows, owned, kv_heads, head_dim, score_scale
):
    row_count = projected_key_rows.shape[0]
    scores = (
        jnp.einsum(
            "rgjd,tgd->rgjt",
            dec_heads,
            projected_key_rows.reshape(row_count, kv_heads, head_dim),
            preferred_element_type=jnp.float32,
        )
        * score_scale
    )
    scores = jnp.where(owned, scores, floor_value)
    part_peak = jnp.max(scores, axis=3)
    weights = jnp.where(owned, jnp.exp(scores - part_peak[..., None]), 0.0)
    part_total = jnp.sum(weights, axis=3)
    part_mixed = jnp.einsum(
        "rgjt,tgd->rgjd",
        weights.astype(jnp.bfloat16),
        projected_value_rows.reshape(row_count, kv_heads, head_dim),
        preferred_element_type=jnp.float32,
    )
    return (part_peak, part_total, part_mixed)


def on_device(
    layout, tp_count, tokens, new_token_states, w_query, key_matrix, value_matrix, w_out, lengths, block_map
):
    local_rows = tokens.shape[0]
    block_rows = local_rows // 2
    request_count = new_token_states.shape[0]
    head_dim = HEAD_SIZE
    query_width = w_query.shape[1]
    kv_width = key_matrix.shape[1]
    kv_heads = kv_width // head_dim
    query_group_count = query_width // kv_width
    score_scale = 1.0 / math.sqrt(head_dim)
    device = lax.axis_index("ctx")
    request_ends = jnp.cumsum(lengths)
    inputs = jnp.concatenate([tokens, new_token_states], axis=0)
    z_count, p_count = layout
    model_width = inputs.shape[1]
    qkv_width = query_width + 2 * kv_width
    if (qkv_width + w_out.shape[0]) % 384 == 0 and 2 * w_out.shape[0] == qkv_width:
        qkv_rows, out_rows = gather_ctx(
            jnp.concatenate([w_query, key_matrix, value_matrix, w_out.T], axis=1),
            layout,
            0,
            parts=True,
        )
        projected_all = jnp.dot(
            inputs,
            qkv_rows.reshape(model_width, qkv_width),
            preferred_element_type=jnp.float32,
        ).astype(jnp.bfloat16)
        out_weight_t = out_rows.reshape(model_width, w_out.shape[0])
    else:
        joined = gather_ctx(
            jnp.concatenate([w_query, key_matrix, value_matrix, w_out.T], axis=1), layout, 0
        )
        projected_all = jnp.dot(
            inputs, joined[:, :qkv_width], preferred_element_type=jnp.float32
        ).astype(jnp.bfloat16)
        out_weight_t = joined[:, qkv_width:]
    query_all = projected_all[:, :query_width]
    key_all = projected_all[:, query_width : query_width + kv_width]
    value_all = projected_all[:, query_width + kv_width :]
    local_query = query_all[:local_rows]
    local_keys = key_all[:local_rows]
    local_values = value_all[:local_rows]
    dec_query = query_all[local_rows:]
    decode_key_rows = key_all[local_rows:]
    decode_value_rows = value_all[local_rows:]
    token_pos = initial_positions(block_map, device * local_rows, local_rows, block_rows)
    token_request = request_index(token_pos, request_ends)
    query_heads = local_query.reshape(local_rows, kv_heads, query_group_count, head_dim)

    def attend(running, shard_pieces, first_row):
        peak_run, total_run, mixed_run = running
        key_piece, value_piece = shard_pieces
        row_count = key_piece.shape[0]
        key_pos = lax.dynamic_slice_in_dim(cache_pos, first_row, row_count, 0)
        key_request = lax.dynamic_slice_in_dim(cache_request, first_row, row_count, 0)
        allowed = (key_request[None, :] == token_request[:, None]) & (
            key_pos[None, :] <= token_pos[:, None]
        )
        scores = (
            jnp.einsum(
                "tgjd,kgd->gjtk",
                query_heads,
                key_piece.reshape(row_count, kv_heads, head_dim),
                preferred_element_type=jnp.float32,
            )
            * score_scale
        )
        scores = jnp.where(allowed, scores, floor_value)
        peak_new = jnp.maximum(peak_run, jnp.max(scores, axis=3))
        weights = jnp.where(allowed, jnp.exp(scores - peak_new[..., None]), 0.0)
        rescale = jnp.exp(peak_run - peak_new)
        total_new = total_run * rescale + jnp.sum(weights, axis=3)
        mixed_new = mixed_run * rescale[..., None] + jnp.einsum(
            "gjtk,kgd->gjtd",
            weights.astype(jnp.bfloat16),
            value_piece.reshape(row_count, kv_heads, head_dim),
            preferred_element_type=jnp.float32,
        )
        return (peak_new, total_new, mixed_new)

    start_state = (
        jnp.full((kv_heads, query_group_count, local_rows), floor_value, jnp.float32),
        jnp.zeros((kv_heads, query_group_count, local_rows), jnp.float32),
        jnp.zeros((kv_heads, query_group_count, local_rows, head_dim), jnp.float32),
    )
    dec_heads = dec_query.reshape(request_count, kv_heads, query_group_count, head_dim)
    request_ids = jnp.arange(request_count, dtype=jnp.int32)
    cache_both = gather_ctx(
        jnp.concatenate([local_keys, local_values], axis=1), layout, 1
    )
    cache_keys = cache_both[:, :kv_width]
    cache_values = cache_both[:, kv_width:]
    total_rows = cache_keys.shape[0]
    step_rows = total_rows
    cache_pos = (
        block_map[:, None] * block_rows + jnp.arange(block_rows, dtype=jnp.int32)[None, :]
    ).reshape(total_rows)
    cache_request = request_index(cache_pos, request_ends)

    def key_step(running, step_index):
        first_row = step_index * step_rows
        pieces = (
            lax.dynamic_slice_in_dim(cache_keys, first_row, step_rows, 0),
            lax.dynamic_slice_in_dim(cache_values, first_row, step_rows, 0),
        )
        return (attend(running, pieces, first_row), None)

    final_state, unused = lax.scan(
        key_step, start_state, jnp.arange(total_rows // step_rows, dtype=jnp.int32)
    )
    peak_run, total_run, mixed_run = final_state
    owned = (cache_request[None, :] == request_ids[:, None])[:, None, None, :]
    cache_peak, cache_total, cache_mixed = softmax_parts(
        dec_heads, cache_keys, cache_values, owned, kv_heads, head_dim, score_scale
    )
    attended = (
        (mixed_run / total_run[..., None]).transpose(2, 0, 1, 3).reshape(local_rows, query_width)
    )
    attended = attended.astype(jnp.bfloat16)
    own_keys = decode_key_rows.reshape(request_count, kv_heads, 1, head_dim).astype(jnp.float32)
    own_values = decode_value_rows.reshape(request_count, kv_heads, 1, head_dim).astype(jnp.float32)
    self_scores = jnp.sum(dec_heads.astype(jnp.float32) * own_keys, axis=3) * score_scale
    peak_all = jnp.maximum(cache_peak, self_scores)
    rescale = jnp.exp(cache_peak - peak_all)
    self_weights = jnp.exp(self_scores - peak_all)
    dec_total = cache_total * rescale + self_weights
    dec_mixed = (
        cache_mixed * rescale[..., None] + round_weights(self_weights)[..., None] * own_values
    )
    dec_attn = (
        (dec_mixed / dec_total[..., None]).reshape(request_count, query_width).astype(jnp.bfloat16)
    )
    attended_all = jnp.concatenate([attended, dec_attn], axis=0)
    projected = lax.dot_general(
        attended_all,
        out_weight_t,
        (((1,), (1,)), ((), ())),
        preferred_element_type=jnp.float32,
    )
    return scatter_sum_tp(projected.astype(jnp.bfloat16), tp_count, 2, split=local_rows)


def solution(mesh):
    return jax.shard_map(
        functools.partial(on_device, ctx_layout(mesh), mesh.shape["tp"]),
        mesh=mesh,
        in_specs=(
            P("ctx", None),
            P(),
            P("ctx", "tp"),
            P("ctx", "tp"),
            P("ctx", "tp"),
            P("tp", "ctx"),
            P(),
            P(),
        ),
        out_specs=(P("ctx", "tp"), P(None, "tp")),
        check_vma=False,
    )
```
